32 devices in a mesh: dp: 8 (over z, y), tensor: 4 (over x, core).
Axes of the slice: x: 2, y: 2, z: 4, core: 2. Of those that a mesh axis runs over, the one named last changes fastest.
Arguments:
- tokens: bfloat16 [16384, 768], P(('dp', 'tensor')), may hold values from -6 to 6
- seq_lengths: int32 [8], replicated, may hold values from 1 to 2048, 10240 in all
- positions: int32 [8, 2048], P('dp'), may hold values from 0 to 2047, each once within a row
- w_query: bfloat16 [768, 768], P('dp', 'tensor'), may hold values from -0.21875 to 0.21875
- w_key: bfloat16 [768, 768], P('dp', 'tensor'), may hold values from -0.21875 to 0.21875
- w_value: bfloat16 [768, 768], P('dp', 'tensor'), may hold values from -0.21875 to 0.21875
- w_out: bfloat16 [768, 768], P('tensor', 'dp'), may hold values from -6 to 6
- w_up: bfloat16 [768, 3072], P('dp', 'tensor'), may hold values from -0.21875 to 0.21875
- w_down: bfloat16 [3072, 768], P('tensor', 'dp'), may hold values from -0.109375 to 0.109375
- b_query: bfloat16 [768], P('tensor'), may hold values from -3 to 3
- b_value: bfloat16 [768], P('tensor'), may hold values from -0.1796875 to 0.1796875
- b_out: bfloat16 [768], replicated, may hold values from -1.796875 to 1.796875
- b_up: bfloat16 [3072], P('tensor'), may hold values from -1.796875 to 1.796875
- b_down: bfloat16 [768], replicated, may hold values from -1.796875 to 1.796875
- gain_attn: bfloat16 [768], replicated, may hold values from 0.5 to 1.5
- shift_attn: bfloat16 [768], replicated, may hold values from -1.796875 to 1.796875
- gain_ffn: bfloat16 [768], replicated, may hold values from 0.5 to 1.5
- shift_ffn: bfloat16 [768], replicated, may hold values from -1.796875 to 1.796875
- out_grad: bfloat16 [16384, 768], P(('dp', 'tensor')), may hold values from -6 to 6
Outputs:
- layer_out: bfloat16 [16384, 768], P(('dp', 'tensor'))
- input_grad: bfloat16 [16384, 768], P(('dp', 'tensor'))
- grad_w_query: float32 [768, 768], P('dp', 'tensor')
- grad_w_key: float32 [768, 768], P('dp', 'tensor')
- grad_w_value: float32 [768, 768], P('dp', 'tensor')
- grad_w_out: float32 [768, 768], P('tensor', 'dp')
- grad_w_up: float32 [768, 3072], P('dp', 'tensor')
- grad_w_down: float32 [3072, 768], P('tensor', 'dp')
- grad_b_query: float32 [768], P('tensor')
- grad_b_value: float32 [768], P('tensor')
- grad_b_out: float32 [768], replicated
- grad_b_up: float32 [3072], P('tensor')
- grad_b_down: float32 [768], replicated
- grad_gain_attn: float32 [768], replicated
- grad_shift_attn: float32 [768], replicated
- grad_gain_ffn: float32 [768], replicated
- grad_shift_ffn: float32 [768], replicated
- rms: float32 [3], replicated
The draws below stay inside these ranges and needn't reach their ends.
Inputs may be any that keep to these rules, and one draw needn't show every extreme that they name: `seq_lengths`: one length for each slot; the longest equals 2048. `positions`: each row is a permutation of 0 to 2047.
All inputs are finite; a program needn't handle non-finite values.
Results may differ from the reference program's by a relative error of at most 0.019.
Values may be sent and summed in bfloat16 or wider, within the bound.
No kernel may reach another device: no remote copies, remote signals or barrier semaphores. Data moves between devices by JAX's collectives and lax.ppermute only.
A program may use at most 128 MiB of HBM per device.

```python
import math
from functools import partial
import jax
import jax.numpy as jnp
import numpy as np
from jax import lax

D = 768
HEADS = 12
HEAD_DIM = 64
FF = 3072
SEQ = 2048
TOKENS = 16384
N_DP = 8


def block_levels(own_key, shape, split, low, largest):
    gain = 1.0
    for position, shards_of in split:
        heights = jax.random.uniform(jax.random.fold_in(jax.random.fold_in(own_key, 6), position), (shards_of,), jnp.float32, low / len(split), largest / len(split))
        gain = gain * jnp.repeat(jnp.exp(heights), shape[position] // shards_of).reshape((-1,) + (1,) * (len(shape) - 1 - position))
    return gain


def profile(count, total, most, skew):
    weights = [(1 << 20) // math.isqrt(grade ** skew) + 1 for grade in range(2, count + 1)]
    surplus, counts = total - most - (count - 1), [1] * (count - 1)
    while surplus > 0:
        free = [i for i in range(count - 1) if counts[i] < most]
        whole, budget = sum([weights[i] for i in free]), surplus
        for i in free:
            addition = min(most - counts[i], max(1, budget * weights[i] // whole), surplus)
            counts[i] = counts[i] + addition
            surplus = surplus - addition
    return np.array([most] + counts)


def uneven(rng, number_of, total, most, lean):
    if number_of == 2:
        one = jax.random.randint(rng, (), max(1, total - most), min(most, total - 1) + 1)
        return jnp.stack([one, total - one])
    lengths = jnp.asarray(profile(number_of, total, most, lean), jnp.int32)
    couples = (number_of - 1) // 2
    giver, receiver = lengths[1:1 + 2 * couples:2], lengths[2:2 + 2 * couples:2]
    room = jnp.minimum(giver - 1, most - receiver)
    passed = jax.random.randint(jax.random.fold_in(rng, 1), (couples,), 0, 1 << 20) % (room + 1)
    lengths = lengths.at[1:1 + 2 * couples:2].set(giver - passed).at[2:2 + 2 * couples:2].set(receiver + passed)
    return lengths[jax.random.permutation(jax.random.fold_in(rng, 2), number_of)]


def normal_values(own_key, extent, width, most, split=(), dtype=jnp.bfloat16):
    loudness = block_levels(own_key, extent, split, -0.22, 0.18) if split else 1.0
    entries = jax.random.normal(own_key, extent, jnp.float32) * width * loudness
    return jnp.minimum(jnp.maximum(entries, -most), most).astype(dtype)


def setup_inputs(seed: int = 0) -> dict:
    key_list = jax.random.split(jax.random.key(seed), 20)
    return {
        "tokens": normal_values(key_list[0], (TOKENS, D), 1.0, 6.0, ((0, 32),)),
        "seq_lengths": uneven(key_list[1], N_DP, N_DP * SEQ * 5 // 8, SEQ, 1).astype(jnp.int32),
        "positions": jax.vmap(lambda own: jax.random.permutation(own, SEQ))(jax.random.split(key_list[2], N_DP)).reshape((N_DP, SEQ)).astype(jnp.int32),
        "w_query": normal_values(key_list[3], (D, D), D ** -0.5, 0.21875, ((0, 8), (1, 4))),
        "w_key": normal_values(key_list[4], (D, D), D ** -0.5, 0.21875, ((0, 8), (1, 4))),
        "w_value": normal_values(key_list[5], (D, D), D ** -0.5, 0.21875, ((0, 8), (1, 4))),
        "w_out": normal_values(key_list[6], (D, D), 1 ** -0.5, 6.0, ((0, 4), (1, 8))),
        "w_up": normal_values(key_list[7], (D, FF), D ** -0.5, 0.21875, ((0, 8), (1, 4))),
        "w_down": normal_values(key_list[8], (FF, D), FF ** -0.5, 0.109375, ((0, 4), (1, 8))),
        "b_query": normal_values(key_list[9], (D,), 0.5, 3.0, ((0, 4),)),
        "b_value": normal_values(key_list[10], (D,), 0.03, 0.1796875, ((0, 4),)),
        "b_out": normal_values(key_list[11], (D,), 0.3, 1.796875),
        "b_up": normal_values(key_list[12], (FF,), 0.3, 1.796875, ((0, 4),)),
        "b_down": normal_values(key_list[13], (D,), 0.3, 1.796875),
        "gain_attn": jnp.clip(1.0 + 0.1 * jax.random.normal(key_list[14], (D,), jnp.float32), 0.5, 1.5).astype(jnp.bfloat16),
        "shift_attn": normal_values(key_list[15], (D,), 0.3, 1.796875),
        "gain_ffn": jnp.clip(1.0 + 0.1 * jax.random.normal(key_list[16], (D,), jnp.float32), 0.5, 1.5).astype(jnp.bfloat16),
        "shift_ffn": normal_values(key_list[17], (D,), 0.3, 1.796875),
        "out_grad": normal_values(key_list[18], (TOKENS, D), 1.0, 6.0, ((0, 32),)),
    }


@jax.custom_vjp
def low(v):
    return lax.optimization_barrier(v.astype(jnp.bfloat16)).astype(jnp.float32)

@jax.custom_vjp
def low_back(v):
    return v

def low_keep(v):
    return (low(v), None)

def low_pass(kept, grad):
    return (grad,)

def back_keep(v):
    return (v, None)

def back_low(kept, grad):
    return (low(grad),)
low.defvjp(low_keep, low_pass)
low_back.defvjp(back_keep, back_low)
HIGHEST = lax.Precision.HIGHEST
EPSILON = 1e-12
MASKED = -1e+30

def norm_rows(rows, scale_vec, shift_vec):
    average = lax.optimization_barrier(jnp.mean(rows, axis=-1, keepdims=True))
    centred = rows - average
    variance = lax.optimization_barrier(jnp.mean(centred * centred, axis=-1, keepdims=True))
    return centred * lax.rsqrt(variance + EPSILON) * scale_vec + shift_vec

def attend_block(query_block, keys_all, values_all, key_valid):
    scores = jnp.einsum('qhd,khd->hqk', query_block, keys_all, precision=HIGHEST) * HEAD_DIM ** (-0.5)
    scores = low_back(scores)
    scores = jnp.where(key_valid[None, None, :], scores, MASKED)
    probs = jax.nn.softmax(scores, axis=-1)
    return jnp.einsum('hqk,khd->qhd', low(probs), values_all, precision=HIGHEST)

def layer_forward(inputs, key_valid, w_query, w_key, w_value, w_out, w_up, w_down, b_query, b_value, b_out, b_up, b_down, gain_attn, shift_attn, gain_ffn, shift_ffn):
    queries = low(low_back(jnp.dot(inputs, w_query, precision=HIGHEST) + b_query))
    keys_all = low(low_back(jnp.dot(inputs, w_key, precision=HIGHEST)))
    values_all = low(low_back(jnp.dot(inputs, w_value, precision=HIGHEST) + b_value))
    block_rows = min(512, SEQ)
    shaped = queries.reshape(SEQ // block_rows, block_rows, HEADS, HEAD_DIM)
    keys_all = keys_all.reshape(SEQ, HEADS, HEAD_DIM)
    values_all = values_all.reshape(SEQ, HEADS, HEAD_DIM)
    blockwise = jax.checkpoint(partial(attend_block, keys_all=keys_all, values_all=values_all, key_valid=key_valid))
    attended = lax.map(blockwise, shaped)
    attended = low(low_back(attended.reshape(SEQ, D)))
    attn_out = low_back(jnp.dot(attended, w_out, precision=HIGHEST) + b_out)
    normed = norm_rows(inputs + attn_out, gain_attn, shift_attn)
    hidden_pre = low_back(jnp.dot(low(normed), w_up, precision=HIGHEST) + b_up)
    hidden = low(jax.nn.gelu(hidden_pre, approximate=False))
    ffn_out = low_back(jnp.dot(hidden, w_down, precision=HIGHEST) + b_down)
    result = norm_rows(normed + ffn_out, gain_ffn, shift_ffn)
    return (result, (attn_out, ffn_out))

def reference(tokens, seq_lengths, positions, w_query, w_key, w_value, w_out, w_up, w_down, b_query, b_value, b_out, b_up, b_down, gain_attn, shift_attn, gain_ffn, shift_ffn, out_grad):
    weights = tuple((element.astype(jnp.float32) for element in (w_query, w_key, w_value, w_out, w_up, w_down, b_query, b_value, b_out, b_up, b_down, gain_attn, shift_attn, gain_ffn, shift_ffn)))
    inputs_all = tokens.astype(jnp.float32).reshape(N_DP, SEQ, D)
    cotangents = out_grad.astype(jnp.float32).reshape(N_DP, SEQ, D)
    valid_all = positions < seq_lengths[:, None]

    def per_group(totals, element):
        inputs, cotangent, key_valid = element

        def wrapped(inputs_in, *params):
            return layer_forward(inputs_in, key_valid, *params)
        result, pull_back, extras = jax.vjp(wrapped, inputs, *weights, has_aux=True)
        gradients = pull_back(cotangent)
        row_mask = key_valid[:, None]
        squares = jnp.stack([jnp.sum(jnp.where(row_mask, field * field, jnp.float32(0.0))) for field in (inputs, extras[0], extras[1])])
        new_totals = tuple((total + grad_one for total, grad_one in zip(totals, gradients[1:])))
        return (new_totals, (result, gradients[0], squares))
    initial = tuple((jnp.zeros(weight_one.shape, jnp.float32) for weight_one in weights))
    totals, (results, input_grads, squares) = lax.scan(per_group, initial, (inputs_all, cotangents, valid_all))
    count = jnp.sum(seq_lengths).astype(jnp.float32) * D
    rms = jnp.sqrt(lax.optimization_barrier(jnp.sum(squares, axis=0)) / count)
    return (results.reshape(TOKENS, D).astype(jnp.bfloat16), input_grads.reshape(TOKENS, D).astype(jnp.bfloat16), totals[0], totals[1], totals[2], totals[3], totals[4], totals[5], totals[6], totals[7], totals[8], totals[9], totals[10], totals[11], totals[12], totals[13], totals[14], rms)
```

```python
import functools

import jax
import jax.numpy as jnp
from jax import lax
from jax.experimental import pallas as pl
from jax.experimental.pallas import tpu as pltpu
from jax.sharding import PartitionSpec as P

HEAD_DIM = 64
LANES = 128
EPSILON = 1e-12
MASKED = -1e30
BF16 = jnp.bfloat16
F32 = jnp.float32
NT = (((1,), (1,)), ((), ()))
TN = (((0,), (0,)), ((), ()))
VMEM_LIMIT = 64 << 20


def dot(left, right):
    return jnp.dot(left, right, preferred_element_type=F32)


def dot_nt(left, right):
    return lax.dot_general(left, right, NT, preferred_element_type=F32)


def dot_tn(left, right):
    return lax.dot_general(left, right, TN, preferred_element_type=F32)


def in_three(column):
    first = column.astype(BF16)
    rest = column - first.astype(F32)
    second = rest.astype(BF16)
    third = (rest - second.astype(F32)).astype(BF16)
    return first, second, third


def swap(value, axis, bits):
    size = lax.axis_size(axis)
    return lax.ppermute(value, axis, [(i, i ^ bits) for i in range(size)])


def bit_of(axis, bit):
    return (lax.axis_index(axis) >> bit) & 1


def gather_bits(block, axis, order, at):
    done = []
    for bit in order:
        place = at + sum(other > bit for other in done)
        got = swap(block, axis, 1 << bit)
        upper = bit_of(axis, bit) == 1
        low = jnp.where(upper, got, block)
        high = jnp.where(upper, block, got)
        block = jnp.stack([low, high], axis=place)
        done.append(bit)
    return block


def scatter_bits(partial, axis, order, at):
    left = sorted(order, reverse=True)
    for bit in order:
        place = at + left.index(bit)
        mine = bit_of(axis, bit)
        away = lax.dynamic_index_in_dim(partial, 1 - mine, place, keepdims=False)
        keep = lax.dynamic_index_in_dim(partial, mine, place, keepdims=False)
        got = swap(away.astype(BF16), axis, 1 << bit)
        partial = keep.astype(F32) + got.astype(F32)
        left.remove(bit)
    return partial


def forward_kernel(*refs, rows, heads):
    x_refs, (w_ref, b_ref, mask_ref), rest = refs[:4], refs[4:7], refs[7:]
    q_out, k_out, v_out, o_out = rest[:4]
    packed = rest[4:8]
    q_s, k_s, v_s = rest[8:]
    seq = 4 * rows
    block = rows // 2
    lane = lax.broadcasted_iota(jnp.int32, (1, LANES), 1)
    head_lane = lane < HEAD_DIM
    one_q = jnp.where(lane == HEAD_DIM, 1.0, 0.0)
    one_k = jnp.where((lane > HEAD_DIM) & (lane <= HEAD_DIM + 3), 1.0, 0.0)
    one_v = jnp.where((lane >= HEAD_DIM) & (lane < HEAD_DIM + 3), 1.0, 0.0)
    for j in range(4):
        part = pl.ds(j * rows, rows)
        both = dot(x_refs[j][...], w_ref[0]) + b_ref[0]
        first = both[:, :LANES]
        second = jnp.concatenate([both[:, LANES:], both[:, LANES:]], axis=1)
        query = first.astype(BF16).astype(F32) * (HEAD_DIM**-0.5)
        q_s[part, :] = jnp.where(head_lane, query, one_q).astype(BF16)
        key = jnp.where(head_lane, pltpu.roll(first, HEAD_DIM, 1), one_k)
        k_s[part, :] = jnp.where(lane == HEAD_DIM, mask_ref[part, :], key).astype(BF16)
        v_s[part, :] = jnp.where(head_lane, second, one_v).astype(BF16)
    k_out[0] = k_s[...]
    v_out[0] = v_s[...]

    def scores_of(i):
        query = q_s[pl.ds(i * block, block), :]
        scores = dot_nt(query, k_s[...])
        return query, scores, jnp.max(scores, axis=-1, keepdims=True)

    def attend(i, query, scores, top):
        expon = jnp.exp(scores - top).astype(BF16)
        total = dot(expon, v_s[...])
        row_sum = total[:, HEAD_DIM : HEAD_DIM + 1]
        out = total * (1.0 / row_sum)
        place = pl.ds(i * block, block)
        o_out[0, place, :] = out
        one, two, three = in_three(-(top + jnp.log(row_sum)))
        q_out[0, place, :] = jnp.where(
            lane == HEAD_DIM + 1,
            one,
            jnp.where(lane == HEAD_DIM + 2, two, jnp.where(lane == HEAD_DIM + 3, three, query)),
        )
        return out

    blocks = seq // block
    held = scores_of(0)
    even = None
    for i in range(blocks):
        following = scores_of(i + 1) if i + 1 < blocks else None
        out = attend(i, *held)
        if i % 2 == 0:
            even = out
        else:
            pair = jnp.where(head_lane, even, pltpu.roll(out, HEAD_DIM, 1))
            packed[i // 2][0] = pair.astype(BF16)
        held = following


def attention_forward(parts, weight, bias, mask):
    rows, width = parts[0].shape
    heads = weight.shape[0]
    seq = 4 * rows
    block = rows // 2
    per_head = pl.BlockSpec((1, seq, LANES), lambda h: (h, 0, 0))
    whole = pl.BlockSpec((rows, width), lambda h: (0, 0))
    piece = pl.BlockSpec((1, block, LANES), lambda h: (h, 0, 0))
    kept = jax.ShapeDtypeStruct((heads, seq, LANES), BF16)
    return pl.pallas_call(
        functools.partial(forward_kernel, rows=rows, heads=heads),
        grid=(heads,),
        in_specs=[whole] * 4
        + [
            pl.BlockSpec((1,) + weight.shape[1:], lambda h: (h, 0, 0)),
            pl.BlockSpec((1,) + bias.shape[1:], lambda h: (h, 0, 0)),
            pl.BlockSpec((seq, LANES), lambda h: (0, 0)),
        ],
        out_specs=[per_head] * 4 + [piece] * 4,
        out_shape=[kept, kept, kept, jax.ShapeDtypeStruct((heads, seq, LANES), F32)]
        + [jax.ShapeDtypeStruct((heads, block, LANES), BF16)] * 4,
        scratch_shapes=[pltpu.VMEM((seq, LANES), BF16)] * 3,
        compiler_params=pltpu.CompilerParams(vmem_limit_bytes=VMEM_LIMIT - (1 << 20)),
        cost_estimate=pl.CostEstimate(
            flops=heads * (4 * seq * seq * 256 + 2 * seq * width * 256),
            bytes_accessed=8 << 20,
            transcendentals=heads * seq * seq,
        ),
        name="attention_forward",
    )(*parts, weight, bias, mask)


def backward_kernel(*refs, rows, heads):
    q_ref, k_ref, v_ref, o_ref = refs[:4]
    d_refs, x_refs, w_ref = refs[4:8], refs[8:12], refs[12]
    gw_ref, gb_ref = refs[13:15]
    dx_refs = refs[15:19]
    x_t, dx_s, dk_s, dv_s, g_s = refs[19:]
    seq = 4 * rows
    block = rows // 2
    head = pl.program_id(0)
    lane = lax.broadcasted_iota(jnp.int32, (1, LANES), 1)
    head_lane = lane < HEAD_DIM
    scale = HEAD_DIM**-0.5

    @pl.when(head == 0)
    def _():
        for j in range(4):
            x_t[:, j * rows : (j + 1) * rows] = x_refs[j][...].T

    for i in range(seq // block):
        place = pl.ds(i * block, block)
        query = q_ref[0, place, :]
        grad = d_refs[i // 2][0].astype(F32)
        if i % 2 == 1:
            grad = pltpu.roll(grad, HEAD_DIM, 1)
        grad = jnp.where(head_lane, grad, 0.0)
        delta = jnp.sum(grad * o_ref[0, place, :], axis=-1, keepdims=True)
        one, two, three = in_three(-delta)
        grad = grad.astype(BF16)
        grad_and = jnp.where(
            lane == HEAD_DIM,
            one,
            jnp.where(lane == HEAD_DIM + 1, two, jnp.where(lane == HEAD_DIM + 2, three, grad)),
        )
        probs = jnp.exp(dot_nt(k_ref[0], query))
        lifted = dot_nt(v_ref[0], grad_and)
        grad_scores = (probs * lifted).astype(BF16)
        values_part = dot(probs.astype(BF16), grad)
        keys_part = dot(grad_scores, query)
        if i == 0:
            dv_s[...] = values_part
            dk_s[...] = keys_part
        else:
            dv_s[...] += values_part
            dk_s[...] += keys_part
        grad_query = dot_tn(grad_scores, k_ref[0]) * scale
        g_s[place, :LANES] = jnp.where(head_lane, grad_query, 0.0).astype(BF16)
    both = jnp.where(head_lane, g_s[:, :LANES].astype(F32), pltpu.roll(dk_s[...], HEAD_DIM, 1))
    g_s[:, :LANES] = both.astype(BF16)
    g_s[:, LANES:] = dv_s[:, :HEAD_DIM].astype(BF16)
    grads = g_s[...]
    gb_ref[0] = jnp.sum(grads.astype(F32), axis=0, keepdims=True)
    gw_ref[0] = dot(x_t[...], grads).astype(BF16)
    for j in range(4):
        part = pl.ds(j * rows, rows)
        passed = dot_nt(g_s[part, :], w_ref[0])

        @pl.when(head == 0)
        def _():
            dx_s[part, :] = passed

        @pl.when((head > 0) & (head < heads - 1))
        def _():
            dx_s[part, :] += passed

        @pl.when(head == heads - 1)
        def _():
            dx_refs[j][...] = (dx_s[part, :] + passed).astype(BF16)


def attention_backward(kept, grads, parts, weight):
    rows, width = parts[0].shape
    heads = weight.shape[0]
    seq = 4 * rows
    block = rows // 2
    per_head = pl.BlockSpec((1, seq, LANES), lambda h: (h, 0, 0))
    whole = pl.BlockSpec((rows, width), lambda h: (0, 0))
    piece = pl.BlockSpec((1, block, LANES), lambda h: (h, 0, 0))
    three = 3 * HEAD_DIM
    w_spec = pl.BlockSpec((1, width, three), lambda h: (h, 0, 0))
    return pl.pallas_call(
        functools.partial(backward_kernel, rows=rows, heads=heads),
        grid=(heads,),
        in_specs=[per_head] * 4 + [piece] * 4 + [whole] * 4 + [w_spec],
        out_specs=[w_spec, pl.BlockSpec((1, 1, three), lambda h: (h, 0, 0))] + [whole] * 4,
        out_shape=[
            jax.ShapeDtypeStruct((heads, width, three), BF16),
            jax.ShapeDtypeStruct((heads, 1, three), F32),
        ]
        + [jax.ShapeDtypeStruct((rows, width), BF16)] * 4,
        scratch_shapes=[
            pltpu.VMEM((width, seq), BF16),
            pltpu.VMEM((seq, width), F32),
            pltpu.VMEM((seq, LANES), F32),
            pltpu.VMEM((seq, LANES), F32),
            pltpu.VMEM((seq, three), BF16),
        ],
        compiler_params=pltpu.CompilerParams(vmem_limit_bytes=VMEM_LIMIT - (1 << 20)),
        cost_estimate=pl.CostEstimate(
            flops=heads * (10 * seq * seq * 256 + 4 * seq * width * 256),
            bytes_accessed=16 << 20,
            transcendentals=heads * seq * seq,
        ),
        name="attention_backward",
    )(*kept, *grads, *parts, weight)


def middle_kernel(*refs, rows, width, pieces):
    att = refs[:4]
    x_ref, og_ref, mask_ref, wo_ref, up_ref, down_ref, bup_ref, vec_ref = refs[4:12]
    lo_ref, done_ref, sums_ref, gbup_ref, gup_ref, gdown_ref, gout_ref = refs[12:19]
    ga = refs[19:23]
    att_s, wo_s, hid_s, slope_s, nrm_s, nb_s, n1_s, rs_s, ffn_s, gf_s, gft_s, nbt_s, acc_s, pre_s = (
        refs[23:]
    )
    step = pl.program_id(0)
    chunk = 128
    cols = width // pieces
    lane = lax.broadcasted_iota(jnp.int32, (1, LANES), 1)
    head_lane = lane < HEAD_DIM
    half = rows // 2
    b_out, b_down, gain_a, shift_a, gain_f, shift_f = (vec_ref[i : i + 1, :] for i in range(6))

    def row_loop(work):
        @pl.loop(0, rows // chunk)
        def _(i):
            work(pl.ds(pl.multiple_of(i * chunk, chunk), chunk))

    def add_sum(index, value):
        sums_ref[index : index + 1, :] += jnp.sum(value, axis=0, keepdims=True)

    def mean(value):
        return jnp.mean(value, axis=-1, keepdims=True)

    def normal(value):
        centred = value - mean(value)
        inverse = lax.rsqrt(mean(centred * centred) + EPSILON)
        return centred * inverse, inverse

    def norm_back(grad, unit, inverse, gain):
        scaled = grad * gain
        return (scaled - mean(scaled) - unit * mean(scaled * unit)) * inverse

    @pl.when(step == 0)
    def _():
        sums_ref[...] = jnp.zeros_like(sums_ref)
        for j in range(pieces):
            for h in range(cols // HEAD_DIM):
                at = j * cols + h * HEAD_DIM
                att_s[:half, at : at + HEAD_DIM] = att[j][h][:, :HEAD_DIM]
                att_s[half:, at : at + HEAD_DIM] = att[j][h][:, HEAD_DIM:]
            wo_s[:, j * cols : (j + 1) * cols] = wo_ref[j]
        ffn_s[...] = dot_nt(att_s[...], wo_s[...])

        def first_norm(r):
            value = x_ref[r, :].astype(F32)
            attn = ffn_s[r, :] + b_out
            valid = mask_ref[r, :1] > 0.0
            add_sum(6, jnp.where(valid, value * value, 0.0))
            add_sum(7, jnp.where(valid, attn * attn, 0.0))
            unit, inverse = normal(value + attn)
            normed = unit * gain_a + shift_a
            n1_s[r, :] = unit
            rs_s[r, :] = jnp.broadcast_to(inverse, (chunk, LANES))
            nrm_s[r, :] = normed
            nb_s[r, :] = normed.astype(BF16)

        row_loop(first_norm)

    @pl.when(step < pieces)
    def _():
        pre_s[...] = dot(nb_s[...], up_ref[0]) + bup_ref[0]

        def gelu(r):
            pre = pre_s[r, :]
            cdf = 0.5 * (1.0 + lax.erf(pre * (0.5**0.5)))
            pdf = jnp.exp(pre * pre * -0.5) * (2.0 * jnp.pi) ** -0.5
            hid_s[step, r, :] = (pre * cdf).astype(BF16)
            slope_s[step, r, :] = cdf + pre * pdf

        row_loop(gelu)
        part = dot_nt(hid_s[step], down_ref[0])

        @pl.when(step == 0)
        def _():
            ffn_s[...] = part

        @pl.when(step > 0)
        def _():
            ffn_s[...] += part

    @pl.when(step == pieces - 1)
    def _():
        def second_norm(r):
            ffn = ffn_s[r, :] + b_down
            valid = mask_ref[r, :1] > 0.0
            add_sum(8, jnp.where(valid, ffn * ffn, 0.0))
            unit, inverse = normal(nrm_s[r, :] + ffn)
            lo_ref[r, :] = (unit * gain_f + shift_f).astype(BF16)
            grad = og_ref[r, :].astype(F32)
            add_sum(4, grad * unit)
            add_sum(5, grad)
            d_two = norm_back(grad, unit, inverse, gain_f)
            low = d_two.astype(BF16)
            add_sum(1, low.astype(F32))
            acc_s[r, :] = d_two
            gf_s[r, :] = low

        row_loop(second_norm)
        gft_s[...] = gf_s[...].T
        nbt_s[...] = nb_s[...].T

    @pl.when(step >= pieces)
    def _():
        j = 2 * pieces - 1 - step
        grad_hidden = dot(gf_s[...], down_ref[0])
        pre_s[...] = grad_hidden * slope_s[j]
        low = pre_s[...].astype(BF16)
        gbup_ref[0] = jnp.sum(low.astype(F32), axis=0, keepdims=True)
        gdown_ref[0] = dot(gft_s[...], hid_s[j]).astype(BF16)
        gup_ref[0] = dot(nbt_s[...], low).astype(BF16)
        acc_s[...] += dot_nt(low, up_ref[0])

    @pl.when(step == 2 * pieces - 1)
    def _():
        def first_back(r):
            grad = acc_s[r, :]
            unit = n1_s[r, :]
            add_sum(2, grad * unit)
            add_sum(3, grad)
            d_one = norm_back(grad, unit, rs_s[r, :1], gain_a)
            low = d_one.astype(BF16)
            add_sum(0, low.astype(F32))
            done_ref[r, :] = d_one
            gf_s[r, :] = low

        row_loop(first_back)
        low = gf_s[...]
        gout = dot_tn(low, att_s[...])
        for j in range(pieces):
            gout_ref[j] = gout[:, j * cols : (j + 1) * cols].astype(BF16)
        back = dot(low, wo_s[...]).astype(BF16)
        for j in range(pieces):
            for h in range(cols // HEAD_DIM):
                at = j * cols + h * HEAD_DIM
                ga[j][h, :, :HEAD_DIM] = back[:half, at : at + HEAD_DIM]
                ga[j][h, :, HEAD_DIM:] = back[half:, at : at + HEAD_DIM]


def middle(att, tokens, out_grad, row_mask, w_out, w_up, w_down, b_up, vectors):
    rows, width = tokens.shape
    pieces = w_up.shape[0]
    hidden = w_up.shape[2]
    heads, half, _ = att[0].shape
    cols = width // pieces

    def fixed(shape):
        return pl.BlockSpec(shape, lambda s: (0,) * len(shape))

    def chunked(shape):
        return pl.BlockSpec((1,) + shape, lambda s: (jnp.minimum(s, 2 * pieces - 1 - s), 0, 0))

    def late(shape):
        return pl.BlockSpec((1,) + shape, lambda s: (jnp.minimum(pieces - 1, 2 * pieces - 1 - s), 0, 0))

    shape = jax.ShapeDtypeStruct
    return pl.pallas_call(
        functools.partial(middle_kernel, rows=rows, width=width, pieces=pieces),
        grid=(2 * pieces,),
        in_specs=[fixed(att[0].shape)] * 4
        + [fixed((rows, width))] * 2
        + [
            fixed(row_mask.shape),
            fixed(w_out.shape),
            chunked((width, hidden)),
            chunked((width, hidden)),
            chunked((1, hidden)),
            fixed(vectors.shape),
        ],
        out_specs=[
            fixed((rows, width)),
            fixed((rows, width)),
            fixed((16, width)),
            late((1, hidden)),
            late((width, hidden)),
            late((width, hidden)),
            fixed((pieces, width, cols)),
        ]
        + [fixed(att[0].shape)] * 4,
        out_shape=[
            shape((rows, width), BF16),
            shape((rows, width), F32),
            shape((16, width), F32),
            shape((pieces, 1, hidden), F32),
            shape((pieces, width, hidden), BF16),
            shape((pieces, width, hidden), BF16),
            shape((pieces, width, cols), BF16),
        ]
        + [shape(att[0].shape, BF16)] * 4,
        scratch_shapes=[
            pltpu.VMEM((rows, width), BF16),
            pltpu.VMEM((width, width), BF16),
            pltpu.VMEM((pieces, rows, hidden), BF16),
            pltpu.VMEM((pieces, rows, hidden), F32),
            pltpu.VMEM((rows, width), F32),
            pltpu.VMEM((rows, width), BF16),
            pltpu.VMEM((rows, width), F32),
            pltpu.VMEM((rows, LANES), F32),
            pltpu.VMEM((rows, width), F32),
            pltpu.VMEM((rows, width), BF16),
            pltpu.VMEM((width, rows), BF16),
            pltpu.VMEM((width, rows), BF16),
            pltpu.VMEM((rows, width), F32),
            pltpu.VMEM((rows, hidden), F32),
        ],
        compiler_params=pltpu.CompilerParams(vmem_limit_bytes=VMEM_LIMIT - (1 << 20)),
        cost_estimate=pl.CostEstimate(
            flops=6 * rows * width * (width + 2 * pieces * hidden),
            bytes_accessed=48 << 20,
            transcendentals=rows * pieces * hidden,
        ),
        name="middle",
    )(*att, tokens, out_grad, row_mask, w_out, w_up, w_down, b_up, vectors)


def body(
    tokens,
    seq_lengths,
    positions,
    w_query,
    w_key,
    w_value,
    w_out,
    w_up,
    w_down,
    b_query,
    b_value,
    b_out,
    b_up,
    b_down,
    gain_attn,
    shift_attn,
    gain_ffn,
    shift_ffn,
    out_grad,
):
    group = lax.axis_index("dp")
    member = lax.axis_index("tensor")
    dp_count = lax.axis_size("dp")
    bits = dp_count.bit_length() - 1
    down_order = list(range(bits))[::-1]
    rows, width = tokens.shape
    own_cols = w_query.shape[1]
    heads = own_cols // HEAD_DIM
    share = w_query.shape[0]
    hidden = w_up.shape[1]

    across = swap(tokens, "tensor", 2)
    parts = [tokens, swap(tokens, "tensor", 1), across, swap(across, "tensor", 1)]

    by_head = [w.reshape(share, heads, HEAD_DIM) for w in (w_query, w_key, w_value)]
    own_qkv = jnp.stack(by_head, axis=2).reshape(share, heads, 3 * HEAD_DIM).transpose(1, 0, 2)
    w_qkv = gather_bits(own_qkv, "dp", down_order, 1).reshape(heads, width, 3 * HEAD_DIM)

    bias_q = b_query.astype(F32).reshape(heads, HEAD_DIM)
    bias_v = b_value.astype(F32).reshape(heads, HEAD_DIM)
    bias = jnp.stack([bias_q, jnp.zeros_like(bias_q), bias_v], axis=1).reshape(heads, 1, 3 * HEAD_DIM)

    length = lax.dynamic_index_in_dim(seq_lengths, group, 0, keepdims=False)
    valid = (positions[0] < length).reshape(4, rows)
    valid = jnp.stack([lax.dynamic_index_in_dim(valid, member ^ j, 0, keepdims=False) for j in range(4)])
    key_bias = jnp.where(valid.reshape(4 * rows, 1), 0.0, MASKED).astype(F32)
    key_mask = jnp.broadcast_to(key_bias, (4 * rows, LANES))
    row_mask = jnp.broadcast_to(valid[0][:, None].astype(F32), (rows, LANES))

    q, k, v, attended_f, *pieces = attention_forward(parts, w_qkv, bias, key_mask)

    rest = jnp.concatenate([w_up, w_down.T, w_out.T], axis=1)
    rest = gather_bits(rest, "dp", down_order, 0).reshape(width, -1)
    beyond = swap(rest, "tensor", 2)
    packs = [rest, swap(rest, "tensor", 1), beyond, swap(beyond, "tensor", 1)]
    up_all = jnp.stack([pack[:, :hidden] for pack in packs])
    down_all = jnp.stack([pack[:, hidden : 2 * hidden] for pack in packs])
    out_all = jnp.stack([pack[:, 2 * hidden :] for pack in packs])
    own_b_up = b_up.astype(F32).reshape(1, hidden)
    b_up_all = jnp.stack([own_b_up] + [swap(own_b_up, "tensor", j) for j in (1, 2, 3)])
    vectors = jnp.stack(
        [vec.astype(F32) for vec in (b_out, b_down, gain_attn, shift_attn, gain_ffn, shift_ffn)] + [jnp.zeros((width,), F32)] * 2
    )
    att = [pieces[0]] + [swap(pieces[j], "tensor", j) for j in (1, 2, 3)]
    layer_out, d_one, sums, g_b_up, g_up, g_down, g_out, *back = middle(
        att, tokens, out_grad, row_mask, out_all, up_all, down_all, b_up_all, vectors
    )
    grads = [back[0]] + [swap(back[j], "tensor", j) for j in (1, 2, 3)]

    g_qkv, g_bias, *dx = attention_backward((q, k, v, attended_f), grads, parts, w_qkv)

    near = [dx[0].astype(F32) + swap(dx[1], "tensor", 1).astype(F32)]
    far = (dx[2].astype(F32) + swap(dx[3], "tensor", 1).astype(F32)).astype(BF16)
    input_grad = (d_one + near[0] + swap(far, "tensor", 2).astype(F32)).astype(BF16)

    packs = jnp.concatenate([g_up, g_down, g_out], axis=2)
    got = swap(packs[1::2], "tensor", 1)
    packs = packs[0::2].astype(F32) + got.astype(F32)
    pack = packs[0] + swap(packs[1].astype(BF16), "tensor", 2).astype(F32)
    two = (2,) * bits
    pack = scatter_bits(pack.reshape(two + (share, -1)), "dp", list(range(bits)), 0)
    g_qkv = scatter_bits(g_qkv.reshape((heads,) + two + (share, -1)), "dp", list(range(bits)), 1)
    g_qkv = g_qkv.reshape(heads, share, 3, HEAD_DIM)
    g_q, g_k, g_v = (g_qkv[:, :, i].transpose(1, 0, 2).reshape(share, own_cols) for i in range(3))

    small = jnp.concatenate([sums[:9], jnp.zeros((1, width), F32)])
    ups = g_b_up[:, 0]
    sent = jnp.concatenate([small, ups[1:2], ups[3:4]])
    got = swap(sent, "tensor", 1)
    small, ups = small + got[:10], ups[0::2] + got[10:]
    got = swap(jnp.concatenate([small, ups[1:2]]), "tensor", 2)
    small = jnp.concatenate([small + got[:10], ups[:1] + got[10:]])
    bias_rows = g_bias.reshape(heads, 3, HEAD_DIM)
    for bit in range(bits):
        small = small + swap(small, "dp", 1 << bit)
        bias_rows = bias_rows + swap(bias_rows, "dp", 1 << bit)
    count = jnp.sum(seq_lengths).astype(F32) * width
    rms = jnp.sqrt(jnp.sum(small[6:9], axis=-1) / count)
    return (
        layer_out,
        input_grad,
        g_q,
        g_k,
        g_v,
        pack[:, 2 * hidden :].T,
        pack[:, :hidden],
        pack[:, hidden : 2 * hidden].T,
        bias_rows[:, 0].reshape(own_cols),
        bias_rows[:, 2].reshape(own_cols),
        small[0],
        small[10],
        small[1],
        small[2],
        small[3],
        small[4],
        small[5],
        rms,
    )


def solution(mesh):
    in_specs = (
        P(("dp", "tensor"), None),
        P(),
        P("dp", None),
        P("dp", "tensor"),
        P("dp", "tensor"),
        P("dp", "tensor"),
        P("tensor", "dp"),
        P("dp", "tensor"),
        P("tensor", "dp"),
        P("tensor"),
        P("tensor"),
        P(),
        P("tensor"),
        P(),
        P(),
        P(),
        P(),
        P(),
        P(("dp", "tensor"), None),
    )
    out_specs = (
        P(("dp", "tensor"), None),
        P(("dp", "tensor"), None),
        P("dp", "tensor"),
        P("dp", "tensor"),
        P("dp", "tensor"),
        P("tensor", "dp"),
        P("dp", "tensor"),
        P("tensor", "dp"),
        P("tensor"),
        P("tensor"),
        P(),
        P("tensor"),
        P(),
        P(),
        P(),
        P(),
        P(),
        P(),
    )
    return jax.shard_map(body, mesh=mesh, in_specs=in_specs, out_specs=out_specs, check_vma=False)
```

```python
import functools

import jax
import jax.numpy as jnp
from jax import lax
from jax.experimental import pallas as pl
from jax.experimental.pallas import tpu as pltpu
from jax.sharding import PartitionSpec as P

HEAD_DIM = 64
LANES = 128
EPSILON = 1e-12
MASKED = -1e30
BF16 = jnp.bfloat16
F32 = jnp.float32
NT = (((1,), (1,)), ((), ()))
TN = (((0,), (0,)), ((), ()))
VMEM_LIMIT = 64 << 20


def dot(left, right):
    return jnp.dot(left, right, preferred_element_type=F32)


def dot_nt(left, right):
    return lax.dot_general(left, right, NT, preferred_element_type=F32)


def dot_tn(left, right):
    return lax.dot_general(left, right, TN, preferred_element_type=F32)


def place_of(mask, height, placed):
    start = (lax.axis_index("dp") ^ mask) * height if placed else 0
    return pl.ds(pl.multiple_of(start, height), height)


def valid_row(positions_ref, lengths_ref, j, rows):
    start = (lax.axis_index("tensor") ^ j) * rows
    own = positions_ref[:, pl.ds(pl.multiple_of(start, rows), rows)]
    return own < lengths_ref[lax.axis_index("dp")]


def in_three(column):
    first = column.astype(BF16)
    rest = column - first.astype(F32)
    second = rest.astype(BF16)
    third = (rest - second.astype(F32)).astype(BF16)
    return first, second, third


def swap(value, axis, bits):
    size = lax.axis_size(axis)
    return lax.ppermute(value, axis, [(i, i ^ bits) for i in range(size)])


def bit_of(axis, bit):
    return (lax.axis_index(axis) >> bit) & 1


def gather_bits(block, axis, order, at):
    done = []
    for bit in order:
        place = at + sum(other > bit for other in done)
        got = swap(block, axis, 1 << bit)
        upper = bit_of(axis, bit) == 1
        low = jnp.where(upper, got, block)
        high = jnp.where(upper, block, got)
        block = jnp.stack([low, high], axis=place)
        done.append(bit)
    return block


def scatter_bits(partial, axis, order, at):
    left = sorted(order, reverse=True)
    for bit in order:
        place = at + left.index(bit)
        mine = bit_of(axis, bit)
        away = lax.dynamic_index_in_dim(partial, 1 - mine, place, keepdims=False)
        keep = lax.dynamic_index_in_dim(partial, mine, place, keepdims=False)
        got = swap(away.astype(BF16), axis, 1 << bit)
        partial = keep.astype(F32) + got.astype(F32)
        left.remove(bit)
    return partial


def after(value, *others):
    return lax.optimization_barrier((value,) + others)[0]


def params():
    return pltpu.CompilerParams(vmem_limit_bytes=VMEM_LIMIT - (1 << 20))


def cost(flops, moved, exps=0):
    return pl.CostEstimate(flops=flops, bytes_accessed=moved, transcendentals=exps)


SMEM_SPEC = pl.BlockSpec(memory_space=pltpu.SMEM)
VMEM_SPEC = pl.BlockSpec(memory_space=pltpu.VMEM)
ANY_SPEC = pl.BlockSpec(memory_space=pl.ANY)


def project_kernel(*refs, masks, heads, placed):
    x_refs, w_refs = refs[:4], refs[4 : 4 + len(masks)]
    bq_ref, bv_ref, positions_ref, lengths_ref, q_out, k_out, v_out, w_s = refs[4 + len(masks) :]
    rows = x_refs[0].shape[0]
    for ref, entries in zip(w_refs, masks, strict=True):
        for z, mask in enumerate(entries):
            w_s[place_of(mask, ref.shape[1], placed), :] = ref[z]
    lane = lax.broadcasted_iota(jnp.int32, (1, LANES), 1)
    head_lane = lane < HEAD_DIM
    one_q = jnp.where(lane == HEAD_DIM, 1.0, 0.0)
    one_k = jnp.where((lane > HEAD_DIM) & (lane <= HEAD_DIM + 3), 1.0, 0.0)
    one_v = jnp.where((lane >= HEAD_DIM) & (lane < HEAD_DIM + 3), 1.0, 0.0)
    b_query = bq_ref[...].astype(F32)
    bias = jnp.concatenate([b_query, jnp.zeros_like(b_query), bv_ref[...].astype(F32)], axis=1)
    for j in range(4):
        part = pl.ds(j * rows, rows)
        whole = dot(x_refs[j][...], w_s[...]) + bias
        masked = jnp.where(valid_row(positions_ref, lengths_ref, j, rows), 0.0, MASKED)
        masked = jnp.broadcast_to(masked, (LANES, rows)).T

        def columns(group):
            start = group // 2 * LANES
            both = whole[:, start : start + LANES]
            if both.shape[1] < LANES:
                both = jnp.concatenate([both, both], axis=1)
            return pltpu.roll(both, HEAD_DIM, 1) if group % 2 else both

        for h in range(heads):
            query = columns(h).astype(BF16).astype(F32) * (HEAD_DIM**-0.5)
            q_out[h, part, :] = jnp.where(head_lane, query, one_q).astype(BF16)
            key = jnp.where(head_lane, columns(heads + h), one_k)
            k_out[h, part, :] = jnp.where(lane == HEAD_DIM, masked, key).astype(BF16)
            value = jnp.where(head_lane, columns(2 * heads + h), one_v)
            v_out[h, part, :] = value.astype(BF16)


def project(parts, pieces, masks, b_query, b_value, positions, lengths, heads, placed):
    rows, width = parts[0].shape
    seq = 4 * rows
    return pl.pallas_call(
        functools.partial(project_kernel, masks=masks, heads=heads, placed=placed),
        in_specs=[VMEM_SPEC] * (7 + len(pieces)) + [SMEM_SPEC],
        out_specs=[VMEM_SPEC] * 3,
        out_shape=[jax.ShapeDtypeStruct((heads, seq, LANES), BF16)] * 3,
        scratch_shapes=[pltpu.VMEM((width, pieces[0].shape[2]), BF16)],
        compiler_params=params(),
        cost_estimate=cost(1000, 1000),
        name="project",
    )(*parts, *pieces, b_query, b_value, positions, lengths)


def forward_kernel(q_ref, k_ref, v_ref, *refs, unroll):
    q_out, o_out, own, near, far, packed = refs[-6:]
    seq = q_ref.shape[1]
    block = seq // 8
    lane = lax.broadcasted_iota(jnp.int32, (1, LANES), 1)
    head_lane = lane < HEAD_DIM

    def place(i):
        return pl.ds(pl.multiple_of(i * block, block), block)

    def scores_of(i):
        query = q_ref[0, place(i), :]
        scores = dot_nt(query, k_ref[0])
        return query, scores, jnp.max(scores, axis=-1, keepdims=True)

    def attend(i, query, scores, top):
        expon = jnp.exp(scores - top).astype(BF16)
        total = dot(expon, v_ref[0])
        row_sum = total[:, HEAD_DIM : HEAD_DIM + 1]
        out = total * (1.0 / row_sum)
        o_out[place(i), :] = out
        one, two, three = in_three(-(top + jnp.log(row_sum)))
        q_out[place(i), :] = jnp.where(
            lane == HEAD_DIM + 1,
            one,
            jnp.where(lane == HEAD_DIM + 2, two, jnp.where(lane == HEAD_DIM + 3, three, query)),
        )
        return out

    @pl.loop(0, 8 // unroll)
    def _(step):
        held = scores_of(step * unroll)
        even = None
        for u in range(unroll):
            i = step * unroll + u
            following = scores_of(i + 1) if u < unroll - 1 else None
            out = attend(i, *held)
            if u % 2 == 0:
                even = out
            else:
                pair = jnp.where(head_lane, even, pltpu.roll(out, HEAD_DIM, 1))
                packed[step * (unroll // 2) + u // 2] = pair.astype(BF16)
            held = following

    own[0] = packed[0]
    near[0] = packed[1]
    far[0, 0] = packed[2]
    far[1, 0] = packed[3]


def attention_forward(head, q, k, v, packed):
    heads, seq, _ = q.shape
    block = seq // 8
    one = pl.BlockSpec((1, seq, LANES), lambda i: (head, 0, 0))
    flat = pl.BlockSpec((seq, LANES), lambda i: (0, 0))
    piece = pl.BlockSpec((1, block, LANES), lambda i: (head, 0, 0))
    pieces = pl.BlockSpec((2, 1, block, LANES), lambda i: (0, head, 0, 0))
    shape = jax.ShapeDtypeStruct
    q_kept, out, *packed = pl.pallas_call(
        functools.partial(forward_kernel, unroll=4),
        grid=(1,),
        in_specs=[one] * 3 + [ANY_SPEC] * len(packed),
        out_specs=[flat, flat, piece, piece, pieces],
        out_shape=[shape((seq, LANES), BF16), shape((seq, LANES), F32)]
        + [shape((heads, block, LANES), BF16)] * 2
        + [shape((2, heads, block, LANES), BF16)],
        scratch_shapes=[pltpu.VMEM((4, block, LANES), BF16)],
        input_output_aliases={3 + i: 2 + i for i in range(len(packed))},
        compiler_params=params(),
        cost_estimate=cost(1000, 1000),
        name="attention_forward",
    )(q, k, v, *packed)
    return q_kept, out, packed


def backward_kernel(q_ref, k_ref, v_ref, o_ref, *refs, placed):
    d_refs, x_refs = refs[:4], refs[4:8]
    g_ref, gb_ref, gw_ref, dk_s, dv_s, gw_s, d_s = refs[-7:]
    seq = q_ref.shape[0]
    block = seq // 8
    rows = seq // 4
    lane = lax.broadcasted_iota(jnp.int32, (1, LANES), 1)
    head_lane = lane < HEAD_DIM
    scale = HEAD_DIM**-0.5
    for j in range(4):
        d_s[j] = d_refs[j][0]
    dk_s[...] = jnp.zeros_like(dk_s)
    dv_s[...] = jnp.zeros_like(dv_s)

    @pl.loop(0, 4)
    def _(j):
        for half in range(2):
            place = pl.ds(pl.multiple_of((2 * j + half) * block, block), block)
            query = q_ref[place, :]
            grad = d_s[j].astype(F32)
            if half == 1:
                grad = pltpu.roll(grad, HEAD_DIM, 1)
            grad = jnp.where(head_lane, grad, 0.0)
            delta = jnp.sum(grad * o_ref[place, :], axis=-1, keepdims=True)
            one, two, three = in_three(-delta)
            grad = grad.astype(BF16)
            grad_and = jnp.where(
                lane == HEAD_DIM,
                one,
                jnp.where(lane == HEAD_DIM + 1, two, jnp.where(lane == HEAD_DIM + 2, three, grad)),
            )
            probs = jnp.exp(dot_nt(k_ref[0], query))
            lifted = dot_nt(v_ref[0], grad_and)
            grad_scores = (probs * lifted).astype(BF16)
            dv_s[...] += dot(probs.astype(BF16), grad)
            dk_s[...] += dot(grad_scores, query)
            grad_query = dot_tn(grad_scores, k_ref[0]) * scale
            g_ref[0, place, :LANES] = jnp.where(head_lane, grad_query, 0.0).astype(BF16)

    both = jnp.where(head_lane, g_ref[0, :, :LANES].astype(F32), pltpu.roll(dk_s[...], HEAD_DIM, 1))
    g_ref[0, :, :LANES] = both.astype(BF16)
    g_ref[0, :, LANES:] = dv_s[:, :HEAD_DIM].astype(BF16)
    grads = g_ref[0]
    gb_ref[...] = jnp.sum(grads.astype(F32), axis=0, keepdims=True)
    total = dot_tn(grads[:rows], x_refs[0][...])
    for j in range(1, 4):
        total += dot_tn(grads[j * rows : (j + 1) * rows], x_refs[j][...])
    gw_s[...] = total.T.astype(BF16)
    for i in range(gw_ref.shape[1]):
        gw_ref[0, i] = gw_s[place_of(i, gw_ref.shape[2], placed), :]


def attention_backward(head, q, k, v, out, grads, parts, blocks, before):
    heads, seq, _ = k.shape
    rows, width = parts[0].shape
    one = pl.BlockSpec((1, seq, LANES), lambda i: (head, 0, 0))
    flat = pl.BlockSpec((seq, LANES), lambda i: (0, 0))
    piece = pl.BlockSpec((1, seq // 8, LANES), lambda i: (head, 0, 0))
    whole = pl.BlockSpec((rows, width), lambda i: (0, 0))
    three = 3 * HEAD_DIM
    share = width // blocks
    shape = jax.ShapeDtypeStruct
    alias = {12: 0, 13: 2} if before else {}
    return pl.pallas_call(
        functools.partial(backward_kernel, placed=blocks > 1),
        grid=(1,),
        in_specs=[flat, one, one, flat] + [piece] * 4 + [whole] * 4 + [ANY_SPEC] * len(before),
        out_specs=[
            pl.BlockSpec((1, seq, three), lambda i: (head, 0, 0)),
            pl.BlockSpec((1, three), lambda i: (0, 0)),
            pl.BlockSpec((1, blocks, share, three), lambda i: (head, 0, 0, 0)),
        ],
        out_shape=[
            shape((heads, seq, three), BF16),
            shape((1, three), F32),
            shape((heads, blocks, share, three), BF16),
        ],
        scratch_shapes=[
            pltpu.VMEM((seq, LANES), F32),
            pltpu.VMEM((seq, LANES), F32),
            pltpu.VMEM((width, three), BF16),
            pltpu.VMEM((4, seq // 8, LANES), BF16),
        ],
        input_output_aliases=alias,
        compiler_params=params(),
        cost_estimate=cost(1000, 1000),
        name="attention_backward",
    )(q, k, v, out, *grads, *parts, *before)


def input_kernel(g_ref, *refs, masks, which, placed):
    w_refs = refs[: len(masks)]
    outs, w_s = refs[len(masks) : -1], refs[-1]
    heads, seq, three = g_ref.shape
    rows = seq // 4
    for ref, entries in zip(w_refs, masks, strict=True):
        for z, mask in enumerate(entries):
            place = place_of(mask, ref.shape[1], placed)
            for h in range(heads):
                for kind in range(3):
                    start = (kind * heads + h) * HEAD_DIM
                    stop = (h * 3 + kind) * HEAD_DIM
                    w_s[place, stop : stop + HEAD_DIM] = ref[z, :, start : start + HEAD_DIM]
    for out, j in zip(outs, which, strict=True):
        part = pl.ds(j * rows, rows)
        total = dot_nt(g_ref[0, part, :], w_s[:, :three])
        for h in range(1, heads):
            total += dot_nt(g_ref[h, part, :], w_s[:, h * three : (h + 1) * three])
        out[...] = total.astype(out.dtype)


def input_part(g_all, pieces, masks, which, placed):
    heads, seq, three = g_all.shape
    width = pieces[0].shape[0] * pieces[0].shape[1] * len(pieces)
    return pl.pallas_call(
        functools.partial(input_kernel, masks=masks, which=which, placed=placed),
        in_specs=[VMEM_SPEC] * (1 + len(pieces)),
        out_specs=[VMEM_SPEC] * len(which),
        out_shape=[jax.ShapeDtypeStruct((seq // 4, width), BF16)] * len(which),
        scratch_shapes=[pltpu.VMEM((width, heads * three), BF16)],
        compiler_params=params(),
        cost_estimate=cost(1000, 1000),
        name="input_part",
    )(g_all, *pieces)


def middle_kernel(*refs, plan, blocks):
    w_refs = refs[: len(plan)]
    refs = refs[len(plan) :]
    own_ref, near_ref, far_ref = refs[:3]
    x_ref, og_ref, positions_ref, lengths_ref, vec_ref = refs[3:8]
    lo_ref, done_ref, sums_ref, gbup_ref, sent, kept = refs[8:14]
    ga = refs[14:18]
    w1_s, w2_s, att_s, wo_s, hid_s, slope_s, nrm_s, nb_s, n1_s, rs_s, ffn_s = refs[18:29]
    gf_s, gft_s, nbt_s, acc_s, pre_s, g_s, bup_s, mask_s, in_sem, down_sem, up_sem, out_sem = refs[29:]
    rows, width = x_ref.shape
    hidden = w2_s.shape[2]
    pieces = 4
    cols = width // pieces
    placed = blocks > 1
    chunk = 128
    share = width // blocks
    half = rows // 2
    b_out, b_down, gain_a, shift_a, gain_f, shift_f = (vec_ref[i : i + 1, :] for i in range(6))

    count = cols // HEAD_DIM
    att = [[own_ref[h] for h in range(count)]]
    for ref, i in ((near_ref, 0), (far_ref, 0), (near_ref, 1)):
        att.append([ref[i, h] for h in range(count)])

    loads = []
    for ref, entries in zip(w_refs, plan, strict=True):
        for index, second, j, row in entries:
            source = ref.at[index]
            target = (w2_s if second else w1_s).at[j].at[place_of(row, source.shape[0], placed)]
            copy = pltpu.make_async_copy(source, target, in_sem.at[len(loads)])
            loads.append((second, copy))
            copy.start()

    def row_loop(work):
        @pl.loop(0, rows // chunk)
        def _(i):
            work(pl.ds(pl.multiple_of(i * chunk, chunk), chunk))

    def add_sum(index, value):
        sums_ref[index : index + 1, :] += jnp.sum(value, axis=0, keepdims=True)

    def mean(value):
        return jnp.mean(value, axis=-1, keepdims=True)

    def normal(value):
        centred = value - mean(value)
        inverse = lax.rsqrt(mean(centred * centred) + EPSILON)
        return centred * inverse, inverse

    def norm_back(grad, unit, inverse, gain):
        scaled = grad * gain
        return (scaled - mean(scaled) - unit * mean(scaled * unit)) * inverse

    sums_ref[...] = jnp.zeros_like(sums_ref)
    own_valid = jnp.where(valid_row(positions_ref, lengths_ref, 0, rows), 1.0, 0.0)
    mask_s[...] = jnp.broadcast_to(own_valid, (LANES, rows)).T
    for j in range(pieces):
        for h in range(cols // HEAD_DIM):
            at = j * cols + h * HEAD_DIM
            att_s[:half, at : at + HEAD_DIM] = att[j][h][:, :HEAD_DIM]
            att_s[half:, at : at + HEAD_DIM] = att[j][h][:, HEAD_DIM:]
    for second, copy in loads:
        if not second:
            copy.wait()
    for j in range(pieces):
        wo_s[:, j * cols : (j + 1) * cols] = w1_s[j, :, hidden : hidden + cols]
        last = w1_s[j, :, hidden + cols - HEAD_DIM :].astype(F32)
        bup_s[j] = last.T[HEAD_DIM : HEAD_DIM + 1, :]
    ffn_s[...] = dot_nt(att_s[...], wo_s[...])

    def first_norm(r):
        value = x_ref[r, :].astype(F32)
        attn = ffn_s[r, :] + b_out
        valid = mask_s[r, :1] > 0.0
        add_sum(6, jnp.where(valid, value * value, 0.0))
        add_sum(7, jnp.where(valid, attn * attn, 0.0))
        unit, inverse = normal(value + attn)
        normed = unit * gain_a + shift_a
        n1_s[r, :] = unit
        rs_s[r, :] = jnp.broadcast_to(inverse, (chunk, LANES))
        nrm_s[r, :] = normed
        nb_s[r, :] = normed.astype(BF16)

    row_loop(first_norm)
    ffn_s[...] = jnp.zeros_like(ffn_s)
    for second, copy in loads:
        if second:
            copy.wait()

    @pl.loop(0, pieces)
    def _(j):
        pre_s[...] = dot(nb_s[...], w1_s[j, :, :hidden]) + bup_s[j]

        def gelu(r):
            pre = pre_s[r, :]
            cdf = 0.5 * (1.0 + lax.erf(pre * (0.5**0.5)))
            pdf = jnp.exp(pre * pre * -0.5) * (2.0 * jnp.pi) ** -0.5
            hid_s[j, r, :] = (pre * cdf).astype(BF16)
            slope_s[j, r, :] = cdf + pre * pdf

        row_loop(gelu)
        ffn_s[...] += dot_nt(hid_s[j], w2_s[j])

    def second_norm(r):
        ffn = ffn_s[r, :] + b_down
        valid = mask_s[r, :1] > 0.0
        add_sum(8, jnp.where(valid, ffn * ffn, 0.0))
        unit, inverse = normal(nrm_s[r, :] + ffn)
        lo_ref[r, :] = (unit * gain_f + shift_f).astype(BF16)
        grad = og_ref[r, :].astype(F32)
        add_sum(4, grad * unit)
        add_sum(5, grad)
        d_two = norm_back(grad, unit, inverse, gain_f)
        low = d_two.astype(BF16)
        add_sum(1, low.astype(F32))
        acc_s[r, :] = d_two
        gf_s[r, :] = low

    row_loop(second_norm)
    gft_s[...] = gf_s[...].T
    nbt_s[...] = nb_s[...].T

    places = [place_of(i, share, placed) for i in range(blocks)]

    def copies(j, lanes, target, place, sem):
        return [
            pltpu.make_async_copy(
                g_s.at[j].at[places[i], lanes], target.at[place, i, :, lanes], sem.at[j, i]
            )
            for i in range(blocks)
        ]

    lanes_d, lanes_u, lanes_o = (
        pl.ds(0, hidden),
        pl.ds(hidden, hidden),
        pl.ds(2 * hidden, cols),
    )
    for away, target in ((1, sent), (0, kept)):

        @pl.loop(0, pieces // 2)
        def _(place):
            j = 2 * place + away
            pre_s[...] = dot(gf_s[...], w2_s[j]) * slope_s[j]
            low = pre_s[...].astype(BF16)
            gbup_ref[j] = jnp.sum(low.astype(F32), axis=0, keepdims=True)
            g_s[j, :, lanes_d] = dot(gft_s[...], hid_s[j]).astype(BF16)
            for copy in copies(j, lanes_d, target, place, down_sem):
                copy.start()
            g_s[j, :, lanes_u] = dot(nbt_s[...], low).astype(BF16)
            for copy in copies(j, lanes_u, target, place, up_sem):
                copy.start()
            acc_s[...] += dot_nt(low, w1_s[j, :, :hidden])

    def first_back(r):
        grad = acc_s[r, :]
        unit = n1_s[r, :]
        add_sum(2, grad * unit)
        add_sum(3, grad)
        d_one = norm_back(grad, unit, rs_s[r, :1], gain_a)
        low = d_one.astype(BF16)
        add_sum(0, low.astype(F32))
        done_ref[r, :] = d_one
        gf_s[r, :] = low

    row_loop(first_back)
    low = gf_s[...]
    gout = dot_tn(low, att_s[...]).astype(BF16)
    for j in range(pieces):
        g_s[j, :, 2 * hidden : 2 * hidden + cols] = gout[:, j * cols : (j + 1) * cols]
        for copy in copies(j, lanes_o, sent if j % 2 else kept, j // 2, out_sem):
            copy.start()
    back = dot(low, wo_s[...]).astype(BF16)
    for j in range(pieces):
        for h in range(cols // HEAD_DIM):
            at = j * cols + h * HEAD_DIM
            ga[j][h, :, :HEAD_DIM] = back[:half, at : at + HEAD_DIM]
            ga[j][h, :, HEAD_DIM:] = back[half:, at : at + HEAD_DIM]
    for j in range(pieces):
        target = sent if j % 2 else kept
        for lanes, sem in ((lanes_d, down_sem), (lanes_u, up_sem), (lanes_o, out_sem)):
            for copy in copies(j, lanes, target, j // 2, sem):
                copy.wait()


def middle(blocks, weights, plan, att, tokens, out_grad, positions, lengths, vectors, hidden):
    rows, width = tokens.shape
    cols = width // 4
    share = width // blocks
    shape = jax.ShapeDtypeStruct
    vmem = pltpu.VMEM
    loads = sum(len(entries) for entries in plan)
    return pl.pallas_call(
        functools.partial(middle_kernel, plan=plan, blocks=blocks),
        in_specs=[ANY_SPEC] * len(weights) + [VMEM_SPEC] * 6 + [SMEM_SPEC, VMEM_SPEC],
        out_specs=[VMEM_SPEC] * 4 + [ANY_SPEC] * 2 + [VMEM_SPEC] * 4,
        out_shape=[
            shape((rows, width), BF16),
            shape((rows, width), F32),
            shape((16, width), F32),
            shape((4, 1, hidden), F32),
        ]
        + [shape((2, blocks, share, 2 * hidden + cols), BF16)] * 2
        + [shape(att[0].shape, BF16)] * 4,
        scratch_shapes=[
            vmem((4, width, weights[0].shape[-1]), BF16),
            vmem((4, width, hidden), BF16),
            vmem((rows, width), BF16),
            vmem((width, width), BF16),
            vmem((4, rows, hidden), BF16),
            vmem((4, rows, hidden), F32),
            vmem((rows, width), F32),
            vmem((rows, width), BF16),
            vmem((rows, width), F32),
            vmem((rows, LANES), F32),
            vmem((rows, width), F32),
            vmem((rows, width), BF16),
            vmem((width, rows), BF16),
            vmem((width, rows), BF16),
            vmem((rows, width), F32),
            vmem((rows, hidden), F32),
            vmem((4, width, 2 * hidden + cols), BF16),
            vmem((4, 1, hidden), F32),
            vmem((rows, LANES), F32),
            pltpu.SemaphoreType.DMA((loads,)),
            pltpu.SemaphoreType.DMA((4, blocks)),
            pltpu.SemaphoreType.DMA((4, blocks)),
            pltpu.SemaphoreType.DMA((4, blocks)),
        ],
        compiler_params=params(),
        cost_estimate=cost(1000, 1000),
        name="middle",
    )(*weights, *att, tokens, out_grad, positions, lengths, vectors)


def body(
    tokens,
    seq_lengths,
    positions,
    w_query,
    w_key,
    w_value,
    w_out,
    w_up,
    w_down,
    b_query,
    b_value,
    b_out,
    b_up,
    b_down,
    gain_attn,
    shift_attn,
    gain_ffn,
    shift_ffn,
    out_grad,
):
    group = lax.axis_index("dp")
    member = lax.axis_index("tensor")
    dp_count = lax.axis_size("dp")
    bits = dp_count.bit_length() - 1
    rows, width = tokens.shape
    own_cols = w_query.shape[1]
    heads = own_cols // HEAD_DIM
    share = w_query.shape[0]
    hidden = w_up.shape[1]
    placed = share % 16 == 0 and bits >= 2
    blocks = dp_count if placed else 1
    def core(value):
        return swap(value, "tensor", 1)

    def cross(value):
        return swap(value, "tensor", 2)

    def grow(value, masks, bit, *hold):
        got = after(swap(value, "dp", 1 << bit), *hold)
        both = jnp.stack([value, got], axis=1).reshape((-1,) + value.shape[1:])
        return both, [m ^ b for m in masks for b in (0, 1 << bit)]

    across = cross(tokens)
    parts = [tokens, core(tokens), across, core(across)]
    own_qkv = jnp.concatenate([w_query, w_key, w_value], axis=1)[None]
    own_b_up = lax.dynamic_slice_in_dim(b_up, group * share, share, 0)[:, None]
    spare = -(hidden + own_cols) % LANES
    one = jnp.concatenate([w_up, w_out.T, jnp.broadcast_to(own_b_up, (share, spare))], axis=1)[None]
    two = w_down.T[None]
    biases = [b_query.reshape(1, -1), b_value.reshape(1, -1)]
    vectors = [b_out, b_down, gain_attn, shift_attn, gain_ffn, shift_ffn]
    vectors = jnp.stack([vec.astype(F32) for vec in vectors] + [jnp.zeros((width,), F32)] * 2)

    kept = []
    if placed:
        top = bits - 1
        masks = [0]
        w_part, masks = grow(own_qkv, masks, top, one, two, biases, vectors)
        one = after(one, w_part)
        for bit in range(top - 1, 0, -1):
            w_part, masks = grow(w_part, masks, bit)
        one, one_masks = grow(one, [0], top, w_part)
        two = after(two, across)
        two = jnp.stack([two, cross(two)], axis=1)
        w_qkv = [w_part, swap(w_part, "dp", 1)]
        w_masks = [masks, [m ^ 1 for m in masks]]
        positions = after(positions, two)
        q, k, v = project(parts, w_qkv, w_masks, *biases, positions, seq_lengths, heads, placed)

        for bit in range(top - 1, 0, -1):
            one, one_masks = grow(one, one_masks, bit, q)
        even = (one, one_masks)
        odd = (swap(one, "dp", 1), [m ^ 1 for m in one_masks])
        even_far = (cross(one), one_masks)
        q = after(q, one)
        q_kept, out, packed = attention_forward(0, q, k, v, [])
        kept.append((q_kept, out))
        two, two_masks = grow(two, [0], top, q_kept)
        twos = [(two, two_masks)]
        packed = list(after(packed, two))
        for h in range(1, heads):
            q_kept, out, packed = attention_forward(h, q, k, v, packed)
            kept.append((q_kept, out))
            if h == 1:
                for bit in range(top - 1, 0, -1):
                    twos += [(swap(w, "dp", 1 << bit), [m ^ (1 << bit) for m in ms]) for w, ms in twos]
                odd = (after(odd[0], q_kept), odd[1])
                odd_far = (cross(odd[0]), odd[1])
                first = len(twos)
                twos.append((swap(after(two, q_kept), "dp", 1), [m ^ 1 for m in two_masks]))
                packed = list(after(packed, odd[0]))
        later = [(after(w, q_kept), ms) for w, ms in twos[1:first]]
        twos = [twos[0]] + later + twos[first:] + [(swap(w, "dp", 1), [m ^ 1 for m in ms]) for w, ms in later]
        ones = [even, odd, even_far, odd_far]
    else:
        w_qkv = [gather_bits(own_qkv[0], "dp", range(bits), 0).reshape(1, width, -1)]
        w_masks = [[0]]
        one = gather_bits(one[0], "dp", range(bits), 0).reshape(1, width, -1)
        two = gather_bits(two[0], "dp", range(bits), 0).reshape(1, width, -1)
        q, k, v = project(parts, w_qkv, w_masks, *biases, positions, seq_lengths, heads, placed)
        packed = []
        for h in range(heads):
            q_kept, out, packed = attention_forward(h, q, k, v, packed)
            kept.append((q_kept, out))
        ones = [(one, [0]), (cross(one), [0])]
        twos = [(jnp.stack([two, cross(two)], axis=1), [0])]
    att_far = cross(packed[2])
    att = [packed[0], core(jnp.stack([packed[1], att_far[1]])), att_far]
    weights, plan = [], []
    for near in range(2):
        for a, (array, masks) in enumerate(ones):
            weights.append(core(after(array, q_kept)) if near else array)
            far = a // (len(ones) // 2)
            plan.append([((z,), False, near + 2 * far, mask) for z, mask in enumerate(masks)])
        for array, masks in twos:
            weights.append(core(after(array, q_kept)) if near else array)
            plan.append(
                [
                    ((z, far), True, near + 2 * far, mask)
                    for z, mask in enumerate(masks)
                    for far in range(2)
                ]
            )
    layer_out, d_one, sums, g_b_up, sent, own_sum, *back = middle(
        blocks, weights, plan, att, tokens, out_grad, positions, seq_lengths, vectors, hidden
    )
    grads = [back[0]] + [swap(back[j], "tensor", j) for j in (1, 2, 3)]

    def add(*terms):
        total = terms[0].astype(F32)
        for term in terms[1:]:
            total = total + term.astype(F32)
        return total

    def axes_of(array, lead):
        return array.reshape(array.shape[:lead] + (2,) * bits + array.shape[lead + 1 :])

    class Sum:
        def __init__(self, terms, names):
            self.terms, self.names = terms, list(names)

        def split(self, name):
            at = self.names.index(name)
            pick = functools.partial(lax.index_in_dim, axis=at, keepdims=False)
            away = add(*[pick(t, 1) for t in self.terms]).astype(BF16)
            self.terms = [pick(t, 0) for t in self.terms]
            self.names.remove(name)
            return away

        def join(self, got):
            self.terms.append(got)

    def send(away, name):
        return cross(away) if name == "x" else swap(away, "dp", 1 << name)

    names = list(range(bits))[::-1]
    late = list(range(1, bits))
    got_sum = core(sent)
    if placed:
        terms = [axes_of(own_sum, 1), axes_of(got_sum, 1)]
        down = Sum([t[..., :hidden] for t in terms], ["x"] + names)
        up = Sum([t[..., hidden:] for t in terms], ["x"] + names)
        pair = down.split("x"), up.split(0)
        grads, pair = after((grads, pair), d_one)

    small = jnp.concatenate([sums[:9], jnp.zeros((1, width), F32)])
    ups = g_b_up[:, 0]
    got_small = core(jnp.concatenate([small, ups[1:2], ups[3:4]]))

    g_bias, before = [], []
    for h in range(heads):
        q_kept = kept[h][0]
        if placed and h == heads - 1:
            down.join(after(send(pair[0], "x"), *before[:1]))
            up.join(after(send(pair[1], 0), *before[:1]))
            pair = down.split(0), up.split("x")
            q_kept, pair = after((q_kept, pair), *before[:1])
        g_all, b_head, g_w = attention_backward(
            h, q_kept, k, v, kept[h][1], grads, parts, blocks, before
        )
        before = [g_all, g_w]
        g_bias.append(b_head)
        if h == 0:
            got = after(got_small, g_all)
            small, ups = small + got[:10], ups[0::2] + got[10:]
            got_small = cross(jnp.concatenate([small, ups[1:2]]))
    got_small = after(got_small, g_all)
    if placed:
        down.join(after(send(pair[0], 0), g_all))
        up.join(after(send(pair[1], "x"), g_all))

        def both(name):
            return jnp.concatenate([down.split(name), up.split(name)], axis=-1)

        def join_both(got):
            down.join(got[..., :hidden])
            up.join(got[..., hidden:])

        move = both(late[0])
        g_w, got_small, g_bias, g_all = after((g_w, got_small, g_bias, g_all), move)
        qkv = Sum([axes_of(g_w, 1)], ["h"] + names)
        qkv_move = qkv.split(0)
        g_all, qkv_move = after((g_all, qkv_move), move)
    small = jnp.concatenate([small + got_small[:10], ups[:1] + got_small[10:]])
    spare = width - heads * 3 * HEAD_DIM
    bias_row = jnp.pad(jnp.concatenate(g_bias, axis=1), ((0, 0), (0, spare)))
    small = jnp.concatenate([small, bias_row])
    g_all, small = after((g_all, small), d_one)
    first = input_part(g_all, w_qkv, w_masks, (3, 2), placed)
    crossed = add(first[1], core(first[0])).astype(BF16)
    g_all, crossed = after((g_all, crossed), *first)
    second = input_part(g_all, w_qkv, w_masks, (1, 0), placed)
    crossed = cross(crossed)
    if placed:
        qkv.join(after(send(qkv_move, 0), *second))
        qkv_move = qkv.split(late[0])
        join_both(after(send(move, late[0]), qkv_move))
        for at, name in enumerate(late[1:]):
            move = both(name)
            qkv.join(after(send(qkv_move, late[at]), move))
            qkv_move = qkv.split(name)
            join_both(after(send(move, name), qkv_move))
        qkv.join(send(qkv_move, late[-1]))
    small = small + after(swap(small, "dp", 1), *second)
    for bit in range(1, bits):
        small = small + swap(small, "dp", 1 << bit)
    near = core(second[0])
    input_grad = add(d_one, second[1], near, crossed).astype(BF16)
    if placed:
        g_down = add(*down.terms)
        g_up = add(*up.terms)
        g_qkv = add(*qkv.terms).reshape(heads, share, 3, HEAD_DIM)
    else:
        two_s = (2,) * bits
        total = add(own_sum, got_sum)
        total = total[0] + cross(total[1].astype(BF16)).astype(F32)
        total = scatter_bits(total.reshape(two_s + (share, -1)), "dp", range(bits), 0)
        g_down, g_up = total[:, :hidden], total[:, hidden:]
        g_qkv = g_w.reshape((heads,) + two_s + (share, -1))
        g_qkv = scatter_bits(g_qkv, "dp", range(bits), 1).reshape(heads, share, 3, HEAD_DIM)
    g_q, g_k, g_v = (g_qkv[:, :, i].transpose(1, 0, 2).reshape(share, own_cols) for i in range(3))
    bias_rows = small[11, : heads * 3 * HEAD_DIM].reshape(heads, 3, HEAD_DIM)
    count = jnp.sum(seq_lengths).astype(F32) * width
    rms = jnp.sqrt(jnp.sum(small[6:9], axis=-1) / count)
    return (
        layer_out,
        input_grad,
        g_q,
        g_k,
        g_v,
        g_up[:, hidden:].T,
        g_up[:, :hidden],
        g_down.T,
        bias_rows[:, 0].reshape(own_cols),
        bias_rows[:, 2].reshape(own_cols),
        small[0],
        small[10],
        small[1],
        small[2],
        small[3],
        small[4],
        small[5],
        rms,
    )


def solution(mesh):
    in_specs = (
        P(("dp", "tensor"), None),
        P(),
        P("dp", None),
        P("dp", "tensor"),
        P("dp", "tensor"),
        P("dp", "tensor"),
        P("tensor", "dp"),
        P("dp", "tensor"),
        P("tensor", "dp"),
        P("tensor"),
        P("tensor"),
        P(),
        P("tensor"),
        P(),
        P(),
        P(),
        P(),
        P(),
        P(("dp", "tensor"), None),
    )
    out_specs = (
        P(("dp", "tensor"), None),
        P(("dp", "tensor"), None),
        P("dp", "tensor"),
        P("dp", "tensor"),
        P("dp", "tensor"),
        P("tensor", "dp"),
        P("dp", "tensor"),
        P("tensor", "dp"),
        P("tensor"),
        P("tensor"),
        P(),
        P("tensor"),
        P(),
        P(),
        P(),
        P(),
        P(),
        P(),
    )
    return jax.shard_map(body, mesh=mesh, in_specs=in_specs, out_specs=out_specs, check_vma=False)
```

```python
import functools
import itertools

import jax
import jax.numpy as jnp
from jax import lax
from jax.experimental import pallas as pl
from jax.experimental.pallas import tpu as pltpu
from jax.sharding import PartitionSpec as P

HEAD_DIM = 64
LANES = 128
EPSILON = 1e-12
MASKED = -1e30
BF16 = jnp.bfloat16
F32 = jnp.float32
NT = (((1,), (1,)), ((), ()))
TN = (((0,), (0,)), ((), ()))
VMEM_LIMIT = 64 << 20
EXTRA = 16


def dot(left, right):
    return jnp.dot(left, right, preferred_element_type=F32)


def dot_nt(left, right):
    return lax.dot_general(left, right, NT, preferred_element_type=F32)


def dot_tn(left, right):
    return lax.dot_general(left, right, TN, preferred_element_type=F32)


def place_of(mask, height, placed):
    start = (lax.axis_index("dp") ^ mask) * height if placed else 0
    return pl.ds(pl.multiple_of(start, height), height)


def valid_row(positions_ref, lengths_ref, j, rows):
    start = (lax.axis_index("tensor") ^ j) * rows
    own = positions_ref[:, pl.ds(pl.multiple_of(start, rows), rows)]
    return own < lengths_ref[lax.axis_index("dp")]


def in_three(column):
    first = column.astype(BF16)
    rest = column - first.astype(F32)
    second = rest.astype(BF16)
    third = (rest - second.astype(F32)).astype(BF16)
    return first, second, third


def swap(value, axis, bits):
    size = lax.axis_size(axis)
    return lax.ppermute(value, axis, [(i, i ^ bits) for i in range(size)])


def bit_of(axis, bit):
    return (lax.axis_index(axis) >> bit) & 1


def gather_bits(block, axis, order, at):
    done = []
    for bit in order:
        place = at + sum(other > bit for other in done)
        got = swap(block, axis, 1 << bit)
        upper = bit_of(axis, bit) == 1
        low = jnp.where(upper, got, block)
        high = jnp.where(upper, block, got)
        block = jnp.stack([low, high], axis=place)
        done.append(bit)
    return block


def scatter_bits(partial, axis, order, at):
    left = sorted(order, reverse=True)
    for bit in order:
        place = at + left.index(bit)
        mine = bit_of(axis, bit)
        away = lax.dynamic_index_in_dim(partial, 1 - mine, place, keepdims=False)
        keep = lax.dynamic_index_in_dim(partial, mine, place, keepdims=False)
        got = swap(away.astype(BF16), axis, 1 << bit)
        partial = keep.astype(F32) + got.astype(F32)
        left.remove(bit)
    return partial


def after(value, *others):
    return lax.optimization_barrier((value,) + others)[0]


def params():
    return pltpu.CompilerParams(vmem_limit_bytes=VMEM_LIMIT - (1 << 20))


def cost(flops, moved, exps=0):
    return pl.CostEstimate(flops=flops, bytes_accessed=moved, transcendentals=exps)


SMEM_SPEC = pl.BlockSpec(memory_space=pltpu.SMEM)
VMEM_SPEC = pl.BlockSpec(memory_space=pltpu.VMEM)
ANY_SPEC = pl.BlockSpec(memory_space=pl.ANY)
HBM_SPEC = pl.BlockSpec(memory_space=pltpu.HBM)


def project_kernel(*refs, masks, heads, placed):
    x_refs, w_refs = refs[:4], refs[4 : 4 + len(masks)]
    bq_ref, bv_ref, positions_ref, lengths_ref, q_out, k_out, v_out, w_s = refs[4 + len(masks) :]
    rows = x_refs[0].shape[0]
    for ref, entries in zip(w_refs, masks, strict=True):
        for z, mask in enumerate(entries):
            w_s[place_of(mask, ref.shape[1], placed), :] = ref[z]
    lane = lax.broadcasted_iota(jnp.int32, (1, LANES), 1)
    head_lane = lane < HEAD_DIM
    one_q = jnp.where(lane == HEAD_DIM, 1.0, 0.0)
    one_k = jnp.where((lane > HEAD_DIM) & (lane <= HEAD_DIM + 3), 1.0, 0.0)
    one_v = jnp.where((lane >= HEAD_DIM) & (lane < HEAD_DIM + 3), 1.0, 0.0)
    b_query = bq_ref[...].astype(F32)
    bias = jnp.concatenate([b_query, jnp.zeros_like(b_query), bv_ref[...].astype(F32)], axis=1)
    for j in range(4):
        part = pl.ds(j * rows, rows)
        whole = dot(x_refs[j][...], w_s[...]) + bias
        masked = jnp.where(valid_row(positions_ref, lengths_ref, j, rows), 0.0, MASKED)
        masked = jnp.broadcast_to(masked, (LANES, rows)).T

        def columns(group):
            start = group // 2 * LANES
            both = whole[:, start : start + LANES]
            if both.shape[1] < LANES:
                both = jnp.concatenate([both, both], axis=1)
            return pltpu.roll(both, HEAD_DIM, 1) if group % 2 else both

        for h in range(heads):
            query = columns(h).astype(BF16).astype(F32) * (HEAD_DIM**-0.5)
            q_out[h, part, :] = jnp.where(head_lane, query, one_q).astype(BF16)
            key = jnp.where(head_lane, columns(heads + h), one_k)
            k_out[h, part, :] = jnp.where(lane == HEAD_DIM, masked, key).astype(BF16)
            value = jnp.where(head_lane, columns(2 * heads + h), one_v)
            v_out[h, part, :] = value.astype(BF16)


def project(parts, pieces, masks, b_query, b_value, positions, lengths, heads, placed):
    rows, width = parts[0].shape
    seq = 4 * rows
    return pl.pallas_call(
        functools.partial(project_kernel, masks=masks, heads=heads, placed=placed),
        in_specs=[VMEM_SPEC] * (7 + len(pieces)) + [SMEM_SPEC],
        out_specs=[VMEM_SPEC] * 3,
        out_shape=[jax.ShapeDtypeStruct((heads, seq, LANES), BF16)] * 3,
        scratch_shapes=[pltpu.VMEM((width, pieces[0].shape[2]), BF16)],
        compiler_params=params(),
        cost_estimate=cost(1000, 1000),
        name="project",
    )(*parts, *pieces, b_query, b_value, positions, lengths)


def forward_kernel(q_ref, k_ref, v_ref, *refs, unroll):
    q_out, o_out, own, near, far, packed = refs[-6:]
    seq = q_ref.shape[1]
    block = seq // 8
    lane = lax.broadcasted_iota(jnp.int32, (1, LANES), 1)
    head_lane = lane < HEAD_DIM

    def place(i):
        return pl.ds(pl.multiple_of(i * block, block), block)

    def scores_of(i):
        query = q_ref[0, place(i), :]
        scores = dot_nt(query, k_ref[0])
        return query, scores, jnp.max(scores, axis=-1, keepdims=True)

    def attend(i, query, scores, top):
        expon = jnp.exp(scores - top).astype(BF16)
        total = dot(expon, v_ref[0])
        row_sum = total[:, HEAD_DIM : HEAD_DIM + 1]
        out = total * (1.0 / row_sum)
        o_out[place(i), :] = out
        one, two, three = in_three(-(top + jnp.log(row_sum)))
        q_out[place(i), :] = jnp.where(
            lane == HEAD_DIM + 1,
            one,
            jnp.where(lane == HEAD_DIM + 2, two, jnp.where(lane == HEAD_DIM + 3, three, query)),
        )
        return out

    @pl.loop(0, 8 // unroll)
    def _(step):
        held = scores_of(step * unroll)
        even = None
        for u in range(unroll):
            i = step * unroll + u
            following = scores_of(i + 1) if u < unroll - 1 else None
            out = attend(i, *held)
            if u % 2 == 0:
                even = out
            else:
                pair = jnp.where(head_lane, even, pltpu.roll(out, HEAD_DIM, 1))
                packed[step * (unroll // 2) + u // 2] = pair.astype(BF16)
            held = following

    own[0] = packed[0]
    near[0] = packed[1]
    far[0, 0] = packed[2]
    far[1, 0] = packed[3]


def attention_forward(head, q, k, v, packed):
    heads, seq, _ = q.shape
    block = seq // 8
    one = pl.BlockSpec((1, seq, LANES), lambda i: (head, 0, 0))
    flat = pl.BlockSpec((seq, LANES), lambda i: (0, 0))
    piece = pl.BlockSpec((1, block, LANES), lambda i: (head, 0, 0))
    pieces = pl.BlockSpec((2, 1, block, LANES), lambda i: (0, head, 0, 0))
    shape = jax.ShapeDtypeStruct
    q_kept, out, *packed = pl.pallas_call(
        functools.partial(forward_kernel, unroll=4),
        grid=(1,),
        in_specs=[one] * 3 + [ANY_SPEC] * len(packed),
        out_specs=[flat, flat, piece, piece, pieces],
        out_shape=[shape((seq, LANES), BF16), shape((seq, LANES), F32)]
        + [shape((heads, block, LANES), BF16)] * 2
        + [shape((2, heads, block, LANES), BF16)],
        scratch_shapes=[pltpu.VMEM((4, block, LANES), BF16)],
        input_output_aliases={3 + i: 2 + i for i in range(len(packed))},
        compiler_params=params(),
        cost_estimate=cost(1000, 1000),
        name="attention_forward",
    )(q, k, v, *packed)
    return q_kept, out, packed


def backward_kernel(q_ref, k_ref, v_ref, o_ref, *refs, placed):
    d_refs, x_refs = refs[:4], refs[4:8]
    g_ref, gw_ref, dk_s, dv_s, gw_s, d_s = refs[-6:]
    seq = q_ref.shape[0]
    block = seq // 8
    rows = seq // 4
    lane = lax.broadcasted_iota(jnp.int32, (1, LANES), 1)
    head_lane = lane < HEAD_DIM
    scale = HEAD_DIM**-0.5
    for j in range(4):
        d_s[j] = d_refs[j][0]
    dk_s[...] = jnp.zeros_like(dk_s)
    dv_s[...] = jnp.zeros_like(dv_s)

    @pl.loop(0, 4)
    def _(j):
        for half in range(2):
            place = pl.ds(pl.multiple_of((2 * j + half) * block, block), block)
            query = q_ref[place, :]
            grad = d_s[j].astype(F32)
            if half == 1:
                grad = pltpu.roll(grad, HEAD_DIM, 1)
            grad = jnp.where(head_lane, grad, 0.0)
            delta = jnp.sum(grad * o_ref[place, :], axis=-1, keepdims=True)
            one, two, three = in_three(-delta)
            grad = grad.astype(BF16)
            grad_and = jnp.where(
                lane == HEAD_DIM,
                one,
                jnp.where(lane == HEAD_DIM + 1, two, jnp.where(lane == HEAD_DIM + 2, three, grad)),
            )
            probs = jnp.exp(dot_nt(k_ref[0], query))
            lifted = dot_nt(v_ref[0], grad_and)
            grad_scores = (probs * lifted).astype(BF16)
            dv_s[...] += dot(probs.astype(BF16), grad)
            dk_s[...] += dot(grad_scores, query)
            grad_query = dot_tn(grad_scores, k_ref[0]) * scale
            g_ref[0, place, :LANES] = jnp.where(head_lane, grad_query, 0.0).astype(BF16)

    both = jnp.where(head_lane, g_ref[0, :, :LANES].astype(F32), pltpu.roll(dk_s[...], HEAD_DIM, 1))
    g_ref[0, :, :LANES] = both.astype(BF16)
    g_ref[0, :, LANES:] = dv_s[:, :HEAD_DIM].astype(BF16)
    grads = g_ref[0]
    bias = jnp.sum(grads.astype(F32), axis=0, keepdims=True)
    share = gw_ref.shape[2]
    line = lax.broadcasted_iota(jnp.int32, (share, 1), 0)
    side = jnp.where(line < 8, bias[:, :HEAD_DIM], 0.0)
    side = jnp.where((line >= 8) & (line < 16), bias[:, LANES:], side).astype(BF16)
    total = dot_tn(grads[:rows], x_refs[0][...])
    for j in range(1, 4):
        total += dot_tn(grads[j * rows : (j + 1) * rows], x_refs[j][...])
    gw_s[...] = total.T.astype(BF16)
    for i in range(gw_ref.shape[1]):
        gw_ref[0, i, :, : 3 * HEAD_DIM] = gw_s[place_of(i, share, placed), :]
        gw_ref[0, i, :, 3 * HEAD_DIM :] = side


def attention_backward(head, q, k, v, out, grads, parts, blocks, before):
    heads, seq, _ = k.shape
    rows, width = parts[0].shape
    one = pl.BlockSpec((1, seq, LANES), lambda i: (head, 0, 0))
    flat = pl.BlockSpec((seq, LANES), lambda i: (0, 0))
    piece = pl.BlockSpec((1, seq // 8, LANES), lambda i: (head, 0, 0))
    whole = pl.BlockSpec((rows, width), lambda i: (0, 0))
    three = 3 * HEAD_DIM
    share = width // blocks
    shape = jax.ShapeDtypeStruct
    alias = {12: 0, 13: 1} if before else {}
    return pl.pallas_call(
        functools.partial(backward_kernel, placed=blocks > 1),
        grid=(1,),
        in_specs=[flat, one, one, flat] + [piece] * 4 + [whole] * 4 + [ANY_SPEC] * len(before),
        out_specs=[
            pl.BlockSpec((1, seq, three), lambda i: (head, 0, 0)),
            pl.BlockSpec((1, blocks, share, 4 * HEAD_DIM), lambda i: (head, 0, 0, 0)),
        ],
        out_shape=[
            shape((heads, seq, three), BF16),
            shape((heads, blocks, share, 4 * HEAD_DIM), BF16),
        ],
        scratch_shapes=[
            pltpu.VMEM((seq, LANES), F32),
            pltpu.VMEM((seq, LANES), F32),
            pltpu.VMEM((width, three), BF16),
            pltpu.VMEM((4, seq // 8, LANES), BF16),
        ],
        input_output_aliases=alias,
        compiler_params=params(),
        cost_estimate=cost(1000, 1000),
        name="attention_backward",
    )(q, k, v, out, *grads, *parts, *before)


def input_kernel(g_ref, *refs, masks, which, placed):
    w_refs = refs[: len(masks)]
    outs, w_s = refs[len(masks) : -1], refs[-1]
    heads, seq, three = g_ref.shape
    for ref, entries in zip(w_refs, masks, strict=True):
        for z, mask in enumerate(entries):
            place = place_of(mask, ref.shape[1], placed)
            for h in range(heads):
                for kind in range(3):
                    start = (kind * heads + h) * HEAD_DIM
                    stop = (h * 3 + kind) * HEAD_DIM
                    w_s[place, stop : stop + HEAD_DIM] = ref[z, :, start : start + HEAD_DIM]
    for out, (start, count) in zip(outs, which, strict=True):
        part = pl.ds(start, count)
        total = dot_nt(g_ref[0, part, :], w_s[:, :three])
        for h in range(1, heads):
            total += dot_nt(g_ref[h, part, :], w_s[:, h * three : (h + 1) * three])
        out[...] = total.astype(out.dtype)


def input_part(g_all, pieces, masks, which, placed):
    heads, seq, three = g_all.shape
    width = pieces[0].shape[0] * pieces[0].shape[1] * len(pieces)
    return pl.pallas_call(
        functools.partial(input_kernel, masks=masks, which=which, placed=placed),
        in_specs=[VMEM_SPEC] * (1 + len(pieces)),
        out_specs=[VMEM_SPEC] * len(which),
        out_shape=[jax.ShapeDtypeStruct((count, width), BF16) for _, count in which],
        scratch_shapes=[pltpu.VMEM((width, heads * three), BF16)],
        compiler_params=params(),
        cost_estimate=cost(1000, 1000),
        name="input_part",
    )(g_all, *pieces)


def middle_kernel(*refs, plan, blocks):
    w_refs = refs[: len(plan)]
    refs = refs[len(plan) :]
    own_ref, near_ref, far_ref = refs[:3]
    x_ref, og_ref, positions_ref, lengths_ref, vec_ref = refs[3:8]
    lo_ref, done_ref, sent_d, kept_d, sent_u, kept_u = refs[8:14]
    ga = refs[14:18]
    w1_s, w2_s, att_s, wo_s, hid_s, slope_s, nrm_s, nb_s, n1_s, rs_s, ffn_s = refs[18:29]
    gf_s, gft_s, nbt_s, acc_s, pre_s, g_s, bup_s, mask_s, sums_ref, low_s, in_sem, down_sem, up_sem, out_sem, low_sem = refs[29:]
    rows, width = x_ref.shape
    hidden = w2_s.shape[2]
    pieces = 4
    cols = width // pieces
    placed = blocks > 1
    chunk = 128
    share = width // blocks
    half = rows // 2
    b_out, b_down, gain_a, shift_a, gain_f, shift_f = (vec_ref[i : i + 1, :] for i in range(6))

    count = cols // HEAD_DIM
    att = [[own_ref[h] for h in range(count)]]
    for ref, i in ((near_ref, 0), (far_ref, 0), (near_ref, 1)):
        att.append([ref[i, h] for h in range(count)])

    loads = []
    for ref, entries in zip(w_refs, plan, strict=True):
        for index, second, j, row in entries:
            source = ref.at[index]
            target = (w2_s if second else w1_s).at[j].at[place_of(row, source.shape[0], placed)]
            copy = pltpu.make_async_copy(source, target, in_sem.at[len(loads)])
            loads.append((second, copy))
            copy.start()

    def row_loop(work):
        @pl.loop(0, rows // chunk)
        def _(i):
            work(pl.ds(pl.multiple_of(i * chunk, chunk), chunk))

    def add_sum(index, value):
        sums_ref[index : index + 1, :] += jnp.sum(value, axis=0, keepdims=True)

    def mean(value):
        return jnp.mean(value, axis=-1, keepdims=True)

    def normal(value):
        centred = value - mean(value)
        inverse = lax.rsqrt(mean(centred * centred) + EPSILON)
        return centred * inverse, inverse

    def norm_back(grad, unit, inverse, gain):
        scaled = grad * gain
        return (scaled - mean(scaled) - unit * mean(scaled * unit)) * inverse

    sums_ref[...] = jnp.zeros_like(sums_ref)
    own_valid = jnp.where(valid_row(positions_ref, lengths_ref, 0, rows), 1.0, 0.0)
    mask_s[...] = jnp.broadcast_to(own_valid, (LANES, rows)).T
    for j in range(pieces):
        for h in range(cols // HEAD_DIM):
            at = j * cols + h * HEAD_DIM
            att_s[:half, at : at + HEAD_DIM] = att[j][h][:, :HEAD_DIM]
            att_s[half:, at : at + HEAD_DIM] = att[j][h][:, HEAD_DIM:]
    for second, copy in loads:
        if not second:
            copy.wait()
    for j in range(pieces):
        wo_s[:, j * cols : (j + 1) * cols] = w1_s[j, :, hidden : hidden + cols]
        last = w1_s[j, :, hidden + cols - HEAD_DIM :].astype(F32)
        bup_s[j] = last.T[HEAD_DIM : HEAD_DIM + 1, :]
    ffn_s[...] = dot_nt(att_s[...], wo_s[...])

    def first_norm(r):
        value = x_ref[r, :].astype(F32)
        attn = ffn_s[r, :] + b_out
        valid = mask_s[r, :1] > 0.0
        add_sum(6, jnp.where(valid, value * value, 0.0))
        add_sum(7, jnp.where(valid, attn * attn, 0.0))
        unit, inverse = normal(value + attn)
        normed = unit * gain_a + shift_a
        n1_s[r, :] = unit
        rs_s[r, :] = jnp.broadcast_to(inverse, (chunk, LANES))
        nrm_s[r, :] = normed
        nb_s[r, :] = normed.astype(BF16)

    row_loop(first_norm)
    ffn_s[...] = jnp.zeros_like(ffn_s)
    for second, copy in loads:
        if second:
            copy.wait()

    @pl.loop(0, pieces)
    def _(j):
        pre_s[...] = dot(nb_s[...], w1_s[j, :, :hidden]) + bup_s[j]

        def gelu(r):
            pre = pre_s[r, :]
            cdf = 0.5 * (1.0 + lax.erf(pre * (0.5**0.5)))
            pdf = jnp.exp(pre * pre * -0.5) * (2.0 * jnp.pi) ** -0.5
            hid_s[j, r, :] = (pre * cdf).astype(BF16)
            slope_s[j, r, :] = cdf + pre * pdf

        row_loop(gelu)
        ffn_s[...] += dot_nt(hid_s[j], w2_s[j])

    def second_norm(r):
        ffn = ffn_s[r, :] + b_down
        valid = mask_s[r, :1] > 0.0
        add_sum(8, jnp.where(valid, ffn * ffn, 0.0))
        unit, inverse = normal(nrm_s[r, :] + ffn)
        lo_ref[r, :] = (unit * gain_f + shift_f).astype(BF16)
        grad = og_ref[r, :].astype(F32)
        add_sum(4, grad * unit)
        add_sum(5, grad)
        d_two = norm_back(grad, unit, inverse, gain_f)
        low = d_two.astype(BF16)
        add_sum(1, low.astype(F32))
        acc_s[r, :] = d_two
        gf_s[r, :] = low

    row_loop(second_norm)
    gft_s[...] = gf_s[...].T
    nbt_s[...] = nb_s[...].T

    places = [place_of(i, share, placed) for i in range(blocks)]

    def copies(j, lanes, target, place, sem, to):
        return [
            pltpu.make_async_copy(
                g_s.at[j].at[places[i], lanes], target.at[place, i, pl.ds(0, share), to], sem.at[j, i]
            )
            for i in range(blocks)
        ]

    lanes_d, lanes_u, lanes_o = (
        pl.ds(0, hidden),
        pl.ds(hidden, hidden),
        pl.ds(2 * hidden, cols),
    )
    to_d, to_u, to_o = pl.ds(0, hidden), pl.ds(0, hidden), pl.ds(hidden, cols)
    for away, target_d, target_u in ((1, sent_d, sent_u), (0, kept_d, kept_u)):

        @pl.loop(0, pieces // 2)
        def _(place):
            j = 2 * place + away
            pre_s[...] = dot(gf_s[...], w2_s[j]) * slope_s[j]
            low = pre_s[...].astype(BF16)
            sums_ref[pl.ds(10 + j, 1), :] = jnp.sum(low.astype(F32), axis=0, keepdims=True)
            g_s[j, :, lanes_d] = dot(gft_s[...], hid_s[j]).astype(BF16)
            for copy in copies(j, lanes_d, target_d, place, down_sem, to_d):
                copy.start()
            g_s[j, :, lanes_u] = dot(nbt_s[...], low).astype(BF16)
            for copy in copies(j, lanes_u, target_u, place, up_sem, to_u):
                copy.start()
            acc_s[...] += dot_nt(low, w1_s[j, :, :hidden])

    def first_back(r):
        grad = acc_s[r, :]
        unit = n1_s[r, :]
        add_sum(2, grad * unit)
        add_sum(3, grad)
        d_one = norm_back(grad, unit, rs_s[r, :1], gain_a)
        low = d_one.astype(BF16)
        add_sum(0, low.astype(F32))
        done_ref[r, :] = d_one
        gf_s[r, :] = low

    row_loop(first_back)
    low = gf_s[...]
    gout = dot_tn(low, att_s[...]).astype(BF16)
    for j in range(pieces):
        g_s[j, :, 2 * hidden : 2 * hidden + cols] = gout[:, j * cols : (j + 1) * cols]
        for copy in copies(j, lanes_o, sent_u if j % 2 else kept_u, j // 2, out_sem, to_o):
            copy.start()
    small = []
    for j in range(pieces):
        low_s[j] = jnp.concatenate([sums_ref[:9], sums_ref[10 + j : 11 + j], sums_ref[9:15]]).astype(BF16)
        target = sent_d if j % 2 else kept_d
        for i in range(blocks):
            under = target.at[j // 2, i, pl.ds(share, EXTRA), :]
            small.append(pltpu.make_async_copy(low_s.at[j], under, low_sem.at[j, i]))
            small[-1].start()
    back = dot(low, wo_s[...]).astype(BF16)
    for j in range(pieces):
        for h in range(cols // HEAD_DIM):
            at = j * cols + h * HEAD_DIM
            ga[j][h, :, :HEAD_DIM] = back[:half, at : at + HEAD_DIM]
            ga[j][h, :, HEAD_DIM:] = back[half:, at : at + HEAD_DIM]
    for j in range(pieces):
        target_d, target_u = (sent_d, sent_u) if j % 2 else (kept_d, kept_u)
        for copy in copies(j, lanes_d, target_d, j // 2, down_sem, to_d):
            copy.wait()
        for copy in copies(j, lanes_u, target_u, j // 2, up_sem, to_u):
            copy.wait()
        for copy in copies(j, lanes_o, target_u, j // 2, out_sem, to_o):
            copy.wait()
    for copy in small:
        copy.wait()


def middle(blocks, weights, plan, att, tokens, out_grad, positions, lengths, vectors, hidden):
    rows, width = tokens.shape
    cols = width // 4
    share = width // blocks
    shape = jax.ShapeDtypeStruct
    vmem = pltpu.VMEM
    loads = sum(len(entries) for entries in plan)
    return pl.pallas_call(
        functools.partial(middle_kernel, plan=plan, blocks=blocks),
        in_specs=[ANY_SPEC] * len(weights) + [VMEM_SPEC] * 6 + [SMEM_SPEC, VMEM_SPEC],
        out_specs=[VMEM_SPEC] * 2 + [ANY_SPEC] * 4 + [VMEM_SPEC] * 4,
        out_shape=[
            shape((rows, width), BF16),
            shape((rows, width), F32),
        ]
        + [shape((2, blocks, share + EXTRA, hidden), BF16)] * 2
        + [shape((2, blocks, share, hidden + cols), BF16)] * 2
        + [shape(att[0].shape, BF16)] * 4,
        scratch_shapes=[
            vmem((4, width, weights[0].shape[-1]), BF16),
            vmem((4, width, hidden), BF16),
            vmem((rows, width), BF16),
            vmem((width, width), BF16),
            vmem((4, rows, hidden), BF16),
            vmem((4, rows, hidden), F32),
            vmem((rows, width), F32),
            vmem((rows, width), BF16),
            vmem((rows, width), F32),
            vmem((rows, LANES), F32),
            vmem((rows, width), F32),
            vmem((rows, width), BF16),
            vmem((width, rows), BF16),
            vmem((width, rows), BF16),
            vmem((rows, width), F32),
            vmem((rows, hidden), F32),
            vmem((4, width, 2 * hidden + cols), BF16),
            vmem((4, 1, hidden), F32),
            vmem((rows, LANES), F32),
            vmem((16, width), F32),
            vmem((4, EXTRA, width), BF16),
            pltpu.SemaphoreType.DMA((loads,)),
            pltpu.SemaphoreType.DMA((4, blocks)),
            pltpu.SemaphoreType.DMA((4, blocks)),
            pltpu.SemaphoreType.DMA((4, blocks)),
            pltpu.SemaphoreType.DMA((4, blocks)),
        ],
        compiler_params=params(),
        cost_estimate=cost(1000, 1000),
        name="middle",
    )(*weights, *att, tokens, out_grad, positions, lengths, vectors)


def reduce_kernel(*refs, jobs, inputs, outputs, terms, extra, extra_in):
    ins = refs[:inputs]
    more = refs[inputs : inputs + extra_in]
    outs = refs[inputs + extra_in : inputs + extra_in + outputs]
    rest = refs[inputs + extra_in + outputs :]
    extra_out = rest[: len(rest) - terms - 1]
    held, sems = rest[len(extra_out) : -1], rest[-1]
    loads = []
    for _, _, _, parts in jobs:
        for source, index, start, size in parts:
            at = len(loads)
            picked = ins[source].at[index + (slice(None), pl.ds(start, size))]
            loads.append(pltpu.make_async_copy(picked, held[at], sems.at[at]))
            loads[-1].start()
    at = 0
    for out, start, lead, parts in jobs:
        mine = range(at, at + len(parts))
        at += len(parts)
        for i in mine:
            loads[i].wait()
        size = parts[0][3]
        for index in itertools.product(*map(range, lead)):
            total = held[mine[0]][index].astype(F32)
            for i in mine[1:]:
                total += held[i][index].astype(F32)
            target = outs[out]
            target[index + (slice(None), slice(start, start + size))] = total.astype(target.dtype)
    if extra is not None:
        extra(outs, more, extra_out)


class Sum:
    def __init__(self, names, width):
        self.names, self.width, self.terms, self.picks = list(names), width, [], {}

    def join(self, array, start=0, names=None):
        self.terms.append((array, start, list(self.names if names is None else names)))

    def parts(self, picks):
        return [
            (array, tuple(picks.get(name, slice(None)) for name in names), start, self.width)
            for array, start, names in self.terms
        ]

    def away(self, name):
        parts = self.parts({**self.picks, name: 1})
        self.picks[name] = 0
        self.names.remove(name)
        return parts

    def all(self):
        return self.parts(self.picks)


def reduce_call(name, groups, dtype, extra=None, extra_in=(), extra_out=(), keep=True):
    arrays, jobs, shapes, scratch = [], [], [], []
    for out, columns in enumerate(groups):
        start = 0
        for parts in columns:
            coded = []
            for array, index, first, size in parts:
                known = [i for i, other in enumerate(arrays) if other is array]
                if not known:
                    arrays.append(array)
                coded.append((known[0] if known else len(arrays) - 1, index, first, size))
                sizes = [n for n, i in zip(array.shape, index) if isinstance(i, slice)]
                sizes += [array.shape[-2], size]
                scratch.append(pltpu.VMEM(tuple(sizes), array.dtype))
            jobs.append((out, start, tuple(sizes[:-2]), coded))
            start += coded[0][3]
        shapes.append(tuple(sizes[:-1]) + (start,))
    outs = [jax.ShapeDtypeStruct(shape, dtype) for shape in shapes]
    held = [] if keep else [pltpu.VMEM(shape, dtype) for shape in shapes]
    result = pl.pallas_call(
        functools.partial(
            reduce_kernel if keep else reduce_inside,
            jobs=jobs,
            inputs=len(arrays),
            outputs=len(outs),
            terms=len(scratch),
            extra=extra,
            extra_in=len(extra_in),
        ),
        in_specs=[HBM_SPEC] * len(arrays) + [VMEM_SPEC] * len(extra_in),
        out_specs=[VMEM_SPEC] * (len(outs) * keep + len(extra_out)),
        out_shape=outs * keep + list(extra_out),
        scratch_shapes=held + scratch + [pltpu.SemaphoreType.DMA((len(scratch),))],
        compiler_params=params(),
        cost_estimate=cost(1000, 1000),
        name=name,
    )(*arrays, *extra_in)
    return result


def reduce_inside(*refs, inputs, extra_in, outputs, terms, **rest):
    front = inputs + extra_in
    results = refs[front : len(refs) - outputs - terms - 1]
    held = refs[len(refs) - outputs - terms - 1 : len(refs) - terms - 1]
    order = refs[:front] + held + results + refs[len(refs) - terms - 1 :]
    reduce_kernel(*order, inputs=inputs, extra_in=extra_in, outputs=outputs, terms=terms, **rest)


def body(
    tokens,
    seq_lengths,
    positions,
    w_query,
    w_key,
    w_value,
    w_out,
    w_up,
    w_down,
    b_query,
    b_value,
    b_out,
    b_up,
    b_down,
    gain_attn,
    shift_attn,
    gain_ffn,
    shift_ffn,
    out_grad,
):
    group = lax.axis_index("dp")
    member = lax.axis_index("tensor")
    dp_count = lax.axis_size("dp")
    bits = dp_count.bit_length() - 1
    rows, width = tokens.shape
    own_cols = w_query.shape[1]
    heads = own_cols // HEAD_DIM
    share = w_query.shape[0]
    hidden = w_up.shape[1]
    placed = share % 16 == 0 and bits == 3 and heads == 3
    blocks = dp_count if placed else 1
    def core(value):
        return swap(value, "tensor", 1)

    def cross(value):
        return swap(value, "tensor", 2)

    def grow(value, got, masks, bit):
        both = jnp.stack([value, got], axis=1).reshape((-1,) + value.shape[1:])
        return both, [m ^ b for m in masks for b in (0, bit)]

    across = cross(tokens)
    beside = core(tokens)
    own_qkv = jnp.concatenate([w_query, w_key, w_value], axis=1)[None]
    own_b_up = lax.dynamic_slice_in_dim(b_up, group * share, share, 0)[:, None]
    spare = -(hidden + own_cols) % LANES
    one = jnp.concatenate([w_up, w_out.T, jnp.broadcast_to(own_b_up, (share, spare))], axis=1)[None]
    two = w_down.T[None]
    biases = [b_query.reshape(1, -1), b_value.reshape(1, -1)]
    vectors = [b_out, b_down, gain_attn, shift_attn, gain_ffn, shift_ffn]
    vectors = jnp.stack([vec.astype(F32) for vec in vectors] + [jnp.zeros((width,), F32)] * 2)

    kept = []
    if placed:
        got_w = after(swap(own_qkv, "dp", 4), one, two)
        w_part, w_mask = grow(own_qkv, got_w, [0], 4)
        one = after(one, w_part)
        got_w, got_one, across = after((swap(w_part, "dp", 2), swap(one, "dp", 4), across), w_part)
        w_part, w_mask = grow(w_part, got_w, w_mask, 2)
        one, one_mask = grow(one, got_one, [0], 4)

        two = after(two, across)
        round_three = (swap(w_part, "dp", 1), swap(one, "dp", 2), cross(two), core(across))
        round_three = after((round_three, biases, vectors), w_part)
        (got_w, got_one, got_two, beyond), biases, vectors = round_three
        w_qkv, w_masks = [w_part, got_w], [w_mask, [m ^ 1 for m in w_mask]]
        one, one_mask = grow(one, got_one, one_mask, 2)
        two = jnp.stack([two, got_two], axis=1)
        parts = [tokens, beside, across, beyond]

        round_four = (swap(two, "dp", 4), swap(one, "dp", 1), cross(one), core(one))
        positions = after(positions, one, two)
        q, k, v = project(parts, w_qkv, w_masks, *biases, positions, seq_lengths, heads, placed)
        q_kept, out, packed = attention_forward(0, q, k, v, [])
        kept.append((q_kept, out))
        got_two, odd, even_far, even_near = after(round_four, q_kept)
        two, two_mask = grow(two, got_two, [0], 4)

        round_five = (swap(two, "dp", 2), cross(odd), swap(two, "dp", 1), core(even_far))
        packed, odd, two, even_far = after((packed, odd, two, even_far), q_kept)
        q_kept, out, packed = attention_forward(1, q, k, v, packed)
        kept.append((q_kept, out))
        q = after(q, q_kept)
        q_kept, out, packed = attention_forward(2, q, k, v, packed)
        kept.append((q_kept, out))
        two_late, odd_far, two_odd, both_near = after(round_five, q_kept)

        far_odd = [m ^ 1 for m in one_mask]
        two_mask_odd = [m ^ 1 for m in two_mask]
        late_mask, last_mask = [m ^ 2 for m in two_mask], [m ^ 3 for m in two_mask]
        two_last = swap(two_late, "dp", 1)
        att_far = cross(packed[2])
        odd, two = after((odd, two), two_late)
        two_near, odd_near = core(two), core(odd)
        odd_far, two_late, two_odd = after((odd_far, two_late, two_odd), two_near, odd_near)
        odd_far_near, late_near, two_odd_near = core(odd_far), core(two_late), core(two_odd)
        two_last, att_far = after((two_last, att_far), odd_far_near, late_near, two_odd_near)
        att_near = core(jnp.stack([packed[1], att_far[1]]))
        ones = [(one, one_mask), (odd, far_odd), (even_far, one_mask), (odd_far, far_odd)]
        twos = [(two, two_mask), (two_odd, two_mask_odd), (two_late, late_mask), (two_last, last_mask)]
        early = [even_near, odd_near, both_near, odd_far_near, two_near, two_odd_near, late_near]
        early.append(core(two_last))
    else:
        w_qkv = [gather_bits(own_qkv[0], "dp", range(bits), 0).reshape(1, width, -1)]
        w_masks = [[0]]
        one = gather_bits(one[0], "dp", range(bits), 0).reshape(1, width, -1)
        two = gather_bits(two[0], "dp", range(bits), 0).reshape(1, width, -1)
        parts = [tokens, beside, across, core(across)]
        q, k, v = project(parts, w_qkv, w_masks, *biases, positions, seq_lengths, heads, placed)
        packed = []
        for h in range(heads):
            q_kept, out, packed = attention_forward(h, q, k, v, packed)
            kept.append((q_kept, out))
        ones = [(one, [0]), (cross(one), [0])]
        twos = [(jnp.stack([two, cross(two)], axis=1), [0])]
        early = [core(array) for array, _ in ones + twos]
        att_far = cross(packed[2])
        att_near = core(jnp.stack([packed[1], att_far[1]]))
    att = [packed[0], att_near, att_far]
    weights = [array for array, _ in ones + twos] + early
    plan = []
    for near in range(2):
        for a, (_, masks) in enumerate(ones):
            far = a // (len(ones) // 2)
            plan.append([((z,), False, near + 2 * far, mask) for z, mask in enumerate(masks)])
        for _, masks in twos:
            plan.append(
                [
                    ((z, far), True, near + 2 * far, mask)
                    for z, mask in enumerate(masks)
                    for far in range(2)
                ]
            )
    layer_out, d_one, sent_d, kept_d, sent_u, kept_u, *back = middle(
        blocks, weights, plan, att, tokens, out_grad, positions, seq_lengths, vectors, hidden
    )
    grads = [back[0]] + [swap(back[j], "tensor", j) for j in (1, 2, 3)]

    def add(*terms):
        total = terms[0].astype(F32)
        for term in terms[1:]:
            total = total + term.astype(F32)
        return total

    def send(away, name):
        return cross(away) if name == "x" else swap(away, "dp", 1 << name)

    def axes_of(array, lead):
        return array.reshape(array.shape[:lead] + (2,) * bits + array.shape[lead + 1 :])

    names = list(range(bits))[::-1]
    late = list(range(1, bits))
    shape = jax.ShapeDtypeStruct
    three = 3 * HEAD_DIM

    got_d, got_u = core(sent_d), core(sent_u)
    before = []
    if placed:
        down, up = Sum(["x"] + names, hidden), Sum(["x"] + names, hidden + own_cols)
        for total, arrays in ((down, (kept_d, got_d)), (up, (kept_u, got_u))):
            for array in arrays:
                total.join(axes_of(array, 1))
        move_d, move_u = reduce_call("sum_first", [[down.away("x")], [up.away(0)]], BF16)
        move_d, move_u = after((move_d, move_u), grads)
        grads = after(grads, move_d)
        down_names, up_names = ["x"] + late + [0], [0, "x"] + late
    for h in range(heads):
        q_kept = kept[h][0]
        if placed and h == heads - 1:
            last = before[:1]
            down.join(after(send(move_d, down_names.pop(0)), *last))
            up.join(after(send(move_u, up_names.pop(0)), *last))
            groups = [[down.away(down_names[0])], [up.away(up_names[0])]]
            move_d, move_u = reduce_call("sum_second", groups, BF16)
            q_kept = after(q_kept, move_d)
        g_all, g_w = attention_backward(
            h, q_kept, k, v, kept[h][1], grads, parts, blocks, before
        )
        before = [g_all, g_w]
    if placed:
        got_d = after(send(move_d, down_names.pop(0)), g_all)
        got_u = after(send(move_u, up_names.pop(0)), g_all)
        down.join(got_d)
        up.join(got_u)
        g_all, got_d, got_u = after((g_all, got_d, got_u), g_w)
        g_all = after(g_all, got_d, got_u)
    half = rows // 2
    first = input_part(g_all, w_qkv, w_masks, ((3 * rows, rows), (2 * rows, rows)), placed)
    got_part = core(first[0])
    own_parts = ((rows, half), (rows + half, half), (0, rows))
    if placed:
        qkv = Sum(["h"] + names, 4 * HEAD_DIM)
        qkv.join(axes_of(g_w, 1))
        groups = [[down.away(down_names[0])], [up.away(up_names[0])], [qkv.away(0)]]
        groups.append([[(first[1], (), 0, width), (got_part, (), 0, width)]])
        move_d, move_u, move_qkv, crossed = reduce_call("sum_third", groups, BF16)
        crossed = cross(crossed)
        g_all = after(g_all, move_d)
        second = input_part(g_all, w_qkv, w_masks, own_parts, placed)
        near = [core(part) for part in second[:2]]
        down.join(after(send(move_d, down_names.pop(0)), *second))
        up.join(after(send(move_u, up_names.pop(0)), *second))
        qkv.join(after(send(move_qkv, 0), *second))
        crossed = after(crossed, *second)
        others = list(itertools.product(range(2), repeat=len(late)))[1:]
        groups = [[down.away(down_names[0])], [up.away(up_names[0])]]
        groups += [[qkv.parts({**qkv.picks, **dict(zip(late, pick))})] for pick in others]
        move_d, move_u, *moves_qkv = reduce_call("sum_fourth", groups, BF16)
        down.join(send(move_d, down_names.pop(0)))
        got_u = send(move_u, up_names.pop(0))
        gots_qkv = [
            swap(move, "dp", sum(bit << name for bit, name in zip(pick, late)))
            for move, pick in zip(moves_qkv, others)
        ]
        qkv.picks.update(dict.fromkeys(late, 0))
        for name in late:
            qkv.names.remove(name)

        def finish_down(totals, ins, outs):
            outs[0][...] = totals[0][:share]
            outs[1][...] = totals[0][share:]
            for i in range(2):
                part = pl.ds(i * half, half)
                total = ins[0][part, :]
                for term in (ins[1][part, :], ins[2][part, :], ins[3 + i][...]):
                    total += term.astype(F32)
                outs[2][part, :] = total.astype(BF16)

        g_down, small, input_grad = reduce_call(
            "finish_down",
            [[down.all()]],
            F32,
            finish_down,
            (d_one, second[2], crossed, *near),
            (
                shape((share, hidden), F32),
                shape((EXTRA, width), F32),
                shape((rows, width), BF16),
            ),
            keep=False,
        )
        g_down = g_down.T
        got_u, gots_qkv = after((got_u, gots_qkv), small)
        up.join(got_u)
        for got in gots_qkv:
            qkv.join(got)
    else:
        crossed = cross(add(first[1], got_part).astype(BF16))
        second = input_part(g_all, w_qkv, w_masks, own_parts, placed)
        near = jnp.concatenate([core(part) for part in second[:2]])

    if placed:

        def finish(totals, _, outs):
            g_up, g_qkv = totals
            q_out, k_out, v_out, o_out, up_out, bq_out, bv_out = outs
            for h in range(heads):
                at = pl.ds(h * HEAD_DIM, HEAD_DIM)
                for kind, out in enumerate((q_out, k_out, v_out)):
                    out[:, at] = g_qkv[h, :, kind * HEAD_DIM : (kind + 1) * HEAD_DIM]
                bq_out[:, at] = g_qkv[h, 0:1, three:]
                bv_out[:, at] = g_qkv[h, 8:9, three:]
            up_out[...] = g_up[:, :hidden]
            o_out[...] = g_up[:, hidden:].T

        g_q, g_k, g_v, g_out, g_up, bias_q, bias_v = reduce_call(
            "finish",
            [[up.all()], [qkv.all()]],
            F32,
            finish,
            (),
            (
                [shape((share, own_cols), F32)] * 3
                + [shape((own_cols, share), F32), shape((share, hidden), F32)]
                + [shape((1, own_cols), F32)] * 2
            ),
            keep=False,
        )
        bias_q, bias_v = bias_q[0], bias_v[0]
    else:
        input_grad = add(d_one, second[2], near, crossed).astype(BF16)
        two_s = (2,) * bits

        def whole_sum(mine, got):
            total = add(mine, got)
            return total[0, 0] + cross(total[1, 0].astype(BF16)).astype(F32)

        def home(total, lead):
            shaped = total.reshape(total.shape[:lead] + two_s + (share, total.shape[-1]))
            return scatter_bits(shaped, "dp", range(bits), lead)

        total = whole_sum(kept_d, got_d)
        g_down, small = home(total[:width], 0).T, total[width:]
        total = home(whole_sum(kept_u, got_u), 0)
        g_up, g_out = total[:, :hidden], total[:, hidden:].T
        g_qkv = home(g_w[:, 0, :, :three].astype(F32), 1).reshape(heads, share, 3, HEAD_DIM)
        g_q, g_k, g_v = (g_qkv[:, :, i].transpose(1, 0, 2).reshape(share, own_cols) for i in range(3))
        bias_rows = g_w[:, 0, 0:16:8, three:].astype(F32)
        for bit in range(bits):
            small = small + swap(small, "dp", 1 << bit)
            bias_rows = bias_rows + swap(bias_rows, "dp", 1 << bit)
        bias_q, bias_v = bias_rows[:, 0].reshape(own_cols), bias_rows[:, 1].reshape(own_cols)
    count = jnp.sum(seq_lengths).astype(F32) * width
    rms = jnp.sqrt(jnp.sum(small[6:9], axis=-1) / count)
    return (
        layer_out,
        input_grad,
        g_q,
        g_k,
        g_v,
        g_out,
        g_up,
        g_down,
        bias_q,
        bias_v,
        small[0],
        small[9],
        small[1],
        small[2],
        small[3],
        small[4],
        small[5],
        rms,
    )


def solution(mesh):
    in_specs = (
        P(("dp", "tensor"), None),
        P(),
        P("dp", None),
        P("dp", "tensor"),
        P("dp", "tensor"),
        P("dp", "tensor"),
        P("tensor", "dp"),
        P("dp", "tensor"),
        P("tensor", "dp"),
        P("tensor"),
        P("tensor"),
        P(),
        P("tensor"),
        P(),
        P(),
        P(),
        P(),
        P(),
        P(("dp", "tensor"), None),
    )
    out_specs = (
        P(("dp", "tensor"), None),
        P(("dp", "tensor"), None),
        P("dp", "tensor"),
        P("dp", "tensor"),
        P("dp", "tensor"),
        P("tensor", "dp"),
        P("dp", "tensor"),
        P("tensor", "dp"),
        P("tensor"),
        P("tensor"),
        P(),
        P("tensor"),
        P(),
        P(),
        P(),
        P(),
        P(),
        P(),
    )
    return jax.shard_map(body, mesh=mesh, in_specs=in_specs, out_specs=out_specs, check_vma=False)
```

```python
import functools
import itertools

import jax
import jax.numpy as jnp
from jax import lax
from jax.experimental import pallas as pl
from jax.experimental.pallas import tpu as pltpu
from jax.sharding import PartitionSpec as P

HEAD_DIM = 64
LANES = 128
EPSILON = 1e-12
MASKED = -1e30
BF16 = jnp.bfloat16
F32 = jnp.float32
NT = (((1,), (1,)), ((), ()))
TN = (((0,), (0,)), ((), ()))
EXTRA = 16


def dot(left, right):
    return jnp.dot(left, right, preferred_element_type=F32)


def dot_nt(left, right):
    return lax.dot_general(left, right, NT, preferred_element_type=F32)


def dot_tn(left, right):
    return lax.dot_general(left, right, TN, preferred_element_type=F32)


def place_of(mask, height, placed):
    start = (lax.axis_index("dp") ^ mask) * height if placed else 0
    return pl.ds(pl.multiple_of(start, height), height)


def valid_row(positions_ref, lengths_ref, j, rows):
    start = (lax.axis_index("tensor") ^ j) * rows
    own = positions_ref[:, pl.ds(pl.multiple_of(start, rows), rows)]
    return own < lengths_ref[lax.axis_index("dp")]


def in_three(column):
    first = column.astype(BF16)
    rest = column - first.astype(F32)
    second = rest.astype(BF16)
    third = (rest - second.astype(F32)).astype(BF16)
    return first, second, third


def swap(value, axis, bits):
    size = lax.axis_size(axis)
    return lax.ppermute(value, axis, [(i, i ^ bits) for i in range(size)])


def bit_of(axis, bit):
    return (lax.axis_index(axis) >> bit) & 1


def gather_bits(block, axis, order, at):
    done = []
    for bit in order:
        place = at + sum(other > bit for other in done)
        got = swap(block, axis, 1 << bit)
        upper = bit_of(axis, bit) == 1
        low = jnp.where(upper, got, block)
        high = jnp.where(upper, block, got)
        block = jnp.stack([low, high], axis=place)
        done.append(bit)
    return block


def scatter_bits(partial, axis, order, at):
    left = sorted(order, reverse=True)
    for bit in order:
        place = at + left.index(bit)
        mine = bit_of(axis, bit)
        away = lax.dynamic_index_in_dim(partial, 1 - mine, place, keepdims=False)
        keep = lax.dynamic_index_in_dim(partial, mine, place, keepdims=False)
        got = swap(away.astype(BF16), axis, 1 << bit)
        partial = keep.astype(F32) + got.astype(F32)
        left.remove(bit)
    return partial


def after(value, *others):
    return lax.optimization_barrier((value,) + others)[0]


def params(mebibytes=63):
    return pltpu.CompilerParams(vmem_limit_bytes=mebibytes << 20)


def cost(flops, moved, exps=0):
    return pl.CostEstimate(flops=flops, bytes_accessed=moved, transcendentals=exps)


SMEM_SPEC = pl.BlockSpec(memory_space=pltpu.SMEM)
VMEM_SPEC = pl.BlockSpec(memory_space=pltpu.VMEM)
ANY_SPEC = pl.BlockSpec(memory_space=pl.ANY)
HBM_SPEC = pl.BlockSpec(memory_space=pltpu.HBM)


def project_kernel(*refs, masks, heads, placed):
    x_refs, w_refs = refs[:4], refs[4 : 4 + len(masks)]
    bq_ref, bv_ref, positions_ref, lengths_ref, q_out, k_out, v_out, w_s, x_s, m_s, sems = refs[
        4 + len(masks) :
    ]
    rows = x_refs[0].shape[0]
    loads = [pltpu.make_async_copy(x_refs[j], x_s.at[j], sems.at[j]) for j in range(4)]
    for load in loads:
        load.start()
    for ref, entries in zip(w_refs, masks, strict=True):
        for z, mask in enumerate(entries):
            w_s[place_of(mask, ref.shape[1], placed), :] = ref[z]
    lane = lax.broadcasted_iota(jnp.int32, (1, LANES), 1)
    head_lane = lane < HEAD_DIM
    one_q = jnp.where(lane == HEAD_DIM, 1.0, 0.0)
    one_k = jnp.where((lane > HEAD_DIM) & (lane <= HEAD_DIM + 3), 1.0, 0.0)
    one_v = jnp.where((lane >= HEAD_DIM) & (lane < HEAD_DIM + 3), 1.0, 0.0)
    b_query = bq_ref[...].astype(F32)
    bias = jnp.concatenate([b_query, jnp.zeros_like(b_query), bv_ref[...].astype(F32)], axis=1)
    for j in range(4):
        masked = jnp.where(valid_row(positions_ref, lengths_ref, j, rows), 0.0, MASKED)
        m_s[j] = jnp.broadcast_to(masked, (8, rows))
    for load in loads:
        load.wait()

    @pl.loop(0, 4)
    def _(j):
        part = pl.ds(pl.multiple_of(j * rows, rows), rows)
        whole = dot(x_s[j], w_s[...]) + bias
        masked = jnp.broadcast_to(m_s[j, 0:1, :], (LANES, rows)).T

        def columns(group):
            start = group // 2 * LANES
            both = whole[:, start : start + LANES]
            if both.shape[1] < LANES:
                both = jnp.concatenate([both, both], axis=1)
            return pltpu.roll(both, HEAD_DIM, 1) if group % 2 else both

        for h in range(heads):
            query = columns(h).astype(BF16).astype(F32) * (HEAD_DIM**-0.5)
            q_out[h, part, :] = jnp.where(head_lane, query, one_q).astype(BF16)
            key = jnp.where(head_lane, columns(heads + h), one_k)
            k_out[h, part, :] = jnp.where(lane == HEAD_DIM, masked, key).astype(BF16)
            value = jnp.where(head_lane, columns(2 * heads + h), one_v)
            v_out[h, part, :] = value.astype(BF16)


def project(parts, pieces, masks, b_query, b_value, positions, lengths, heads, placed):
    rows, width = parts[0].shape
    seq = 4 * rows
    return pl.pallas_call(
        functools.partial(project_kernel, masks=masks, heads=heads, placed=placed),
        in_specs=[ANY_SPEC] * 4 + [VMEM_SPEC] * (3 + len(pieces)) + [SMEM_SPEC],
        out_specs=[VMEM_SPEC] * 3,
        out_shape=[jax.ShapeDtypeStruct((heads, seq, LANES), BF16)] * 3,
        scratch_shapes=[
            pltpu.VMEM((width, pieces[0].shape[2]), BF16),
            pltpu.VMEM((4, rows, width), BF16),
            pltpu.VMEM((4, 8, rows), F32),
            pltpu.SemaphoreType.DMA((4,)),
        ],
        compiler_params=params(32),
        cost_estimate=cost(1000, 1000),
        name="project",
    )(*parts, *pieces, b_query, b_value, positions, lengths)


def forward_kernel(q_ref, k_ref, v_ref, *refs, unroll):
    q_out, o_out, own, near, far, packed = refs[-6:]
    seq = q_ref.shape[1]
    block = seq // 8
    lane = lax.broadcasted_iota(jnp.int32, (1, LANES), 1)
    head_lane = lane < HEAD_DIM

    def place(i):
        return pl.ds(pl.multiple_of(i * block, block), block)

    def scores_of(i):
        query = q_ref[0, place(i), :]
        scores = dot_nt(query, k_ref[0])
        return query, scores, jnp.max(scores, axis=-1, keepdims=True)

    def attend(i, query, scores, top):
        expon = jnp.exp(scores - top).astype(BF16)
        total = dot(expon, v_ref[0])
        row_sum = total[:, HEAD_DIM : HEAD_DIM + 1]
        out = total * (1.0 / row_sum)
        o_out[0, place(i), :] = out
        one, two, three = in_three(-(top + jnp.log(row_sum)))
        q_out[0, place(i), :] = jnp.where(
            lane == HEAD_DIM + 1,
            one,
            jnp.where(lane == HEAD_DIM + 2, two, jnp.where(lane == HEAD_DIM + 3, three, query)),
        )
        return out

    @pl.loop(0, 8 // unroll)
    def _(step):
        held = scores_of(step * unroll)
        even = None
        for u in range(unroll):
            i = step * unroll + u
            following = scores_of(i + 1) if u < unroll - 1 else None
            out = attend(i, *held)
            if u % 2 == 0:
                even = out
            else:
                pair = jnp.where(head_lane, even, pltpu.roll(out, HEAD_DIM, 1))
                packed[step * (unroll // 2) + u // 2] = pair.astype(BF16)
            held = following

    own[0] = packed[0]
    near[0] = packed[1]
    far[0, 0] = packed[2]
    far[1, 0] = packed[3]


def attention_forward(first, count, q, k, v, before):
    heads, seq, _ = q.shape
    block = seq // 8
    one = pl.BlockSpec((1, seq, LANES), lambda i: (first + i, 0, 0))
    piece = pl.BlockSpec((1, block, LANES), lambda i: (first + i, 0, 0))
    pieces = pl.BlockSpec((2, 1, block, LANES), lambda i: (0, first + i, 0, 0))
    shape = jax.ShapeDtypeStruct
    return pl.pallas_call(
        functools.partial(forward_kernel, unroll=4),
        grid=(count,),
        in_specs=[one] * 3 + [ANY_SPEC] * len(before),
        out_specs=[one, one, piece, piece, pieces],
        out_shape=[shape((heads, seq, LANES), BF16), shape((heads, seq, LANES), F32)]
        + [shape((heads, block, LANES), BF16)] * 2
        + [shape((2, heads, block, LANES), BF16)],
        scratch_shapes=[pltpu.VMEM((4, block, LANES), BF16)],
        input_output_aliases={3 + i: i for i in range(len(before))},
        compiler_params=params(32),
        cost_estimate=cost(1000, 1000),
        name="attention_forward",
    )(q, k, v, *before)


def backward_kernel(q_ref, k_ref, v_ref, o_ref, *refs, placed):
    d_refs, x_refs = refs[:4], refs[4:8]
    g_ref, gw_ref, dk_s, dv_s, gw_s, d_s = refs[-6:]
    seq = q_ref.shape[1]
    block = seq // 8
    rows = seq // 4
    lane = lax.broadcasted_iota(jnp.int32, (1, LANES), 1)
    head_lane = lane < HEAD_DIM
    scale = HEAD_DIM**-0.5
    for j in range(4):
        d_s[j] = d_refs[j][0]
    dk_s[...] = jnp.zeros_like(dk_s)
    dv_s[...] = jnp.zeros_like(dv_s)

    @pl.loop(0, 4)
    def _(j):
        for half in range(2):
            place = pl.ds(pl.multiple_of((2 * j + half) * block, block), block)
            query = q_ref[0, place, :]
            grad = d_s[j].astype(F32)
            if half == 1:
                grad = pltpu.roll(grad, HEAD_DIM, 1)
            grad = jnp.where(head_lane, grad, 0.0)
            delta = jnp.sum(grad * o_ref[0, place, :], axis=-1, keepdims=True)
            one, two, three = in_three(-delta)
            grad = grad.astype(BF16)
            grad_and = jnp.where(
                lane == HEAD_DIM,
                one,
                jnp.where(lane == HEAD_DIM + 1, two, jnp.where(lane == HEAD_DIM + 2, three, grad)),
            )
            probs = jnp.exp(dot_nt(k_ref[0], query))
            lifted = dot_nt(v_ref[0], grad_and)
            grad_scores = (probs * lifted).astype(BF16)
            dv_s[...] += dot(probs.astype(BF16), grad)
            dk_s[...] += dot(grad_scores, query)
            grad_query = dot_tn(grad_scores, k_ref[0]) * scale
            g_ref[0, place, :LANES] = jnp.where(head_lane, grad_query, 0.0).astype(BF16)

    both = jnp.where(head_lane, g_ref[0, :, :LANES].astype(F32), pltpu.roll(dk_s[...], HEAD_DIM, 1))
    g_ref[0, :, :LANES] = both.astype(BF16)
    g_ref[0, :, LANES:] = dv_s[:, :HEAD_DIM].astype(BF16)
    grads = g_ref[0]
    bias = jnp.sum(grads.astype(F32), axis=0, keepdims=True)
    share = gw_ref.shape[2]
    line = lax.broadcasted_iota(jnp.int32, (share, 1), 0)
    side = jnp.where(line < 8, bias[:, :HEAD_DIM], 0.0)
    side = jnp.where((line >= 8) & (line < 16), bias[:, LANES:], side).astype(BF16)
    total = dot_tn(grads[:rows], x_refs[0][...])
    for j in range(1, 4):
        total += dot_tn(grads[j * rows : (j + 1) * rows], x_refs[j][...])
    gw_s[...] = total.T.astype(BF16)
    for i in range(gw_ref.shape[1]):
        gw_ref[0, i, :, : 3 * HEAD_DIM] = gw_s[place_of(i, share, placed), :]
        gw_ref[0, i, :, 3 * HEAD_DIM :] = side


def attention_backward(first, count, q, k, v, out, grads, parts, blocks, before):
    heads, seq, _ = k.shape
    rows, width = parts[0].shape
    one = pl.BlockSpec((1, seq, LANES), lambda i: (first + i, 0, 0))
    piece = pl.BlockSpec((1, seq // 8, LANES), lambda i: (first + i, 0, 0))
    whole = pl.BlockSpec((rows, width), lambda i: (0, 0))
    three = 3 * HEAD_DIM
    share = width // blocks
    shape = jax.ShapeDtypeStruct
    alias = {12: 0, 13: 1} if before else {}
    return pl.pallas_call(
        functools.partial(backward_kernel, placed=blocks > 1),
        grid=(count,),
        in_specs=[one] * 4 + [piece] * 4 + [whole] * 4 + [ANY_SPEC] * len(before),
        out_specs=[
            pl.BlockSpec((1, seq, three), lambda i: (first + i, 0, 0)),
            pl.BlockSpec((1, blocks, share, 4 * HEAD_DIM), lambda i: (first + i, 0, 0, 0)),
        ],
        out_shape=[
            shape((heads, seq, three), BF16),
            shape((heads, blocks, share, 4 * HEAD_DIM), BF16),
        ],
        scratch_shapes=[
            pltpu.VMEM((seq, LANES), F32),
            pltpu.VMEM((seq, LANES), F32),
            pltpu.VMEM((width, three), BF16),
            pltpu.VMEM((4, seq // 8, LANES), BF16),
        ],
        input_output_aliases=alias,
        compiler_params=params(),
        cost_estimate=cost(1000, 1000),
        name="attention_backward",
    )(q, k, v, out, *grads, *parts, *before)


def input_kernel(g_ref, *refs, masks, which, placed):
    w_refs = refs[: len(masks)]
    outs, w_s = refs[len(masks) : -1], refs[-1]
    heads, seq, three = g_ref.shape
    for ref, entries in zip(w_refs, masks, strict=True):
        for z, mask in enumerate(entries):
            place = place_of(mask, ref.shape[1], placed)
            for h in range(heads):
                for kind in range(3):
                    start = (kind * heads + h) * HEAD_DIM
                    stop = (h * 3 + kind) * HEAD_DIM
                    w_s[place, stop : stop + HEAD_DIM] = ref[z, :, start : start + HEAD_DIM]
    for out, (start, count) in zip(outs, which, strict=True):
        part = pl.ds(start, count)
        total = dot_nt(g_ref[0, part, :], w_s[:, :three])
        for h in range(1, heads):
            total += dot_nt(g_ref[h, part, :], w_s[:, h * three : (h + 1) * three])
        out[...] = total.astype(out.dtype)


def input_part(g_all, pieces, masks, which, placed):
    heads, seq, three = g_all.shape
    width = pieces[0].shape[0] * pieces[0].shape[1] * len(pieces)
    return pl.pallas_call(
        functools.partial(input_kernel, masks=masks, which=which, placed=placed),
        in_specs=[VMEM_SPEC] * (1 + len(pieces)),
        out_specs=[VMEM_SPEC] * len(which),
        out_shape=[jax.ShapeDtypeStruct((count, width), BF16) for _, count in which],
        scratch_shapes=[pltpu.VMEM((width, heads * three), BF16)],
        compiler_params=params(),
        cost_estimate=cost(1000, 1000),
        name="input_part",
    )(g_all, *pieces)


def middle_kernel(*refs, plan, blocks):
    w_refs = refs[: len(plan)]
    refs = refs[len(plan) :]
    own_ref, near_ref, far_ref = refs[:3]
    x_ref, og_ref, positions_ref, lengths_ref, vec_ref = refs[3:8]
    lo_ref, done_ref, sent_d, kept_d, sent_u, kept_u = refs[8:14]
    ga = refs[14:18]
    w1_s, w2_s, att_s, wo_s, hid_s, slope_s, nrm_s, nb_s, n1_s, rs_s, ffn_s = refs[18:29]
    gf_s, gft_s, nbt_s, acc_s, pre_s, g_s, bup_s, mask_s, sums_ref, low_s, two_s, act_s, in_sem, down_sem, up_sem, out_sem, low_sem = refs[29:]
    rows, width = x_ref.shape
    hidden = w2_s.shape[2]
    pieces = 4
    cols = width // pieces
    placed = blocks > 1
    chunk = 128
    share = width // blocks
    half = rows // 2
    b_out, b_down, gain_a, shift_a, gain_f, shift_f = (vec_ref[i : i + 1, :] for i in range(6))

    count = cols // HEAD_DIM
    att = [[own_ref[h] for h in range(count)]]
    for ref, i in ((near_ref, 0), (far_ref, 0), (near_ref, 1)):
        att.append([ref[i, h] for h in range(count)])

    loads = []
    for ref, entries in zip(w_refs, plan, strict=True):
        for index, second, j, row in entries:
            source = ref.at[index]
            target = (w2_s if second else w1_s).at[j].at[place_of(row, source.shape[0], placed)]
            copy = pltpu.make_async_copy(source, target, in_sem.at[len(loads)])
            loads.append((second, copy))
            copy.start()

    def row_loop(work):
        @pl.loop(0, rows // chunk)
        def _(i):
            work(pl.ds(pl.multiple_of(i * chunk, chunk), chunk))

    def add_sum(index, value):
        sums_ref[index : index + 1, :] += jnp.sum(value, axis=0, keepdims=True)

    def mean(value):
        return jnp.mean(value, axis=-1, keepdims=True)

    def normal(value):
        centred = value - mean(value)
        inverse = lax.rsqrt(mean(centred * centred) + EPSILON)
        return centred * inverse, inverse

    def norm_back(grad, unit, inverse, gain):
        scaled = grad * gain
        return (scaled - mean(scaled) - unit * mean(scaled * unit)) * inverse

    sums_ref[...] = jnp.zeros_like(sums_ref)
    own_valid = jnp.where(valid_row(positions_ref, lengths_ref, 0, rows), 1.0, 0.0)
    mask_s[...] = jnp.broadcast_to(own_valid, (LANES, rows)).T
    for j in range(pieces):
        for h in range(cols // HEAD_DIM):
            at = j * cols + h * HEAD_DIM
            att_s[:half, at : at + HEAD_DIM] = att[j][h][:, :HEAD_DIM]
            att_s[half:, at : at + HEAD_DIM] = att[j][h][:, HEAD_DIM:]
    for second, copy in loads:
        if not second:
            copy.wait()
    for j in range(pieces):
        wo_s[:, j * cols : (j + 1) * cols] = w1_s[j, :, hidden : hidden + cols]
        last = w1_s[j, :, hidden + cols - HEAD_DIM :].astype(F32)
        bup_s[j] = last.T[HEAD_DIM : HEAD_DIM + 1, :]
    ffn_s[...] = dot_nt(att_s[...], wo_s[...])

    def first_norm(r):
        value = x_ref[r, :].astype(F32)
        attn = ffn_s[r, :] + b_out
        valid = mask_s[r, :1] > 0.0
        add_sum(6, jnp.where(valid, value * value, 0.0))
        add_sum(7, jnp.where(valid, attn * attn, 0.0))
        unit, inverse = normal(value + attn)
        normed = unit * gain_a + shift_a
        n1_s[r, :] = unit
        rs_s[r, :] = jnp.broadcast_to(inverse, (chunk, LANES))
        nrm_s[r, :] = normed
        nb_s[r, :] = normed.astype(BF16)

    row_loop(first_norm)
    ffn_s[...] = jnp.zeros_like(ffn_s)
    for second, copy in loads:
        if second:
            copy.wait()

    wide = 256
    per = hidden // wide

    def chunk_of(c):
        return c // per, pl.ds(pl.multiple_of(c % per * wide, wide), wide)

    def product_of(c):
        j, at = chunk_of(c)
        return dot(nb_s[...], w1_s[j, :, at]) + bup_s[j, :, at]

    act_s[...] = jnp.zeros_like(act_s)
    two_s[0] = product_of(0)
    count = pieces * per

    @pl.loop(0, count)
    def _(c):
        j, at = chunk_of(c)
        back, behind = chunk_of(jnp.maximum(c - 1, 0))
        now = c % 2
        two_s[1 - now] = product_of(jnp.minimum(c + 1, count - 1))
        ffn_s[...] += dot_nt(act_s[...], w2_s[back, :, behind])
        pre = two_s[now]
        cdf = 0.5 * (1.0 + lax.erf(pre * (0.5**0.5)))
        pdf = jnp.exp(pre * pre * -0.5) * (2.0 * jnp.pi) ** -0.5
        act = (pre * cdf).astype(BF16)
        hid_s[j, :, at] = act
        slope_s[j, :, at] = cdf + pre * pdf
        act_s[...] = act

    ffn_s[...] += dot_nt(act_s[...], w2_s[pieces - 1, :, (per - 1) * wide :])

    def second_norm(r):
        ffn = ffn_s[r, :] + b_down
        valid = mask_s[r, :1] > 0.0
        add_sum(8, jnp.where(valid, ffn * ffn, 0.0))
        unit, inverse = normal(nrm_s[r, :] + ffn)
        lo_ref[r, :] = (unit * gain_f + shift_f).astype(BF16)
        grad = og_ref[r, :].astype(F32)
        add_sum(4, grad * unit)
        add_sum(5, grad)
        d_two = norm_back(grad, unit, inverse, gain_f)
        low = d_two.astype(BF16)
        add_sum(1, low.astype(F32))
        acc_s[r, :] = d_two
        gf_s[r, :] = low

    row_loop(second_norm)
    gft_s[...] = gf_s[...].T
    nbt_s[...] = nb_s[...].T

    places = [place_of(i, share, placed) for i in range(blocks)]

    def copies(j, lanes, target, place, sem, to):
        return [
            pltpu.make_async_copy(
                g_s.at[j].at[places[i], lanes], target.at[place, i, pl.ds(0, share), to], sem.at[j, i]
            )
            for i in range(blocks)
        ]

    lanes_d, lanes_u, lanes_o = (
        pl.ds(0, hidden),
        pl.ds(hidden, hidden),
        pl.ds(2 * hidden, cols),
    )
    to_d, to_u, to_o = pl.ds(0, hidden), pl.ds(0, hidden), pl.ds(hidden, cols)
    def start_all(j, place, lanes, to, sem, targets):
        for away in (1, 0):

            @pl.when(j % 2 == away)
            def _():
                for copy in copies(j, lanes, targets[1 - away], place, sem, to):
                    copy.start()

    @pl.loop(0, pieces)
    def _(step):
        away = 1 - step // (pieces // 2)
        place = step % (pieces // 2)
        j = 2 * place + away
        pre_s[...] = dot(gf_s[...], w2_s[j]) * slope_s[j]
        low = pre_s[...].astype(BF16)
        sums_ref[pl.ds(10 + j, 1), :] = jnp.sum(low.astype(F32), axis=0, keepdims=True)
        g_s[j, :, lanes_d] = dot(gft_s[...], hid_s[j]).astype(BF16)
        start_all(j, place, lanes_d, to_d, down_sem, (sent_d, kept_d))
        g_s[j, :, lanes_u] = dot(nbt_s[...], low).astype(BF16)
        start_all(j, place, lanes_u, to_u, up_sem, (sent_u, kept_u))
        acc_s[...] += dot_nt(low, w1_s[j, :, :hidden])

    def first_back(r):
        grad = acc_s[r, :]
        unit = n1_s[r, :]
        add_sum(2, grad * unit)
        add_sum(3, grad)
        d_one = norm_back(grad, unit, rs_s[r, :1], gain_a)
        low = d_one.astype(BF16)
        add_sum(0, low.astype(F32))
        done_ref[r, :] = d_one
        gf_s[r, :] = low

    row_loop(first_back)
    low = gf_s[...]
    gout = dot_tn(low, att_s[...]).astype(BF16)
    for j in range(pieces):
        g_s[j, :, 2 * hidden : 2 * hidden + cols] = gout[:, j * cols : (j + 1) * cols]
        for copy in copies(j, lanes_o, sent_u if j % 2 else kept_u, j // 2, out_sem, to_o):
            copy.start()
    small = []
    for j in range(pieces):
        low_s[j] = jnp.concatenate([sums_ref[:9], sums_ref[10 + j : 11 + j], sums_ref[9:15]]).astype(BF16)
        target = sent_d if j % 2 else kept_d
        for i in range(blocks):
            under = target.at[j // 2, i, pl.ds(share, EXTRA), :]
            small.append(pltpu.make_async_copy(low_s.at[j], under, low_sem.at[j, i]))
            small[-1].start()
    back = dot(low, wo_s[...]).astype(BF16)
    for j in range(pieces):
        for h in range(cols // HEAD_DIM):
            at = j * cols + h * HEAD_DIM
            ga[j][h, :, :HEAD_DIM] = back[:half, at : at + HEAD_DIM]
            ga[j][h, :, HEAD_DIM:] = back[half:, at : at + HEAD_DIM]
    for j in range(pieces):
        target_d, target_u = (sent_d, sent_u) if j % 2 else (kept_d, kept_u)
        for copy in copies(j, lanes_d, target_d, j // 2, down_sem, to_d):
            copy.wait()
        for copy in copies(j, lanes_u, target_u, j // 2, up_sem, to_u):
            copy.wait()
        for copy in copies(j, lanes_o, target_u, j // 2, out_sem, to_o):
            copy.wait()
    for copy in small:
        copy.wait()


def middle(blocks, weights, plan, att, tokens, out_grad, positions, lengths, vectors, hidden):
    rows, width = tokens.shape
    cols = width // 4
    share = width // blocks
    shape = jax.ShapeDtypeStruct
    vmem = pltpu.VMEM
    loads = sum(len(entries) for entries in plan)
    return pl.pallas_call(
        functools.partial(middle_kernel, plan=plan, blocks=blocks),
        in_specs=[ANY_SPEC] * len(weights) + [VMEM_SPEC] * 6 + [SMEM_SPEC, VMEM_SPEC],
        out_specs=[VMEM_SPEC] * 2 + [ANY_SPEC] * 4 + [VMEM_SPEC] * 4,
        out_shape=[
            shape((rows, width), BF16),
            shape((rows, width), F32),
        ]
        + [shape((2, blocks, share + EXTRA, hidden), BF16)] * 2
        + [shape((2, blocks, share, hidden + cols), BF16)] * 2
        + [shape(att[0].shape, BF16)] * 4,
        scratch_shapes=[
            vmem((4, width, weights[0].shape[-1]), BF16),
            vmem((4, width, hidden), BF16),
            vmem((rows, width), BF16),
            vmem((width, width), BF16),
            vmem((4, rows, hidden), BF16),
            vmem((4, rows, hidden), F32),
            vmem((rows, width), F32),
            vmem((rows, width), BF16),
            vmem((rows, width), F32),
            vmem((rows, LANES), F32),
            vmem((rows, width), F32),
            vmem((rows, width), BF16),
            vmem((width, rows), BF16),
            vmem((width, rows), BF16),
            vmem((rows, width), F32),
            vmem((rows, hidden), F32),
            vmem((4, width, 2 * hidden + cols), BF16),
            vmem((4, 1, hidden), F32),
            vmem((rows, LANES), F32),
            vmem((16, width), F32),
            vmem((4, EXTRA, width), BF16),
            vmem((2, rows, 256), F32),
            vmem((rows, 256), BF16),
            pltpu.SemaphoreType.DMA((loads,)),
            pltpu.SemaphoreType.DMA((4, blocks)),
            pltpu.SemaphoreType.DMA((4, blocks)),
            pltpu.SemaphoreType.DMA((4, blocks)),
            pltpu.SemaphoreType.DMA((4, blocks)),
        ],
        compiler_params=params(),
        cost_estimate=cost(1000, 1000),
        name="middle",
    )(*weights, *att, tokens, out_grad, positions, lengths, vectors)


def reduce_kernel(*refs, jobs, inputs, outputs, terms, extra, extra_in):
    ins = refs[:inputs]
    more = refs[inputs : inputs + extra_in]
    outs = refs[inputs + extra_in : inputs + extra_in + outputs]
    rest = refs[inputs + extra_in + outputs :]
    extra_out = rest[: len(rest) - terms - 1]
    held, sems = rest[len(extra_out) : -1], rest[-1]
    loads = []
    for _, _, _, parts in jobs:
        for source, index, start, size in parts:
            at = len(loads)
            picked = ins[source].at[index + (slice(None), pl.ds(start, size))]
            loads.append(pltpu.make_async_copy(picked, held[at], sems.at[at]))
            loads[-1].start()
    at = 0
    for out, start, lead, parts in jobs:
        mine = range(at, at + len(parts))
        at += len(parts)
        for i in mine:
            loads[i].wait()
        size = parts[0][3]
        for index in itertools.product(*map(range, lead)):
            total = held[mine[0]][index].astype(F32)
            for i in mine[1:]:
                total += held[i][index].astype(F32)
            target = outs[out]
            target[index + (slice(None), slice(start, start + size))] = total.astype(target.dtype)
    if extra is not None:
        extra(outs, more, extra_out)


class Sum:
    def __init__(self, names, width):
        self.names, self.width, self.terms, self.picks = list(names), width, [], {}

    def join(self, array, start=0, names=None):
        self.terms.append((array, start, list(self.names if names is None else names)))

    def parts(self, picks):
        return [
            (array, tuple(picks.get(name, slice(None)) for name in names), start, self.width)
            for array, start, names in self.terms
        ]

    def away(self, name):
        parts = self.parts({**self.picks, name: 1})
        self.picks[name] = 0
        self.names.remove(name)
        return parts

    def all(self):
        return self.parts(self.picks)


def reduce_call(name, groups, dtype, extra=None, extra_in=(), extra_out=(), keep=True):
    arrays, jobs, shapes, scratch = [], [], [], []
    for out, columns in enumerate(groups):
        start = 0
        for parts in columns:
            coded = []
            for array, index, first, size in parts:
                known = [i for i, other in enumerate(arrays) if other is array]
                if not known:
                    arrays.append(array)
                coded.append((known[0] if known else len(arrays) - 1, index, first, size))
                sizes = [n for n, i in zip(array.shape, index) if isinstance(i, slice)]
                sizes += [array.shape[-2], size]
                scratch.append(pltpu.VMEM(tuple(sizes), array.dtype))
            jobs.append((out, start, tuple(sizes[:-2]), coded))
            start += coded[0][3]
        shapes.append(tuple(sizes[:-1]) + (start,))
    outs = [jax.ShapeDtypeStruct(shape, dtype) for shape in shapes]
    held = [] if keep else [pltpu.VMEM(shape, dtype) for shape in shapes]
    result = pl.pallas_call(
        functools.partial(
            reduce_kernel if keep else reduce_inside,
            jobs=jobs,
            inputs=len(arrays),
            outputs=len(outs),
            terms=len(scratch),
            extra=extra,
            extra_in=len(extra_in),
        ),
        in_specs=[HBM_SPEC] * len(arrays) + [VMEM_SPEC] * len(extra_in),
        out_specs=[VMEM_SPEC] * (len(outs) * keep + len(extra_out)),
        out_shape=outs * keep + list(extra_out),
        scratch_shapes=held + scratch + [pltpu.SemaphoreType.DMA((len(scratch),))],
        compiler_params=params(),
        cost_estimate=cost(1000, 1000),
        name=name,
    )(*arrays, *extra_in)
    return result


def reduce_inside(*refs, inputs, extra_in, outputs, terms, **rest):
    front = inputs + extra_in
    results = refs[front : len(refs) - outputs - terms - 1]
    held = refs[len(refs) - outputs - terms - 1 : len(refs) - terms - 1]
    order = refs[:front] + held + results + refs[len(refs) - terms - 1 :]
    reduce_kernel(*order, inputs=inputs, extra_in=extra_in, outputs=outputs, terms=terms, **rest)


def body(
    tokens,
    seq_lengths,
    positions,
    w_query,
    w_key,
    w_value,
    w_out,
    w_up,
    w_down,
    b_query,
    b_value,
    b_out,
    b_up,
    b_down,
    gain_attn,
    shift_attn,
    gain_ffn,
    shift_ffn,
    out_grad,
):
    group = lax.axis_index("dp")
    member = lax.axis_index("tensor")
    dp_count = lax.axis_size("dp")
    bits = dp_count.bit_length() - 1
    rows, width = tokens.shape
    own_cols = w_query.shape[1]
    heads = own_cols // HEAD_DIM
    share = w_query.shape[0]
    hidden = w_up.shape[1]
    placed = share % 16 == 0 and bits == 3 and heads == 3
    blocks = dp_count if placed else 1
    def core(value):
        return swap(value, "tensor", 1)

    def cross(value):
        return swap(value, "tensor", 2)

    def grow(value, got, masks, bit):
        both = jnp.stack([value, got], axis=1).reshape((-1,) + value.shape[1:])
        return both, [m ^ b for m in masks for b in (0, bit)]

    across = cross(tokens)
    beside = core(tokens)
    own_qkv = jnp.concatenate([w_query, w_key, w_value], axis=1)[None]
    own_b_up = lax.dynamic_slice_in_dim(b_up, group * share, share, 0)[:, None]
    spare = -(hidden + own_cols) % LANES
    one = jnp.concatenate([w_up, w_out.T, jnp.broadcast_to(own_b_up, (share, spare))], axis=1)[None]
    two = w_down.T[None]
    biases = [b_query.reshape(1, -1), b_value.reshape(1, -1)]
    vectors = [b_out, b_down, gain_attn, shift_attn, gain_ffn, shift_ffn]
    vectors = jnp.stack([vec.astype(F32) for vec in vectors] + [jnp.zeros((width,), F32)] * 2)

    if placed:
        got_w = after(swap(own_qkv, "dp", 4), one, two)
        w_part, w_mask = grow(own_qkv, got_w, [0], 4)
        one = after(one, w_part)
        got_w, got_one, across = after((swap(w_part, "dp", 2), swap(one, "dp", 4), across), w_part)
        w_part, w_mask = grow(w_part, got_w, w_mask, 2)
        one, one_mask = grow(one, got_one, [0], 4)

        two = after(two, across)
        round_three = (swap(w_part, "dp", 1), swap(one, "dp", 2), cross(two), core(across))
        round_three = after((round_three, biases, vectors), w_part)
        (got_w, got_one, got_two, beyond), biases, vectors = round_three
        w_qkv, w_masks = [w_part, got_w], [w_mask, [m ^ 1 for m in w_mask]]
        one, one_mask = grow(one, got_one, one_mask, 2)
        two = jnp.stack([two, got_two], axis=1)
        parts = [tokens, beside, across, beyond]

        round_four = (swap(two, "dp", 4), swap(one, "dp", 1), cross(one), core(one))
        positions = after(positions, one, two)
        q, k, v = project(parts, w_qkv, w_masks, *biases, positions, seq_lengths, heads, placed)
        kept = attention_forward(0, 1, q, k, v, [])
        q_kept = kept[0]
        got_two, odd, even_far, even_near = after(round_four, q_kept)
        two, two_mask = grow(two, got_two, [0], 4)

        round_five = (swap(two, "dp", 2), cross(odd), swap(two, "dp", 1), core(even_far))
        kept, odd, two, even_far = after((kept, odd, two, even_far), q_kept)
        q_kept, out, *packed = attention_forward(1, 2, q, k, v, kept)
        kept = [q_kept, out]
        two_late, odd_far, two_odd, both_near = after(round_five, q_kept)

        far_odd = [m ^ 1 for m in one_mask]
        two_mask_odd = [m ^ 1 for m in two_mask]
        late_mask, last_mask = [m ^ 2 for m in two_mask], [m ^ 3 for m in two_mask]
        two_last = swap(two_late, "dp", 1)
        att_far = cross(packed[2])
        odd, two = after((odd, two), two_late)
        two_near, odd_near = core(two), core(odd)
        odd_far, two_late, two_odd = after((odd_far, two_late, two_odd), two_near, odd_near)
        odd_far_near, late_near, two_odd_near = core(odd_far), core(two_late), core(two_odd)
        two_last, att_far = after((two_last, att_far), odd_far_near, late_near, two_odd_near)
        att_near = core(jnp.stack([packed[1], att_far[1]]))
        ones = [(one, one_mask), (odd, far_odd), (even_far, one_mask), (odd_far, far_odd)]
        twos = [(two, two_mask), (two_odd, two_mask_odd), (two_late, late_mask), (two_last, last_mask)]
        early = [even_near, odd_near, both_near, odd_far_near, two_near, two_odd_near, late_near]
        early.append(core(two_last))
    else:
        w_qkv = [gather_bits(own_qkv[0], "dp", range(bits), 0).reshape(1, width, -1)]
        w_masks = [[0]]
        one = gather_bits(one[0], "dp", range(bits), 0).reshape(1, width, -1)
        two = gather_bits(two[0], "dp", range(bits), 0).reshape(1, width, -1)
        parts = [tokens, beside, across, core(across)]
        q, k, v = project(parts, w_qkv, w_masks, *biases, positions, seq_lengths, heads, placed)
        q_kept, out, *packed = attention_forward(0, heads, q, k, v, [])
        kept = [q_kept, out]
        ones = [(one, [0]), (cross(one), [0])]
        twos = [(jnp.stack([two, cross(two)], axis=1), [0])]
        early = [core(array) for array, _ in ones + twos]
        att_far = cross(packed[2])
        att_near = core(jnp.stack([packed[1], att_far[1]]))
    att = [packed[0], att_near, att_far]
    weights = [array for array, _ in ones + twos] + early
    plan = []
    for near in range(2):
        for a, (_, masks) in enumerate(ones):
            far = a // (len(ones) // 2)
            plan.append([((z,), False, near + 2 * far, mask) for z, mask in enumerate(masks)])
        for _, masks in twos:
            plan.append(
                [
                    ((z, far), True, near + 2 * far, mask)
                    for z, mask in enumerate(masks)
                    for far in range(2)
                ]
            )
    layer_out, d_one, sent_d, kept_d, sent_u, kept_u, *back = middle(
        blocks, weights, plan, att, tokens, out_grad, positions, seq_lengths, vectors, hidden
    )
    grads = [back[0]] + [swap(back[j], "tensor", j) for j in (1, 2, 3)]

    def add(*terms):
        total = terms[0].astype(F32)
        for term in terms[1:]:
            total = total + term.astype(F32)
        return total

    def send(away, name):
        return cross(away) if name == "x" else swap(away, "dp", 1 << name)

    def axes_of(array, lead):
        return array.reshape(array.shape[:lead] + (2,) * bits + array.shape[lead + 1 :])

    names = list(range(bits))[::-1]
    late = list(range(1, bits))
    shape = jax.ShapeDtypeStruct
    three = 3 * HEAD_DIM

    got_d, got_u = core(sent_d), core(sent_u)
    if placed:
        down, up = Sum(["x"] + names, hidden), Sum(["x"] + names, hidden + own_cols)
        for total, arrays in ((down, (kept_d, got_d)), (up, (kept_u, got_u))):
            for array in arrays:
                total.join(axes_of(array, 1))
        move_d, move_u = reduce_call("sum_first", [[down.away("x")], [up.away(0)]], BF16)
        move_d, move_u = after((move_d, move_u), grads)
        grads = after(grads, move_d)
        down_names, up_names = ["x"] + late + [0], [0, "x"] + late
    q_kept, out = kept
    if placed:
        before = attention_backward(0, heads - 1, q_kept, k, v, out, grads, parts, blocks, [])
        last = before[0]
        down.join(after(send(move_d, down_names.pop(0)), last))
        up.join(after(send(move_u, up_names.pop(0)), last))
        groups = [[down.away(down_names[0])], [up.away(up_names[0])]]
        move_d, move_u = reduce_call("sum_second", groups, BF16)
        q_kept = after(q_kept, move_d)
        g_all, g_w = attention_backward(
            heads - 1, 1, q_kept, k, v, out, grads, parts, blocks, before
        )
    else:
        g_all, g_w = attention_backward(0, heads, q_kept, k, v, out, grads, parts, blocks, [])
    if placed:
        got_d = after(send(move_d, down_names.pop(0)), g_all)
        got_u = after(send(move_u, up_names.pop(0)), g_all)
        down.join(got_d)
        up.join(got_u)
        g_all, got_d, got_u = after((g_all, got_d, got_u), g_w)
        g_all = after(g_all, got_d, got_u)
    half = rows // 2
    first = input_part(g_all, w_qkv, w_masks, ((3 * rows, rows), (2 * rows, rows)), placed)
    got_part = core(first[0])
    own_parts = ((rows, half), (rows + half, half), (0, rows))
    if placed:
        qkv = Sum(["h"] + names, 4 * HEAD_DIM)
        qkv.join(axes_of(g_w, 1))
        groups = [[down.away(down_names[0])], [up.away(up_names[0])], [qkv.away(0)]]
        groups.append([[(first[1], (), 0, width), (got_part, (), 0, width)]])
        move_d, move_u, move_qkv, crossed = reduce_call("sum_third", groups, BF16)
        crossed = cross(crossed)
        g_all = after(g_all, move_d)
        second = input_part(g_all, w_qkv, w_masks, own_parts, placed)
        near = [core(part) for part in second[:2]]
        down.join(after(send(move_d, down_names.pop(0)), *second))
        up.join(after(send(move_u, up_names.pop(0)), *second))
        qkv.join(after(send(move_qkv, 0), *second))
        crossed = after(crossed, *second)
        others = list(itertools.product(range(2), repeat=len(late)))[1:]
        groups = [[down.away(down_names[0])], [up.away(up_names[0])]]
        groups += [[qkv.parts({**qkv.picks, **dict(zip(late, pick))})] for pick in others]
        move_d, move_u, *moves_qkv = reduce_call("sum_fourth", groups, BF16)
        down.join(send(move_d, down_names.pop(0)))
        got_u = send(move_u, up_names.pop(0))
        gots_qkv = [
            swap(move, "dp", sum(bit << name for bit, name in zip(pick, late)))
            for move, pick in zip(moves_qkv, others)
        ]
        qkv.picks.update(dict.fromkeys(late, 0))
        for name in late:
            qkv.names.remove(name)

        def finish_down(totals, ins, outs):
            outs[0][...] = totals[0][:share]
            outs[1][...] = totals[0][share:]
            for i in range(2):
                part = pl.ds(i * half, half)
                total = ins[0][part, :]
                for term in (ins[1][part, :], ins[2][part, :], ins[3 + i][...]):
                    total += term.astype(F32)
                outs[2][part, :] = total.astype(BF16)

        g_down, small, input_grad = reduce_call(
            "finish_down",
            [[down.all()]],
            F32,
            finish_down,
            (d_one, second[2], crossed, *near),
            (
                shape((share, hidden), F32),
                shape((EXTRA, width), F32),
                shape((rows, width), BF16),
            ),
            keep=False,
        )
        g_down = g_down.T
        got_u, gots_qkv = after((got_u, gots_qkv), small)
        up.join(got_u)
        for got in gots_qkv:
            qkv.join(got)
    else:
        crossed = cross(add(first[1], got_part).astype(BF16))
        second = input_part(g_all, w_qkv, w_masks, own_parts, placed)
        near = jnp.concatenate([core(part) for part in second[:2]])

    if placed:

        def finish(totals, _, outs):
            g_up, g_qkv = totals
            q_out, k_out, v_out, o_out, up_out, bq_out, bv_out = outs
            for h in range(heads):
                at = pl.ds(h * HEAD_DIM, HEAD_DIM)
                for kind, out in enumerate((q_out, k_out, v_out)):
                    out[:, at] = g_qkv[h, :, kind * HEAD_DIM : (kind + 1) * HEAD_DIM]
                bq_out[:, at] = g_qkv[h, 0:1, three:]
                bv_out[:, at] = g_qkv[h, 8:9, three:]
            up_out[...] = g_up[:, :hidden]
            o_out[...] = g_up[:, hidden:].T

        g_q, g_k, g_v, g_out, g_up, bias_q, bias_v = reduce_call(
            "finish",
            [[up.all()], [qkv.all()]],
            F32,
            finish,
            (),
            (
                [shape((share, own_cols), F32)] * 3
                + [shape((own_cols, share), F32), shape((share, hidden), F32)]
                + [shape((1, own_cols), F32)] * 2
            ),
            keep=False,
        )
        bias_q, bias_v = bias_q[0], bias_v[0]
    else:
        input_grad = add(d_one, second[2], near, crossed).astype(BF16)
        two_s = (2,) * bits

        def whole_sum(mine, got):
            total = add(mine, got)
            return total[0, 0] + cross(total[1, 0].astype(BF16)).astype(F32)

        def home(total, lead):
            shaped = total.reshape(total.shape[:lead] + two_s + (share, total.shape[-1]))
            return scatter_bits(shaped, "dp", range(bits), lead)

        total = whole_sum(kept_d, got_d)
        g_down, small = home(total[:width], 0).T, total[width:]
        total = home(whole_sum(kept_u, got_u), 0)
        g_up, g_out = total[:, :hidden], total[:, hidden:].T
        g_qkv = home(g_w[:, 0, :, :three].astype(F32), 1).reshape(heads, share, 3, HEAD_DIM)
        g_q, g_k, g_v = (g_qkv[:, :, i].transpose(1, 0, 2).reshape(share, own_cols) for i in range(3))
        bias_rows = g_w[:, 0, 0:16:8, three:].astype(F32)
        for bit in range(bits):
            small = small + swap(small, "dp", 1 << bit)
            bias_rows = bias_rows + swap(bias_rows, "dp", 1 << bit)
        bias_q, bias_v = bias_rows[:, 0].reshape(own_cols), bias_rows[:, 1].reshape(own_cols)
    count = jnp.sum(seq_lengths).astype(F32) * width
    rms = jnp.sqrt(jnp.sum(small[6:9], axis=-1) / count)
    return (
        layer_out,
        input_grad,
        g_q,
        g_k,
        g_v,
        g_out,
        g_up,
        g_down,
        bias_q,
        bias_v,
        small[0],
        small[9],
        small[1],
        small[2],
        small[3],
        small[4],
        small[5],
        rms,
    )


def solution(mesh):
    in_specs = (
        P(("dp", "tensor"), None),
        P(),
        P("dp", None),
        P("dp", "tensor"),
        P("dp", "tensor"),
        P("dp", "tensor"),
        P("tensor", "dp"),
        P("dp", "tensor"),
        P("tensor", "dp"),
        P("tensor"),
        P("tensor"),
        P(),
        P("tensor"),
        P(),
        P(),
        P(),
        P(),
        P(),
        P(("dp", "tensor"), None),
    )
    out_specs = (
        P(("dp", "tensor"), None),
        P(("dp", "tensor"), None),
        P("dp", "tensor"),
        P("dp", "tensor"),
        P("dp", "tensor"),
        P("tensor", "dp"),
        P("dp", "tensor"),
        P("tensor", "dp"),
        P("tensor"),
        P("tensor"),
        P(),
        P("tensor"),
        P(),
        P(),
        P(),
        P(),
        P(),
        P(),
    )
    return jax.shard_map(body, mesh=mesh, in_specs=in_specs, out_specs=out_specs, check_vma=False)
```

```python
import functools
import itertools
import math

import jax
import jax.numpy as jnp
from jax import lax
from jax.experimental import pallas as pl
from jax.experimental.pallas import tpu as pltpu
from jax.sharding import PartitionSpec as P

HEAD_DIM = 64
LANES = 128
EPSILON = 1e-12
MASKED = -1e30
BF16 = jnp.bfloat16
F32 = jnp.float32
NT = (((1,), (1,)), ((), ()))
TN = (((0,), (0,)), ((), ()))
EXTRA = 16


def dot(left, right):
    return jnp.dot(left, right, preferred_element_type=F32)


def dot_nt(left, right):
    return lax.dot_general(left, right, NT, preferred_element_type=F32)


def dot_tn(left, right):
    return lax.dot_general(left, right, TN, preferred_element_type=F32)


def place_of(mask, height, placed):
    start = (lax.axis_index("dp") ^ mask) * height if placed else 0
    return pl.ds(pl.multiple_of(start, height), height)


def valid_row(positions_ref, lengths_ref, j, rows):
    start = (lax.axis_index("tensor") ^ j) * rows
    own = positions_ref[:, pl.ds(pl.multiple_of(start, rows), rows)]
    return own < lengths_ref[lax.axis_index("dp")]


def in_three(column):
    first = column.astype(BF16)
    rest = column - first.astype(F32)
    second = rest.astype(BF16)
    third = (rest - second.astype(F32)).astype(BF16)
    return first, second, third


def swap(value, axis, bits):
    size = lax.axis_size(axis)
    return lax.ppermute(value, axis, [(i, i ^ bits) for i in range(size)])


def bit_of(axis, bit):
    return (lax.axis_index(axis) >> bit) & 1


def gather_bits(block, axis, order, at):
    done = []
    for bit in order:
        place = at + sum(other > bit for other in done)
        got = swap(block, axis, 1 << bit)
        upper = bit_of(axis, bit) == 1
        low = jnp.where(upper, got, block)
        high = jnp.where(upper, block, got)
        block = jnp.stack([low, high], axis=place)
        done.append(bit)
    return block


def scatter_bits(partial, axis, order, at):
    left = sorted(order, reverse=True)
    for bit in order:
        place = at + left.index(bit)
        mine = bit_of(axis, bit)
        away = lax.dynamic_index_in_dim(partial, 1 - mine, place, keepdims=False)
        keep = lax.dynamic_index_in_dim(partial, mine, place, keepdims=False)
        got = swap(away.astype(BF16), axis, 1 << bit)
        partial = keep.astype(F32) + got.astype(F32)
        left.remove(bit)
    return partial


def after(value, *others):
    return lax.optimization_barrier((value,) + others)[0]


def params(mebibytes=63):
    return pltpu.CompilerParams(vmem_limit_bytes=mebibytes << 20)


def cost(flops, moved, exps=0):
    return pl.CostEstimate(flops=flops, bytes_accessed=moved, transcendentals=exps)


SMEM_SPEC = pl.BlockSpec(memory_space=pltpu.SMEM)
VMEM_SPEC = pl.BlockSpec(memory_space=pltpu.VMEM)
ANY_SPEC = pl.BlockSpec(memory_space=pl.ANY)
HBM_SPEC = pl.BlockSpec(memory_space=pltpu.HBM)


def project_kernel(*refs, masks, heads, placed):
    x_refs, w_refs = refs[:4], refs[4 : 4 + len(masks)]
    bq_ref, bv_ref, positions_ref, lengths_ref, q_out, k_out, v_out, w_s, x_s, m_s, sems = refs[
        4 + len(masks) :
    ]
    rows = x_refs[0].shape[0]
    loads = [pltpu.make_async_copy(x_refs[j], x_s.at[j], sems.at[j]) for j in range(4)]
    for load in loads:
        load.start()
    for ref, entries in zip(w_refs, masks, strict=True):
        for z, mask in enumerate(entries):
            w_s[place_of(mask, ref.shape[1], placed), :] = ref[z]
    lane = lax.broadcasted_iota(jnp.int32, (1, LANES), 1)
    head_lane = lane < HEAD_DIM
    one_q = jnp.where(lane == HEAD_DIM, 1.0, 0.0)
    one_k = jnp.where((lane > HEAD_DIM) & (lane <= HEAD_DIM + 3), 1.0, 0.0)
    one_v = jnp.where((lane >= HEAD_DIM) & (lane < HEAD_DIM + 3), 1.0, 0.0)
    b_query = bq_ref[...].astype(F32)
    bias = jnp.concatenate([b_query, jnp.zeros_like(b_query), bv_ref[...].astype(F32)], axis=1)
    for j in range(4):
        masked = jnp.where(valid_row(positions_ref, lengths_ref, j, rows), 0.0, MASKED)
        m_s[j] = jnp.broadcast_to(masked, (8, rows))
    for load in loads:
        load.wait()

    @pl.loop(0, 4)
    def _(j):
        part = pl.ds(pl.multiple_of(j * rows, rows), rows)
        whole = dot(x_s[j], w_s[...]) + bias
        masked = jnp.broadcast_to(m_s[j, 0:1, :], (LANES, rows)).T

        def columns(group):
            start = group // 2 * LANES
            both = whole[:, start : start + LANES]
            if both.shape[1] < LANES:
                both = jnp.concatenate([both, both], axis=1)
            return pltpu.roll(both, HEAD_DIM, 1) if group % 2 else both

        for h in range(heads):
            query = columns(h).astype(BF16).astype(F32) * (HEAD_DIM**-0.5)
            q_out[h, part, :] = jnp.where(head_lane, query, one_q).astype(BF16)
            key = jnp.where(head_lane, columns(heads + h), one_k)
            k_out[h, part, :] = jnp.where(lane == HEAD_DIM, masked, key).astype(BF16)
            value = jnp.where(head_lane, columns(2 * heads + h), one_v)
            v_out[h, part, :] = value.astype(BF16)


def project(parts, pieces, masks, b_query, b_value, positions, lengths, heads, placed):
    rows, width = parts[0].shape
    seq = 4 * rows
    return pl.pallas_call(
        functools.partial(project_kernel, masks=masks, heads=heads, placed=placed),
        in_specs=[ANY_SPEC] * 4 + [VMEM_SPEC] * (3 + len(pieces)) + [SMEM_SPEC],
        out_specs=[VMEM_SPEC] * 3,
        out_shape=[jax.ShapeDtypeStruct((heads, seq, LANES), BF16)] * 3,
        scratch_shapes=[
            pltpu.VMEM((width, pieces[0].shape[2]), BF16),
            pltpu.VMEM((4, rows, width), BF16),
            pltpu.VMEM((4, 8, rows), F32),
            pltpu.SemaphoreType.DMA((4,)),
        ],
        compiler_params=params(32),
        cost_estimate=cost(1000, 1000),
        name="project",
    )(*parts, *pieces, b_query, b_value, positions, lengths)


def forward_kernel(q_ref, k_ref, v_ref, *refs, unroll):
    q_out, o_out, own, near, far, packed = refs[-6:]
    seq = q_ref.shape[1]
    block = seq // 8
    lane = lax.broadcasted_iota(jnp.int32, (1, LANES), 1)
    head_lane = lane < HEAD_DIM

    def place(i):
        return pl.ds(pl.multiple_of(i * block, block), block)

    def scores_of(i):
        query = q_ref[0, place(i), :]
        scores = dot_nt(query, k_ref[0])
        return query, scores, jnp.max(scores, axis=-1, keepdims=True)

    def attend(i, query, scores, top):
        expon = jnp.exp(scores - top).astype(BF16)
        total = dot(expon, v_ref[0])
        row_sum = total[:, HEAD_DIM : HEAD_DIM + 1]
        out = total * (1.0 / row_sum)
        o_out[0, place(i), :] = out
        one, two, three = in_three(-(top + jnp.log(row_sum)))
        q_out[0, place(i), :] = jnp.where(
            lane == HEAD_DIM + 1,
            one,
            jnp.where(lane == HEAD_DIM + 2, two, jnp.where(lane == HEAD_DIM + 3, three, query)),
        )
        return out

    @pl.loop(0, 8 // unroll)
    def _(step):
        held = scores_of(step * unroll)
        even = None
        for u in range(unroll):
            i = step * unroll + u
            following = scores_of(i + 1) if u < unroll - 1 else None
            out = attend(i, *held)
            if u % 2 == 0:
                even = out
            else:
                pair = jnp.where(head_lane, even, pltpu.roll(out, HEAD_DIM, 1))
                packed[step * (unroll // 2) + u // 2] = pair.astype(BF16)
            held = following

    own[0] = packed[0]
    near[0] = packed[1]
    far[0, 0] = packed[2]
    far[1, 0] = packed[3]


def attention_forward(first, count, q, k, v, before):
    heads, seq, _ = q.shape
    block = seq // 8
    one = pl.BlockSpec((1, seq, LANES), lambda i: (first + i, 0, 0))
    piece = pl.BlockSpec((1, block, LANES), lambda i: (first + i, 0, 0))
    pieces = pl.BlockSpec((2, 1, block, LANES), lambda i: (0, first + i, 0, 0))
    shape = jax.ShapeDtypeStruct
    return pl.pallas_call(
        functools.partial(forward_kernel, unroll=4 if first else 2),
        grid=(count,),
        in_specs=[one] * 3 + [ANY_SPEC] * len(before),
        out_specs=[one, one, piece, piece, pieces],
        out_shape=[shape((heads, seq, LANES), BF16), shape((heads, seq, LANES), F32)]
        + [shape((heads, block, LANES), BF16)] * 2
        + [shape((2, heads, block, LANES), BF16)],
        scratch_shapes=[pltpu.VMEM((4, block, LANES), BF16)],
        input_output_aliases={3 + i: i for i in range(len(before))},
        compiler_params=params(32),
        cost_estimate=cost(1000, 1000),
        name="attention_forward",
    )(q, k, v, *before)


def by_head(w_refs, masks, heads, placed, target):
    for ref, entries in zip(w_refs, masks, strict=True):
        for z, mask in enumerate(entries):
            place = place_of(mask, ref.shape[1], placed)
            for h in range(heads):
                for kind in range(3):
                    start = (kind * heads + h) * HEAD_DIM
                    stop = (h * 3 + kind) * HEAD_DIM
                    target[place, stop : stop + HEAD_DIM] = ref[z, :, start : start + HEAD_DIM]


def through_weights(g_refs, part, w_s):
    three = 3 * HEAD_DIM
    total, h = None, 0
    for ref in g_refs:
        for i in range(ref.shape[0]):
            term = dot_nt(ref[i, part, :], w_s[:, h * three : (h + 1) * three])
            total = term if total is None else total + term
            h += 1
    return total


def backward_kernel(q_ref, k_ref, v_ref, o_ref, *refs, placed, masks, heads):
    d_refs, x_refs = refs[:4], refs[4:8]
    if masks:
        g_ref, gw_ref, *dx_refs, dk_s, dv_s, gw_s, d_s, w_s = refs[-10:]
        by_head(refs[9 : 9 + len(masks)], masks, heads, placed, w_s)
    else:
        g_ref, gw_ref, dk_s, dv_s, gw_s, d_s = refs[-6:]
    seq = q_ref.shape[1]
    block = seq // 8
    rows = seq // 4
    lane = lax.broadcasted_iota(jnp.int32, (1, LANES), 1)
    head_lane = lane < HEAD_DIM
    scale = HEAD_DIM**-0.5
    for j in range(4):
        d_s[j] = d_refs[j][0]
    dk_s[...] = jnp.zeros_like(dk_s)
    dv_s[...] = jnp.zeros_like(dv_s)

    @pl.loop(0, 4)
    def _(j):
        for half in range(2):
            place = pl.ds(pl.multiple_of((2 * j + half) * block, block), block)
            query = q_ref[0, place, :]
            grad = d_s[j].astype(F32)
            if half == 1:
                grad = pltpu.roll(grad, HEAD_DIM, 1)
            grad = jnp.where(head_lane, grad, 0.0)
            delta = jnp.sum(grad * o_ref[0, place, :], axis=-1, keepdims=True)
            one, two, three = in_three(-delta)
            grad = grad.astype(BF16)
            grad_and = jnp.where(
                lane == HEAD_DIM,
                one,
                jnp.where(lane == HEAD_DIM + 1, two, jnp.where(lane == HEAD_DIM + 2, three, grad)),
            )
            probs = jnp.exp(dot_nt(k_ref[0], query))
            lifted = dot_nt(v_ref[0], grad_and)
            grad_scores = (probs * lifted).astype(BF16)
            dv_s[...] += dot(probs.astype(BF16), grad)
            dk_s[...] += dot(grad_scores, query)
            grad_query = dot_tn(grad_scores, k_ref[0]) * scale
            g_ref[0, place, :LANES] = jnp.where(head_lane, grad_query, 0.0).astype(BF16)

    both = jnp.where(head_lane, g_ref[0, :, :LANES].astype(F32), pltpu.roll(dk_s[...], HEAD_DIM, 1))
    g_ref[0, :, :LANES] = both.astype(BF16)
    g_ref[0, :, LANES:] = dv_s[:, :HEAD_DIM].astype(BF16)
    grads = g_ref[0]
    bias = jnp.sum(grads.astype(F32), axis=0, keepdims=True)
    share = gw_ref.shape[2]
    line = lax.broadcasted_iota(jnp.int32, (share, 1), 0)
    side = jnp.where(line < 8, bias[:, :HEAD_DIM], 0.0)
    side = jnp.where((line >= 8) & (line < 16), bias[:, LANES:], side).astype(BF16)
    total = dot_tn(grads[:rows], x_refs[0][...])
    for j in range(1, 4):
        total += dot_tn(grads[j * rows : (j + 1) * rows], x_refs[j][...])
    gw_s[...] = total.T.astype(BF16)
    for i in range(gw_ref.shape[1]):
        gw_ref[0, i, :, : 3 * HEAD_DIM] = gw_s[place_of(i, share, placed), :]
        gw_ref[0, i, :, 3 * HEAD_DIM :] = side
    if masks:
        half = rows // 2
        spread = (3 * rows, 3 * rows + half, 2 * rows)
        for out, start in zip(dx_refs, spread, strict=True):
            count = math.prod(out.shape[:-1])
            total = through_weights((refs[8], g_ref), pl.ds(start, count), w_s)
            out[...] = total.astype(BF16).reshape(out.shape)


def attention_backward(first, count, q, k, v, out, grads, parts, blocks, before, more=()):
    heads, seq, _ = k.shape
    rows, width = parts[0].shape
    one = pl.BlockSpec((1, seq, LANES), lambda i: (first + i, 0, 0))
    piece = pl.BlockSpec((1, seq // 8, LANES), lambda i: (first + i, 0, 0))
    whole = pl.BlockSpec((rows, width), lambda i: (0, 0))
    three = 3 * HEAD_DIM
    share = width // blocks
    shape = jax.ShapeDtypeStruct

    def fixed(array):
        return pl.BlockSpec(array.shape, lambda i: (0,) * len(array.shape))

    others, pieces, masks = more if more else (None, [], ())
    extra = [others, *pieces] if more else []
    dx = [shape((rows // 2, width), BF16)] * 2 + [shape((2, rows // 2, width), BF16)] if more else []
    return pl.pallas_call(
        functools.partial(backward_kernel, placed=blocks > 1, masks=masks, heads=heads),
        grid=(count,),
        in_specs=[one] * 4
        + [piece] * 4
        + [whole] * 4
        + [fixed(array) for array in extra]
        + [ANY_SPEC] * len(before),
        out_specs=[
            pl.BlockSpec((1, seq, three), lambda i: (i, 0, 0)),
            pl.BlockSpec((1, blocks, share, 4 * HEAD_DIM), lambda i: (first + i, 0, 0, 0)),
        ]
        + [fixed(array) for array in dx],
        out_shape=[
            shape((count, seq, three), BF16),
            shape((heads, blocks, share, 4 * HEAD_DIM), BF16),
        ]
        + dx,
        scratch_shapes=[
            pltpu.VMEM((seq, LANES), F32),
            pltpu.VMEM((seq, LANES), F32),
            pltpu.VMEM((width, three), BF16),
            pltpu.VMEM((4, seq // 8, LANES), BF16),
        ]
        + ([pltpu.VMEM((width, heads * three), BF16)] if more else []),
        input_output_aliases={12 + len(extra): 1} if before else {},
        compiler_params=params(),
        cost_estimate=cost(1000, 1000),
        name="attention_backward",
    )(q, k, v, out, *grads, *parts, *extra, *before)


def input_kernel(*refs, masks, which, placed, count, heads):
    g_refs, w_refs = refs[:count], refs[count : count + len(masks)]
    outs, w_s = refs[count + len(masks) : -1], refs[-1]
    by_head(w_refs, masks, heads, placed, w_s)
    for out, (start, size) in zip(outs, which, strict=True):
        out[...] = through_weights(g_refs, pl.ds(start, size), w_s).astype(out.dtype)


def input_part(g_parts, pieces, masks, which, placed):
    heads = sum(part.shape[0] for part in g_parts)
    three = g_parts[0].shape[2]
    width = pieces[0].shape[0] * pieces[0].shape[1] * len(pieces)
    return pl.pallas_call(
        functools.partial(
            input_kernel, masks=masks, which=which, placed=placed, count=len(g_parts), heads=heads
        ),
        in_specs=[VMEM_SPEC] * (len(g_parts) + len(pieces)),
        out_specs=[VMEM_SPEC] * len(which),
        out_shape=[jax.ShapeDtypeStruct((size, width), BF16) for _, size in which],
        scratch_shapes=[pltpu.VMEM((width, heads * three), BF16)],
        compiler_params=params(),
        cost_estimate=cost(1000, 1000),
        name="input_part",
    )(*g_parts, *pieces)


def middle_kernel(*refs, plan, blocks):
    w_refs = refs[: len(plan)]
    refs = refs[len(plan) :]
    own_ref, near_ref, far_ref = refs[:3]
    x_ref, og_ref, positions_ref, lengths_ref, vec_ref = refs[3:8]
    lo_ref, done_ref, sent_d, kept_d, sent_u, kept_u = refs[8:14]
    ga = refs[14:18]
    w1_s, w2_s, att_s, wo_s, hid_s, slope_s, nrm_s, nb_s, n1_s, rs_s, ffn_s = refs[18:29]
    gf_s, gft_s, nbt_s, acc_s, pre_s, g_s, bup_s, mask_s, sums_ref, low_s, two_s, act_s, in_sem, down_sem, up_sem, out_sem, low_sem = refs[29:]
    rows, width = x_ref.shape
    hidden = w2_s.shape[2]
    pieces = 4
    cols = width // pieces
    placed = blocks > 1
    chunk = 128
    share = width // blocks
    half = rows // 2
    b_out, b_down, gain_a, shift_a, gain_f, shift_f = (vec_ref[i : i + 1, :] for i in range(6))

    count = cols // HEAD_DIM
    att = [[own_ref[h] for h in range(count)]]
    for ref, i in ((near_ref, 0), (far_ref, 0), (near_ref, 1)):
        att.append([ref[i, h] for h in range(count)])

    loads = []
    for ref, entries in zip(w_refs, plan, strict=True):
        for index, second, j, row in entries:
            source = ref.at[index]
            target = (w2_s if second else w1_s).at[j].at[place_of(row, source.shape[0], placed)]
            copy = pltpu.make_async_copy(source, target, in_sem.at[len(loads)])
            loads.append((second, copy))
            copy.start()

    def row_loop(work):
        @pl.loop(0, rows // chunk)
        def _(i):
            work(pl.ds(pl.multiple_of(i * chunk, chunk), chunk))

    def add_sum(index, value):
        sums_ref[index : index + 1, :] += jnp.sum(value, axis=0, keepdims=True)

    def mean(value):
        return jnp.mean(value, axis=-1, keepdims=True)

    def normal(value):
        centred = value - mean(value)
        inverse = lax.rsqrt(mean(centred * centred) + EPSILON)
        return centred * inverse, inverse

    def norm_back(grad, unit, inverse, gain):
        scaled = grad * gain
        return (scaled - mean(scaled) - unit * mean(scaled * unit)) * inverse

    sums_ref[...] = jnp.zeros_like(sums_ref)
    own_valid = jnp.where(valid_row(positions_ref, lengths_ref, 0, rows), 1.0, 0.0)
    mask_s[...] = jnp.broadcast_to(own_valid, (LANES, rows)).T
    for j in range(pieces):
        for h in range(cols // HEAD_DIM):
            at = j * cols + h * HEAD_DIM
            att_s[:half, at : at + HEAD_DIM] = att[j][h][:, :HEAD_DIM]
            att_s[half:, at : at + HEAD_DIM] = att[j][h][:, HEAD_DIM:]
    for second, copy in loads:
        if not second:
            copy.wait()
    for j in range(pieces):
        wo_s[:, j * cols : (j + 1) * cols] = w1_s[j, :, hidden : hidden + cols]
        last = w1_s[j, :, hidden + cols - HEAD_DIM :].astype(F32)
        bup_s[j] = last.T[HEAD_DIM : HEAD_DIM + 1, :]
    ffn_s[...] = dot_nt(att_s[...], wo_s[...])

    def first_norm(r):
        value = x_ref[r, :].astype(F32)
        attn = ffn_s[r, :] + b_out
        valid = mask_s[r, :1] > 0.0
        add_sum(6, jnp.where(valid, value * value, 0.0))
        add_sum(7, jnp.where(valid, attn * attn, 0.0))
        unit, inverse = normal(value + attn)
        normed = unit * gain_a + shift_a
        n1_s[r, :] = unit
        rs_s[r, :] = jnp.broadcast_to(inverse, (chunk, LANES))
        nrm_s[r, :] = normed
        nb_s[r, :] = normed.astype(BF16)

    row_loop(first_norm)
    ffn_s[...] = jnp.zeros_like(ffn_s)
    for second, copy in loads:
        if second:
            copy.wait()

    wide = 256
    per = hidden // wide

    def chunk_of(c):
        return c // per, pl.ds(pl.multiple_of(c % per * wide, wide), wide)

    def product_of(c):
        j, at = chunk_of(c)
        return dot(nb_s[...], w1_s[j, :, at]) + bup_s[j, :, at]

    act_s[...] = jnp.zeros_like(act_s)
    two_s[0] = product_of(0)
    count = pieces * per

    @pl.loop(0, count)
    def _(c):
        j, at = chunk_of(c)
        back, behind = chunk_of(jnp.maximum(c - 1, 0))
        now = c % 2
        two_s[1 - now] = product_of(jnp.minimum(c + 1, count - 1))
        ffn_s[...] += dot_nt(act_s[...], w2_s[back, :, behind])
        pre = two_s[now]
        cdf = 0.5 * (1.0 + lax.erf(pre * (0.5**0.5)))
        pdf = jnp.exp(pre * pre * -0.5) * (2.0 * jnp.pi) ** -0.5
        act = (pre * cdf).astype(BF16)
        hid_s[j, :, at] = act
        slope_s[j, :, at] = cdf + pre * pdf
        act_s[...] = act

    ffn_s[...] += dot_nt(act_s[...], w2_s[pieces - 1, :, (per - 1) * wide :])

    def second_norm(r):
        ffn = ffn_s[r, :] + b_down
        valid = mask_s[r, :1] > 0.0
        add_sum(8, jnp.where(valid, ffn * ffn, 0.0))
        unit, inverse = normal(nrm_s[r, :] + ffn)
        lo_ref[r, :] = (unit * gain_f + shift_f).astype(BF16)
        grad = og_ref[r, :].astype(F32)
        add_sum(4, grad * unit)
        add_sum(5, grad)
        d_two = norm_back(grad, unit, inverse, gain_f)
        low = d_two.astype(BF16)
        add_sum(1, low.astype(F32))
        acc_s[r, :] = d_two
        gf_s[r, :] = low

    row_loop(second_norm)
    gft_s[...] = gf_s[...].T
    nbt_s[...] = nb_s[...].T

    places = [place_of(i, share, placed) for i in range(blocks)]

    def copies(j, lanes, target, place, sem, to):
        return [
            pltpu.make_async_copy(
                g_s.at[j].at[places[i], lanes], target.at[place, i, pl.ds(0, share), to], sem.at[j, i]
            )
            for i in range(blocks)
        ]

    lanes_d, lanes_u, lanes_o = (
        pl.ds(0, hidden),
        pl.ds(hidden, hidden),
        pl.ds(2 * hidden, cols),
    )
    to_d, to_u, to_o = pl.ds(0, hidden), pl.ds(0, hidden), pl.ds(hidden, cols)
    def start_all(j, place, lanes, to, sem, targets):
        for away in (1, 0):

            @pl.when(j % 2 == away)
            def _():
                for copy in copies(j, lanes, targets[1 - away], place, sem, to):
                    copy.start()

    @pl.loop(0, pieces)
    def _(step):
        away = 1 - step // (pieces // 2)
        place = step % (pieces // 2)
        j = 2 * place + away
        pre_s[...] = dot(gf_s[...], w2_s[j]) * slope_s[j]
        low = pre_s[...].astype(BF16)
        sums_ref[pl.ds(10 + j, 1), :] = jnp.sum(low.astype(F32), axis=0, keepdims=True)
        g_s[j, :, lanes_d] = dot(gft_s[...], hid_s[j]).astype(BF16)
        start_all(j, place, lanes_d, to_d, down_sem, (sent_d, kept_d))
        g_s[j, :, lanes_u] = dot(nbt_s[...], low).astype(BF16)
        start_all(j, place, lanes_u, to_u, up_sem, (sent_u, kept_u))
        acc_s[...] += dot_nt(low, w1_s[j, :, :hidden])

    def first_back(r):
        grad = acc_s[r, :]
        unit = n1_s[r, :]
        add_sum(2, grad * unit)
        add_sum(3, grad)
        d_one = norm_back(grad, unit, rs_s[r, :1], gain_a)
        low = d_one.astype(BF16)
        add_sum(0, low.astype(F32))
        done_ref[r, :] = d_one
        gf_s[r, :] = low

    row_loop(first_back)
    low = gf_s[...]
    gout = dot_tn(low, att_s[...]).astype(BF16)
    for j in range(pieces):
        g_s[j, :, 2 * hidden : 2 * hidden + cols] = gout[:, j * cols : (j + 1) * cols]
        for copy in copies(j, lanes_o, sent_u if j % 2 else kept_u, j // 2, out_sem, to_o):
            copy.start()
    small = []
    for j in range(pieces):
        low_s[j] = jnp.concatenate([sums_ref[:9], sums_ref[10 + j : 11 + j], sums_ref[9:15]]).astype(BF16)
        target = sent_d if j % 2 else kept_d
        for i in range(blocks):
            under = target.at[j // 2, i, pl.ds(share, EXTRA), :]
            small.append(pltpu.make_async_copy(low_s.at[j], under, low_sem.at[j, i]))
            small[-1].start()
    back = dot(low, wo_s[...]).astype(BF16)
    for j in range(pieces):
        for h in range(cols // HEAD_DIM):
            at = j * cols + h * HEAD_DIM
            ga[j][h, :, :HEAD_DIM] = back[:half, at : at + HEAD_DIM]
            ga[j][h, :, HEAD_DIM:] = back[half:, at : at + HEAD_DIM]
    for j in range(pieces):
        target_d, target_u = (sent_d, sent_u) if j % 2 else (kept_d, kept_u)
        for copy in copies(j, lanes_d, target_d, j // 2, down_sem, to_d):
            copy.wait()
        for copy in copies(j, lanes_u, target_u, j // 2, up_sem, to_u):
            copy.wait()
        for copy in copies(j, lanes_o, target_u, j // 2, out_sem, to_o):
            copy.wait()
    for copy in small:
        copy.wait()


def middle(blocks, weights, plan, att, tokens, out_grad, positions, lengths, vectors, hidden):
    rows, width = tokens.shape
    cols = width // 4
    share = width // blocks
    shape = jax.ShapeDtypeStruct
    vmem = pltpu.VMEM
    loads = sum(len(entries) for entries in plan)
    return pl.pallas_call(
        functools.partial(middle_kernel, plan=plan, blocks=blocks),
        in_specs=[ANY_SPEC] * len(weights) + [VMEM_SPEC] * 6 + [SMEM_SPEC, VMEM_SPEC],
        out_specs=[VMEM_SPEC] * 2 + [ANY_SPEC] * 4 + [VMEM_SPEC] * 4,
        out_shape=[
            shape((rows, width), BF16),
            shape((rows, width), F32),
        ]
        + [shape((2, blocks, share + EXTRA, hidden), BF16)] * 2
        + [shape((2, blocks, share, hidden + cols), BF16)] * 2
        + [shape(att[0].shape, BF16)] * 4,
        scratch_shapes=[
            vmem((4, width, weights[0].shape[-1]), BF16),
            vmem((4, width, hidden), BF16),
            vmem((rows, width), BF16),
            vmem((width, width), BF16),
            vmem((4, rows, hidden), BF16),
            vmem((4, rows, hidden), F32),
            vmem((rows, width), F32),
            vmem((rows, width), BF16),
            vmem((rows, width), F32),
            vmem((rows, LANES), F32),
            vmem((rows, width), F32),
            vmem((rows, width), BF16),
            vmem((width, rows), BF16),
            vmem((width, rows), BF16),
            vmem((rows, width), F32),
            vmem((rows, hidden), F32),
            vmem((4, width, 2 * hidden + cols), BF16),
            vmem((4, 1, hidden), F32),
            vmem((rows, LANES), F32),
            vmem((16, width), F32),
            vmem((4, EXTRA, width), BF16),
            vmem((2, rows, 256), F32),
            vmem((rows, 256), BF16),
            pltpu.SemaphoreType.DMA((loads,)),
            pltpu.SemaphoreType.DMA((4, blocks)),
            pltpu.SemaphoreType.DMA((4, blocks)),
            pltpu.SemaphoreType.DMA((4, blocks)),
            pltpu.SemaphoreType.DMA((4, blocks)),
        ],
        compiler_params=params(),
        cost_estimate=cost(1000, 1000),
        name="middle",
    )(*weights, *att, tokens, out_grad, positions, lengths, vectors)


def reduce_kernel(*refs, jobs, inputs, outputs, terms, extra, extra_in):
    ins = refs[:inputs]
    more = refs[inputs : inputs + extra_in]
    outs = refs[inputs + extra_in : inputs + extra_in + outputs]
    rest = refs[inputs + extra_in + outputs :]
    extra_out = rest[: len(rest) - terms - 1]
    held, sems = rest[len(extra_out) : -1], rest[-1]
    loads = []
    for _, _, _, parts, _ in jobs:
        for source, index, start, size in parts:
            at = len(loads)
            picked = ins[source].at[index + (slice(None), pl.ds(start, size))]
            loads.append(pltpu.make_async_copy(picked, held[at], sems.at[at]))
            loads[-1].start()
    at = 0
    for out, start, lead, parts, base in jobs:
        mine = range(at, at + len(parts))
        at += len(parts)
        for i in mine:
            loads[i].wait()
        size = parts[0][3]
        for index in itertools.product(*map(range, lead)):
            total = held[mine[0]][index].astype(F32)
            for i in mine[1:]:
                total += held[i][index].astype(F32)
            target = outs[out]
            target[base + index + (slice(None), slice(start, start + size))] = total.astype(target.dtype)
    if extra is not None:
        extra(outs, more, extra_out)


class Sum:
    def __init__(self, names, width):
        self.names, self.width, self.terms, self.picks = list(names), width, [], {}

    def join(self, array, start=0, names=None):
        self.terms.append((array, start, list(self.names if names is None else names)))

    def parts(self, picks):
        return [
            (array, tuple(picks.get(name, slice(None)) for name in names), start, self.width)
            for array, start, names in self.terms
        ]

    def away(self, name):
        parts = self.parts({**self.picks, name: 1})
        self.picks[name] = 0
        self.names.remove(name)
        return parts

    def all(self):
        return self.parts(self.picks)


def reduce_call(name, groups, dtype, extra=None, extra_in=(), extra_out=(), keep=True):
    arrays, jobs, shapes, scratch = [], [], [], []
    for out, columns in enumerate(groups):
        start = 0
        stacked = isinstance(columns, tuple)
        for at, parts in enumerate(columns):
            coded = []
            for array, index, first, size in parts:
                known = [i for i, other in enumerate(arrays) if other is array]
                if not known:
                    arrays.append(array)
                coded.append((known[0] if known else len(arrays) - 1, index, first, size))
                sizes = [n for n, i in zip(array.shape, index) if isinstance(i, slice)]
                sizes += [array.shape[-2], size]
                scratch.append(pltpu.VMEM(tuple(sizes), array.dtype))
            jobs.append((out, start, tuple(sizes[:-2]), coded, (at,) if stacked else ()))
            start += 0 if stacked else coded[0][3]
        front = (len(columns),) if stacked else ()
        shapes.append(front + tuple(sizes[:-1]) + (coded[0][3] if stacked else start,))
    outs = [jax.ShapeDtypeStruct(shape, dtype) for shape in shapes]
    held = [] if keep else [pltpu.VMEM(shape, dtype) for shape in shapes]
    result = pl.pallas_call(
        functools.partial(
            reduce_kernel if keep else reduce_inside,
            jobs=jobs,
            inputs=len(arrays),
            outputs=len(outs),
            terms=len(scratch),
            extra=extra,
            extra_in=len(extra_in),
        ),
        in_specs=[HBM_SPEC] * len(arrays) + [VMEM_SPEC] * len(extra_in),
        out_specs=[VMEM_SPEC] * (len(outs) * keep + len(extra_out)),
        out_shape=outs * keep + list(extra_out),
        scratch_shapes=held + scratch + [pltpu.SemaphoreType.DMA((len(scratch),))],
        compiler_params=params(),
        cost_estimate=cost(1000, 1000),
        name=name,
    )(*arrays, *extra_in)
    return result


def reduce_inside(*refs, inputs, extra_in, outputs, terms, **rest):
    front = inputs + extra_in
    results = refs[front : len(refs) - outputs - terms - 1]
    held = refs[len(refs) - outputs - terms - 1 : len(refs) - terms - 1]
    order = refs[:front] + held + results + refs[len(refs) - terms - 1 :]
    reduce_kernel(*order, inputs=inputs, extra_in=extra_in, outputs=outputs, terms=terms, **rest)


def body(
    tokens,
    seq_lengths,
    positions,
    w_query,
    w_key,
    w_value,
    w_out,
    w_up,
    w_down,
    b_query,
    b_value,
    b_out,
    b_up,
    b_down,
    gain_attn,
    shift_attn,
    gain_ffn,
    shift_ffn,
    out_grad,
):
    group = lax.axis_index("dp")
    member = lax.axis_index("tensor")
    dp_count = lax.axis_size("dp")
    bits = dp_count.bit_length() - 1
    rows, width = tokens.shape
    own_cols = w_query.shape[1]
    heads = own_cols // HEAD_DIM
    share = w_query.shape[0]
    hidden = w_up.shape[1]
    placed = share % 16 == 0 and bits == 3 and heads == 3
    blocks = dp_count if placed else 1
    def core(value):
        return swap(value, "tensor", 1)

    def cross(value):
        return swap(value, "tensor", 2)

    def grow(value, got, masks, bit):
        both = jnp.stack([value, got], axis=1).reshape((-1,) + value.shape[1:])
        return both, [m ^ b for m in masks for b in (0, bit)]

    across = cross(tokens)
    beside = core(tokens)
    own_qkv = jnp.concatenate([w_query, w_key, w_value], axis=1)[None]
    own_b_up = lax.dynamic_slice_in_dim(b_up, group * share, share, 0)[:, None]
    spare = -(hidden + own_cols) % LANES
    one = jnp.concatenate([w_up, w_out.T, jnp.broadcast_to(own_b_up, (share, spare))], axis=1)[None]
    two = w_down.T[None]
    biases = [b_query.reshape(1, -1), b_value.reshape(1, -1)]
    vectors = [b_out, b_down, gain_attn, shift_attn, gain_ffn, shift_ffn]
    vectors = jnp.stack([vec.astype(F32) for vec in vectors] + [jnp.zeros((width,), F32)] * 2)

    if placed:
        got_w = after(swap(own_qkv, "dp", 4), one, two)
        w_part, w_mask = grow(own_qkv, got_w, [0], 4)
        one = after(one, w_part)
        got_w, got_one, across = after((swap(w_part, "dp", 2), swap(one, "dp", 4), across), w_part)
        w_part, w_mask = grow(w_part, got_w, w_mask, 2)
        one, one_mask = grow(one, got_one, [0], 4)

        two = after(two, across)
        round_three = (swap(w_part, "dp", 1), swap(one, "dp", 2), cross(two), core(across))
        round_three = after((round_three, biases, vectors), w_part)
        (got_w, got_one, got_two, beyond), biases, vectors = round_three
        w_qkv, w_masks = [w_part, got_w], [w_mask, [m ^ 1 for m in w_mask]]
        one, one_mask = grow(one, got_one, one_mask, 2)
        two = jnp.stack([two, got_two], axis=1)
        parts = [tokens, beside, across, beyond]

        round_four = (swap(two, "dp", 4), swap(one, "dp", 1), cross(one), core(one))
        positions = after(positions, one, two)
        q, k, v = project(parts, w_qkv, w_masks, *biases, positions, seq_lengths, heads, placed)
        kept = attention_forward(0, 1, q, k, v, [])
        q_kept = kept[0]
        got_two, odd, even_far, even_near = after(round_four, q_kept)
        two, two_mask = grow(two, got_two, [0], 4)

        round_five = (swap(two, "dp", 2), cross(odd), swap(two, "dp", 1), core(even_far))
        kept, odd, two, even_far = after((kept, odd, two, even_far), q_kept)
        q_kept, out, *packed = attention_forward(1, 2, q, k, v, kept)
        kept = [q_kept, out]
        two_late, odd_far, two_odd, both_near = after(round_five, q_kept)

        far_odd = [m ^ 1 for m in one_mask]
        two_mask_odd = [m ^ 1 for m in two_mask]
        late_mask, last_mask = [m ^ 2 for m in two_mask], [m ^ 3 for m in two_mask]
        two_last = swap(two_late, "dp", 1)
        att_far = cross(packed[2])
        odd, two = after((odd, two), two_late)
        two_near, odd_near = core(two), core(odd)
        odd_far, two_late, two_odd = after((odd_far, two_late, two_odd), two_near, odd_near)
        odd_far_near, late_near, two_odd_near = core(odd_far), core(two_late), core(two_odd)
        two_last, att_far = after((two_last, att_far), odd_far_near, late_near, two_odd_near)
        att_near = core(jnp.stack([packed[1], att_far[1]]))
        ones = [(one, one_mask), (odd, far_odd), (even_far, one_mask), (odd_far, far_odd)]
        twos = [(two, two_mask), (two_odd, two_mask_odd), (two_late, late_mask), (two_last, last_mask)]
        early = [even_near, odd_near, both_near, odd_far_near, two_near, two_odd_near, late_near]
        early.append(core(two_last))
    else:
        w_qkv = [gather_bits(own_qkv[0], "dp", range(bits), 0).reshape(1, width, -1)]
        w_masks = [[0]]
        one = gather_bits(one[0], "dp", range(bits), 0).reshape(1, width, -1)
        two = gather_bits(two[0], "dp", range(bits), 0).reshape(1, width, -1)
        parts = [tokens, beside, across, core(across)]
        q, k, v = project(parts, w_qkv, w_masks, *biases, positions, seq_lengths, heads, placed)
        q_kept, out, *packed = attention_forward(0, heads, q, k, v, [])
        kept = [q_kept, out]
        ones = [(one, [0]), (cross(one), [0])]
        twos = [(jnp.stack([two, cross(two)], axis=1), [0])]
        early = [core(array) for array, _ in ones + twos]
        att_far = cross(packed[2])
        att_near = core(jnp.stack([packed[1], att_far[1]]))
    att = [packed[0], att_near, att_far]
    weights = [array for array, _ in ones + twos] + early
    plan = []
    for near in range(2):
        for a, (_, masks) in enumerate(ones):
            far = a // (len(ones) // 2)
            plan.append([((z,), False, near + 2 * far, mask) for z, mask in enumerate(masks)])
        for _, masks in twos:
            plan.append(
                [
                    ((z, far), True, near + 2 * far, mask)
                    for z, mask in enumerate(masks)
                    for far in range(2)
                ]
            )
    layer_out, d_one, sent_d, kept_d, sent_u, kept_u, *back = middle(
        blocks, weights, plan, att, tokens, out_grad, positions, seq_lengths, vectors, hidden
    )
    grads = [back[0]] + [swap(back[j], "tensor", j) for j in (1, 2, 3)]

    def add(*terms):
        total = terms[0].astype(F32)
        for term in terms[1:]:
            total = total + term.astype(F32)
        return total

    def send(away, name):
        return cross(away) if name == "x" else swap(away, "dp", 1 << name)

    def axes_of(array, lead):
        return array.reshape(array.shape[:lead] + (2,) * bits + array.shape[lead + 1 :])

    names = list(range(bits))[::-1]
    late = list(range(1, bits))
    shape = jax.ShapeDtypeStruct
    three = 3 * HEAD_DIM

    got_d, got_u = core(sent_d), core(sent_u)
    if placed:
        down, up = Sum(["x"] + names, hidden), Sum(["x"] + names, hidden + own_cols)
        for total, arrays in ((down, (kept_d, got_d)), (up, (kept_u, got_u))):
            for array in arrays:
                total.join(axes_of(array, 1))
        move_d, move_u = reduce_call("sum_first", [[down.away("x")], [up.away(0)]], BF16)
        move_d, move_u = after((move_d, move_u), grads)
        grads = after(grads, move_d)
        down_names, up_names = ["x"] + late + [0], [0, "x"] + late
    q_kept, out = kept
    if placed:
        before = attention_backward(0, heads - 1, q_kept, k, v, out, grads, parts, blocks, [])
        last = before[0]
        down.join(after(send(move_d, down_names.pop(0)), last))
        up.join(after(send(move_u, up_names.pop(0)), last))
        groups = [[down.away(down_names[0])], [up.away(up_names[0])]]
        move_d, move_u = reduce_call("sum_second", groups, BF16)
        q_kept = after(q_kept, move_d)
        more = (before[0], w_qkv, w_masks)
        g_last, g_w, *first = attention_backward(
            heads - 1, 1, q_kept, k, v, out, grads, parts, blocks, before[1:], more
        )
        g_parts = [before[0], g_last]
    else:
        g_all, g_w = attention_backward(0, heads, q_kept, k, v, out, grads, parts, blocks, [])
    if placed:
        down.join(after(send(move_d, down_names.pop(0)), g_last))
        up.join(after(send(move_u, up_names.pop(0)), g_last))
        got_part = [core(part) for part in first[:2]]
    half = rows // 2
    own_parts = ((rows, half), (rows + half, half), (0, rows))
    if placed:
        qkv = Sum(["h"] + names, 4 * HEAD_DIM)
        qkv.join(axes_of(g_w, 1))
        groups = [[down.away(down_names[0])], [up.away(up_names[0])], [qkv.away(0)]]
        groups.append(tuple([(first[2], (i,), 0, width), (got_part[i], (), 0, width)] for i in range(2)))
        move_d, move_u, move_qkv, crossed = reduce_call("sum_third", groups, BF16)
        crossed = cross(crossed)
        g_parts = after(g_parts, move_d)
        second = input_part(g_parts, w_qkv, w_masks, own_parts, placed)
        near = [core(part) for part in second[:2]]
        down.join(after(send(move_d, down_names.pop(0)), *second))
        up.join(after(send(move_u, up_names.pop(0)), *second))
        qkv.join(after(send(move_qkv, 0), *second))
        crossed = after(crossed, *second)
        others = list(itertools.product(range(2), repeat=len(late)))[1:]
        groups = [[down.away(down_names[0])], [up.away(up_names[0])]]
        groups += [[qkv.parts({**qkv.picks, **dict(zip(late, pick))})] for pick in others]
        move_d, move_u, *moves_qkv = reduce_call("sum_fourth", groups, BF16)
        down.join(send(move_d, down_names.pop(0)))
        got_u = send(move_u, up_names.pop(0))
        gots_qkv = [
            swap(move, "dp", sum(bit << name for bit, name in zip(pick, late)))
            for move, pick in zip(moves_qkv, others)
        ]
        qkv.picks.update(dict.fromkeys(late, 0))
        for name in late:
            qkv.names.remove(name)

        def finish_down(totals, ins, outs):
            outs[0][...] = totals[0][:share]
            outs[1][...] = totals[0][share:]
            for i in range(2):
                part = pl.ds(i * half, half)
                total = ins[0][part, :]
                for term in (ins[1][part, :], ins[2][i], ins[3 + i][...]):
                    total += term.astype(F32)
                outs[2][part, :] = total.astype(BF16)

        g_down, small, input_grad = reduce_call(
            "finish_down",
            [[down.all()]],
            F32,
            finish_down,
            (d_one, second[2], crossed, *near),
            (
                shape((share, hidden), F32),
                shape((EXTRA, width), F32),
                shape((rows, width), BF16),
            ),
            keep=False,
        )
        g_down = g_down.T
        got_u, gots_qkv = after((got_u, gots_qkv), small)
        up.join(got_u)
        for got in gots_qkv:
            qkv.join(got)
    else:
        first = input_part([g_all], w_qkv, w_masks, ((3 * rows, rows), (2 * rows, rows)), placed)
        crossed = cross(add(first[1], core(first[0])).astype(BF16))
        second = input_part([g_all], w_qkv, w_masks, own_parts, placed)
        near = jnp.concatenate([core(part) for part in second[:2]])

    if placed:

        def finish(totals, _, outs):
            g_up, g_qkv = totals
            q_out, k_out, v_out, o_out, up_out, bq_out, bv_out = outs
            for h in range(heads):
                at = pl.ds(h * HEAD_DIM, HEAD_DIM)
                for kind, out in enumerate((q_out, k_out, v_out)):
                    out[:, at] = g_qkv[h, :, kind * HEAD_DIM : (kind + 1) * HEAD_DIM]
                bq_out[:, at] = g_qkv[h, 0:1, three:]
                bv_out[:, at] = g_qkv[h, 8:9, three:]
            up_out[...] = g_up[:, :hidden]
            o_out[...] = g_up[:, hidden:].T

        g_q, g_k, g_v, g_out, g_up, bias_q, bias_v = reduce_call(
            "finish",
            [[up.all()], [qkv.all()]],
            F32,
            finish,
            (),
            (
                [shape((share, own_cols), F32)] * 3
                + [shape((own_cols, share), F32), shape((share, hidden), F32)]
                + [shape((1, own_cols), F32)] * 2
            ),
            keep=False,
        )
        bias_q, bias_v = bias_q[0], bias_v[0]
    else:
        input_grad = add(d_one, second[2], near, crossed).astype(BF16)
        two_s = (2,) * bits

        def whole_sum(mine, got):
            total = add(mine, got)
            return total[0, 0] + cross(total[1, 0].astype(BF16)).astype(F32)

        def home(total, lead):
            shaped = total.reshape(total.shape[:lead] + two_s + (share, total.shape[-1]))
            return scatter_bits(shaped, "dp", range(bits), lead)

        total = whole_sum(kept_d, got_d)
        g_down, small = home(total[:width], 0).T, total[width:]
        total = home(whole_sum(kept_u, got_u), 0)
        g_up, g_out = total[:, :hidden], total[:, hidden:].T
        g_qkv = home(g_w[:, 0, :, :three].astype(F32), 1).reshape(heads, share, 3, HEAD_DIM)
        g_q, g_k, g_v = (g_qkv[:, :, i].transpose(1, 0, 2).reshape(share, own_cols) for i in range(3))
        bias_rows = g_w[:, 0, 0:16:8, three:].astype(F32)
        for bit in range(bits):
            small = small + swap(small, "dp", 1 << bit)
            bias_rows = bias_rows + swap(bias_rows, "dp", 1 << bit)
        bias_q, bias_v = bias_rows[:, 0].reshape(own_cols), bias_rows[:, 1].reshape(own_cols)
    count = jnp.sum(seq_lengths).astype(F32) * width
    rms = jnp.sqrt(jnp.sum(small[6:9], axis=-1) / count)
    return (
        layer_out,
        input_grad,
        g_q,
        g_k,
        g_v,
        g_out,
        g_up,
        g_down,
        bias_q,
        bias_v,
        small[0],
        small[9],
        small[1],
        small[2],
        small[3],
        small[4],
        small[5],
        rms,
    )


def solution(mesh):
    in_specs = (
        P(("dp", "tensor"), None),
        P(),
        P("dp", None),
        P("dp", "tensor"),
        P("dp", "tensor"),
        P("dp", "tensor"),
        P("tensor", "dp"),
        P("dp", "tensor"),
        P("tensor", "dp"),
        P("tensor"),
        P("tensor"),
        P(),
        P("tensor"),
        P(),
        P(),
        P(),
        P(),
        P(),
        P(("dp", "tensor"), None),
    )
    out_specs = (
        P(("dp", "tensor"), None),
        P(("dp", "tensor"), None),
        P("dp", "tensor"),
        P("dp", "tensor"),
        P("dp", "tensor"),
        P("tensor", "dp"),
        P("dp", "tensor"),
        P("tensor", "dp"),
        P("tensor"),
        P("tensor"),
        P(),
        P("tensor"),
        P(),
        P(),
        P(),
        P(),
        P(),
        P(),
    )
    return jax.shard_map(body, mesh=mesh, in_specs=in_specs, out_specs=out_specs, check_vma=False)
```

```python
import functools
import itertools
import math

import jax
import jax.numpy as jnp
from jax import lax
from jax.experimental import pallas as pl
from jax.experimental.pallas import tpu as pltpu
from jax.sharding import PartitionSpec as P

HEAD_DIM = 64
LANES = 128
EPSILON = 1e-12
MASKED = -1e30
BF16 = jnp.bfloat16
F32 = jnp.float32
NT = (((1,), (1,)), ((), ()))
TN = (((0,), (0,)), ((), ()))
EXTRA = 16


def dot(left, right):
    return jnp.dot(left, right, preferred_element_type=F32)


def dot_nt(left, right):
    return lax.dot_general(left, right, NT, preferred_element_type=F32)


def dot_tn(left, right):
    return lax.dot_general(left, right, TN, preferred_element_type=F32)


def place_of(mask, height, placed):
    start = (lax.axis_index("dp") ^ mask) * height if placed else 0
    return pl.ds(pl.multiple_of(start, height), height)


def valid_row(positions_ref, lengths_ref, j, rows):
    start = (lax.axis_index("tensor") ^ j) * rows
    own = positions_ref[:, pl.ds(pl.multiple_of(start, rows), rows)]
    return own < lengths_ref[lax.axis_index("dp")]


def in_three(column):
    first = column.astype(BF16)
    rest = column - first.astype(F32)
    second = rest.astype(BF16)
    third = (rest - second.astype(F32)).astype(BF16)
    return first, second, third


def swap(value, axis, bits):
    size = lax.axis_size(axis)
    return lax.ppermute(value, axis, [(i, i ^ bits) for i in range(size)])


def bit_of(axis, bit):
    return (lax.axis_index(axis) >> bit) & 1


def gather_bits(block, axis, order, at):
    done = []
    for bit in order:
        place = at + sum(other > bit for other in done)
        got = swap(block, axis, 1 << bit)
        upper = bit_of(axis, bit) == 1
        low = jnp.where(upper, got, block)
        high = jnp.where(upper, block, got)
        block = jnp.stack([low, high], axis=place)
        done.append(bit)
    return block


def scatter_bits(partial, axis, order, at):
    left = sorted(order, reverse=True)
    for bit in order:
        place = at + left.index(bit)
        mine = bit_of(axis, bit)
        away = lax.dynamic_index_in_dim(partial, 1 - mine, place, keepdims=False)
        keep = lax.dynamic_index_in_dim(partial, mine, place, keepdims=False)
        got = swap(away.astype(BF16), axis, 1 << bit)
        partial = keep.astype(F32) + got.astype(F32)
        left.remove(bit)
    return partial


def after(value, *others):
    return lax.optimization_barrier((value,) + others)[0]


def params(mebibytes=63):
    return pltpu.CompilerParams(vmem_limit_bytes=mebibytes << 20)


def cost(flops, moved, exps=0):
    return pl.CostEstimate(flops=flops, bytes_accessed=moved, transcendentals=exps)


SMEM_SPEC = pl.BlockSpec(memory_space=pltpu.SMEM)
VMEM_SPEC = pl.BlockSpec(memory_space=pltpu.VMEM)
ANY_SPEC = pl.BlockSpec(memory_space=pl.ANY)
HBM_SPEC = pl.BlockSpec(memory_space=pltpu.HBM)


def project_kernel(*refs, masks, heads, placed):
    x_refs, w_refs = refs[:4], refs[4 : 4 + len(masks)]
    bq_ref, bv_ref, positions_ref, lengths_ref, q_out, k_out, v_out, w_s, x_s, m_s, sems = refs[
        4 + len(masks) :
    ]
    rows = x_refs[0].shape[0]
    loads = [pltpu.make_async_copy(x_refs[j], x_s.at[j], sems.at[j]) for j in range(4)]
    for load in loads:
        load.start()
    for ref, entries in zip(w_refs, masks, strict=True):
        for z, mask in enumerate(entries):
            w_s[place_of(mask, ref.shape[1], placed), :] = ref[z]
    lane = lax.broadcasted_iota(jnp.int32, (1, LANES), 1)
    head_lane = lane < HEAD_DIM
    one_q = jnp.where(lane == HEAD_DIM, 1.0, 0.0)
    one_k = jnp.where((lane > HEAD_DIM) & (lane <= HEAD_DIM + 3), 1.0, 0.0)
    one_v = jnp.where((lane >= HEAD_DIM) & (lane < HEAD_DIM + 3), 1.0, 0.0)
    b_query = bq_ref[...].astype(F32)
    bias = jnp.concatenate([b_query, jnp.zeros_like(b_query), bv_ref[...].astype(F32)], axis=1)
    for j in range(4):
        masked = jnp.where(valid_row(positions_ref, lengths_ref, j, rows), 0.0, MASKED)
        m_s[j] = jnp.broadcast_to(masked, (8, rows))
    for load in loads:
        load.wait()

    @pl.loop(0, 4)
    def _(j):
        part = pl.ds(pl.multiple_of(j * rows, rows), rows)
        whole = dot(x_s[j], w_s[...]) + bias
        masked = jnp.broadcast_to(m_s[j, 0:1, :], (LANES, rows)).T

        def columns(group):
            start = group // 2 * LANES
            both = whole[:, start : start + LANES]
            if both.shape[1] < LANES:
                both = jnp.concatenate([both, both], axis=1)
            return pltpu.roll(both, HEAD_DIM, 1) if group % 2 else both

        for h in range(heads):
            query = columns(h).astype(BF16).astype(F32) * (HEAD_DIM**-0.5)
            q_out[h, part, :] = jnp.where(head_lane, query, one_q).astype(BF16)
            key = jnp.where(head_lane, columns(heads + h), one_k)
            k_out[h, part, :] = jnp.where(lane == HEAD_DIM, masked, key).astype(BF16)
            value = jnp.where(head_lane, columns(2 * heads + h), one_v)
            v_out[h, part, :] = value.astype(BF16)


def project(parts, pieces, masks, b_query, b_value, positions, lengths, heads, placed):
    rows, width = parts[0].shape
    seq = 4 * rows
    return pl.pallas_call(
        functools.partial(project_kernel, masks=masks, heads=heads, placed=placed),
        in_specs=[ANY_SPEC] * 4 + [VMEM_SPEC] * (3 + len(pieces)) + [SMEM_SPEC],
        out_specs=[VMEM_SPEC] * 3,
        out_shape=[jax.ShapeDtypeStruct((heads, seq, LANES), BF16)] * 3,
        scratch_shapes=[
            pltpu.VMEM((width, pieces[0].shape[2]), BF16),
            pltpu.VMEM((4, rows, width), BF16),
            pltpu.VMEM((4, 8, rows), F32),
            pltpu.SemaphoreType.DMA((4,)),
        ],
        compiler_params=params(32),
        cost_estimate=cost(1000, 1000),
        name="project",
    )(*parts, *pieces, b_query, b_value, positions, lengths)


def forward_kernel(q_ref, k_ref, v_ref, *refs, unroll):
    q_out, o_out, own, near, far, packed = refs[-6:]
    seq = q_ref.shape[1]
    block = seq // 8
    lane = lax.broadcasted_iota(jnp.int32, (1, LANES), 1)
    head_lane = lane < HEAD_DIM

    def place(i):
        return pl.ds(pl.multiple_of(i * block, block), block)

    def scores_of(i):
        query = q_ref[0, place(i), :]
        scores = dot_nt(query, k_ref[0])
        return query, scores, jnp.max(scores, axis=-1, keepdims=True)

    def attend(i, query, scores, top):
        expon = jnp.exp(scores - top).astype(BF16)
        total = dot(expon, v_ref[0])
        row_sum = total[:, HEAD_DIM : HEAD_DIM + 1]
        out = total * (1.0 / row_sum)
        o_out[0, place(i), :] = out
        one, two, three = in_three(-(top + jnp.log(row_sum)))
        q_out[0, place(i), :] = jnp.where(
            lane == HEAD_DIM + 1,
            one,
            jnp.where(lane == HEAD_DIM + 2, two, jnp.where(lane == HEAD_DIM + 3, three, query)),
        )
        return out

    @pl.loop(0, 8 // unroll)
    def _(step):
        held = scores_of(step * unroll)
        even = None
        for u in range(unroll):
            i = step * unroll + u
            following = scores_of(i + 1) if u < unroll - 1 else None
            out = attend(i, *held)
            if u % 2 == 0:
                even = out
            else:
                pair = jnp.where(head_lane, even, pltpu.roll(out, HEAD_DIM, 1))
                packed[step * (unroll // 2) + u // 2] = pair.astype(BF16)
            held = following

    own[0] = packed[0]
    near[0] = packed[1]
    far[0, 0] = packed[2]
    far[1, 0] = packed[3]


def attention_forward(first, count, q, k, v, before):
    heads, seq, _ = q.shape
    block = seq // 8
    one = pl.BlockSpec((1, seq, LANES), lambda i: (first + i, 0, 0))
    piece = pl.BlockSpec((1, block, LANES), lambda i: (first + i, 0, 0))
    pieces = pl.BlockSpec((2, 1, block, LANES), lambda i: (0, first + i, 0, 0))
    shape = jax.ShapeDtypeStruct
    return pl.pallas_call(
        functools.partial(forward_kernel, unroll=4 if first else 2),
        grid=(count,),
        in_specs=[one] * 3 + [ANY_SPEC] * len(before),
        out_specs=[one, one, piece, piece, pieces],
        out_shape=[shape((heads, seq, LANES), BF16), shape((heads, seq, LANES), F32)]
        + [shape((heads, block, LANES), BF16)] * 2
        + [shape((2, heads, block, LANES), BF16)],
        scratch_shapes=[pltpu.VMEM((4, block, LANES), BF16)],
        input_output_aliases={3 + i: i for i in range(len(before))},
        compiler_params=params(32),
        cost_estimate=cost(1000, 1000),
        name="attention_forward",
    )(q, k, v, *before)


def by_head(w_refs, masks, heads, placed, target):
    for ref, entries in zip(w_refs, masks, strict=True):
        for z, mask in enumerate(entries):
            place = place_of(mask, ref.shape[1], placed)
            for h in range(heads):
                for kind in range(3):
                    start = (kind * heads + h) * HEAD_DIM
                    stop = (h * 3 + kind) * HEAD_DIM
                    target[place, stop : stop + HEAD_DIM] = ref[z, :, start : start + HEAD_DIM]


def through_weights(g_refs, part, w_s):
    three = 3 * HEAD_DIM
    total, h = None, 0
    for ref in g_refs:
        for i in range(ref.shape[0]):
            term = dot_nt(ref[i, part, :], w_s[:, h * three : (h + 1) * three])
            total = term if total is None else total + term
            h += 1
    return total


def backward_kernel(q_ref, k_ref, v_ref, o_ref, *refs, placed, masks, heads):
    d_refs, x_refs = refs[:4], refs[4:8]
    if masks:
        g_ref, gw_ref, *dx_refs, dk_s, dv_s, gw_s, d_s, w_s = refs[-10:]
        by_head(refs[9 : 9 + len(masks)], masks, heads, placed, w_s)
    else:
        g_ref, gw_ref, dk_s, dv_s, gw_s, d_s = refs[-6:]
    seq = q_ref.shape[1]
    block = seq // 8
    rows = seq // 4
    lane = lax.broadcasted_iota(jnp.int32, (1, LANES), 1)
    head_lane = lane < HEAD_DIM
    scale = HEAD_DIM**-0.5
    for j in range(4):
        d_s[j] = d_refs[j][0]
    dk_s[...] = jnp.zeros_like(dk_s)
    dv_s[...] = jnp.zeros_like(dv_s)

    @pl.loop(0, 4)
    def _(j):
        for half in range(2):
            place = pl.ds(pl.multiple_of((2 * j + half) * block, block), block)
            query = q_ref[0, place, :]
            grad = d_s[j].astype(F32)
            if half == 1:
                grad = pltpu.roll(grad, HEAD_DIM, 1)
            grad = jnp.where(head_lane, grad, 0.0)
            delta = jnp.sum(grad * o_ref[0, place, :], axis=-1, keepdims=True)
            one, two, three = in_three(-delta)
            grad = grad.astype(BF16)
            grad_and = jnp.where(
                lane == HEAD_DIM,
                one,
                jnp.where(lane == HEAD_DIM + 1, two, jnp.where(lane == HEAD_DIM + 2, three, grad)),
            )
            probs = jnp.exp(dot_nt(k_ref[0], query))
            lifted = dot_nt(v_ref[0], grad_and)
            grad_scores = (probs * lifted).astype(BF16)
            dv_s[...] += dot(probs.astype(BF16), grad)
            dk_s[...] += dot(grad_scores, query)
            grad_query = dot_tn(grad_scores, k_ref[0]) * scale
            g_ref[0, place, :LANES] = jnp.where(head_lane, grad_query, 0.0).astype(BF16)

    both = jnp.where(head_lane, g_ref[0, :, :LANES].astype(F32), pltpu.roll(dk_s[...], HEAD_DIM, 1))
    g_ref[0, :, :LANES] = both.astype(BF16)
    g_ref[0, :, LANES:] = dv_s[:, :HEAD_DIM].astype(BF16)
    grads = g_ref[0]
    bias = jnp.sum(grads.astype(F32), axis=0, keepdims=True)
    share = gw_ref.shape[2]
    line = lax.broadcasted_iota(jnp.int32, (share, 1), 0)
    side = jnp.where(line < 8, bias[:, :HEAD_DIM], 0.0)
    side = jnp.where((line >= 8) & (line < 16), bias[:, LANES:], side).astype(BF16)
    total = dot_tn(grads[:rows], x_refs[0][...])
    for j in range(1, 4):
        total += dot_tn(grads[j * rows : (j + 1) * rows], x_refs[j][...])
    gw_s[...] = total.T.astype(BF16)
    for i in range(gw_ref.shape[1]):
        gw_ref[0, i, :, : 3 * HEAD_DIM] = gw_s[place_of(i, share, placed), :]
        gw_ref[0, i, :, 3 * HEAD_DIM :] = side
    if masks:
        half = rows // 2
        spread = (3 * rows, 3 * rows + half, 2 * rows)
        for out, start in zip(dx_refs, spread, strict=True):
            count = math.prod(out.shape[:-1])
            total = through_weights((refs[8], g_ref), pl.ds(start, count), w_s)
            out[...] = total.astype(BF16).reshape(out.shape)


def attention_backward(first, count, q, k, v, out, grads, parts, blocks, before, more=()):
    heads, seq, _ = k.shape
    rows, width = parts[0].shape
    one = pl.BlockSpec((1, seq, LANES), lambda i: (first + i, 0, 0))
    piece = pl.BlockSpec((1, seq // 8, LANES), lambda i: (first + i, 0, 0))
    whole = pl.BlockSpec((rows, width), lambda i: (0, 0))
    three = 3 * HEAD_DIM
    share = width // blocks
    shape = jax.ShapeDtypeStruct

    def fixed(array):
        return pl.BlockSpec(array.shape, lambda i: (0,) * len(array.shape))

    others, pieces, masks = more if more else (None, [], ())
    extra = [others, *pieces] if more else []
    dx = [shape((rows // 2, width), BF16)] * 2 + [shape((2, rows // 2, width), BF16)] if more else []
    return pl.pallas_call(
        functools.partial(backward_kernel, placed=blocks > 1, masks=masks, heads=heads),
        grid=(count,),
        in_specs=[one] * 4
        + [piece] * 4
        + [whole] * 4
        + [fixed(array) for array in extra]
        + [ANY_SPEC] * len(before),
        out_specs=[
            pl.BlockSpec((1, seq, three), lambda i: (i, 0, 0)),
            pl.BlockSpec((1, blocks, share, 4 * HEAD_DIM), lambda i: (first + i, 0, 0, 0)),
        ]
        + [fixed(array) for array in dx],
        out_shape=[
            shape((count, seq, three), BF16),
            shape((heads, blocks, share, 4 * HEAD_DIM), BF16),
        ]
        + dx,
        scratch_shapes=[
            pltpu.VMEM((seq, LANES), F32),
            pltpu.VMEM((seq, LANES), F32),
            pltpu.VMEM((width, three), BF16),
            pltpu.VMEM((4, seq // 8, LANES), BF16),
        ]
        + ([pltpu.VMEM((width, heads * three), BF16)] if more else []),
        input_output_aliases={12 + len(extra): 1} if before else {},
        compiler_params=params(),
        cost_estimate=cost(1000, 1000),
        name="attention_backward",
    )(q, k, v, out, *grads, *parts, *extra, *before)


def input_kernel(*refs, masks, which, placed, count, heads):
    g_refs, w_refs = refs[:count], refs[count : count + len(masks)]
    outs, w_s = refs[count + len(masks) : -1], refs[-1]
    by_head(w_refs, masks, heads, placed, w_s)
    for out, (start, size) in zip(outs, which, strict=True):
        out[...] = through_weights(g_refs, pl.ds(start, size), w_s).astype(out.dtype)


def input_part(g_parts, pieces, masks, which, placed):
    heads = sum(part.shape[0] for part in g_parts)
    three = g_parts[0].shape[2]
    width = pieces[0].shape[0] * pieces[0].shape[1] * len(pieces)
    return pl.pallas_call(
        functools.partial(
            input_kernel, masks=masks, which=which, placed=placed, count=len(g_parts), heads=heads
        ),
        in_specs=[VMEM_SPEC] * (len(g_parts) + len(pieces)),
        out_specs=[VMEM_SPEC] * len(which),
        out_shape=[jax.ShapeDtypeStruct((size, width), BF16) for _, size in which],
        scratch_shapes=[pltpu.VMEM((width, heads * three), BF16)],
        compiler_params=params(),
        cost_estimate=cost(1000, 1000),
        name="input_part",
    )(*g_parts, *pieces)


def middle_kernel(*refs, plan, blocks):
    w_refs = refs[: len(plan)]
    refs = refs[len(plan) :]
    own_ref, near_ref, far_ref = refs[:3]
    x_ref, og_ref, positions_ref, lengths_ref, vec_ref = refs[3:8]
    lo_ref, done_ref, sent_d, kept_d, sent_u, kept_u = refs[8:14]
    ga = refs[14:18]
    w1_s, w2_s, att_s, wo_s, hid_s, slope_s, nrm_s, nb_s, n1_s, rs_s, ffn_s = refs[18:29]
    gf_s, gft_s, nbt_s, acc_s, pre_s, g_s, bup_s, mask_s, sums_ref, low_s, two_s, act_s, in_sem, down_sem, up_sem, out_sem, low_sem = refs[29:]
    rows, width = x_ref.shape
    hidden = w2_s.shape[2]
    pieces = 4
    cols = width // pieces
    placed = blocks > 1
    chunk = 128
    share = width // blocks
    half = rows // 2
    b_out, b_down, gain_a, shift_a, gain_f, shift_f = (vec_ref[i : i + 1, :] for i in range(6))

    count = cols // HEAD_DIM
    att = [[own_ref[h] for h in range(count)]]
    for ref, i in ((near_ref, 0), (far_ref, 0), (near_ref, 1)):
        att.append([ref[i, h] for h in range(count)])

    loads = []
    for ref, entries in zip(w_refs, plan, strict=True):
        for index, second, j, row in entries:
            source = ref.at[index]
            target = (w2_s if second else w1_s).at[j].at[place_of(row, source.shape[0], placed)]
            copy = pltpu.make_async_copy(source, target, in_sem.at[len(loads)])
            loads.append((second, copy))
            copy.start()

    def row_loop(work):
        @pl.loop(0, rows // chunk)
        def _(i):
            work(pl.ds(pl.multiple_of(i * chunk, chunk), chunk))

    def add_sum(index, value):
        sums_ref[index : index + 1, :] += jnp.sum(value, axis=0, keepdims=True)

    def mean(value):
        return jnp.mean(value, axis=-1, keepdims=True)

    def normal(value):
        centred = value - mean(value)
        inverse = lax.rsqrt(mean(centred * centred) + EPSILON)
        return centred * inverse, inverse

    def norm_back(grad, unit, inverse, gain):
        scaled = grad * gain
        return (scaled - mean(scaled) - unit * mean(scaled * unit)) * inverse

    sums_ref[...] = jnp.zeros_like(sums_ref)
    own_valid = jnp.where(valid_row(positions_ref, lengths_ref, 0, rows), 1.0, 0.0)
    mask_s[...] = jnp.broadcast_to(own_valid, (LANES, rows)).T
    for j in range(pieces):
        for h in range(cols // HEAD_DIM):
            at = j * cols + h * HEAD_DIM
            att_s[:half, at : at + HEAD_DIM] = att[j][h][:, :HEAD_DIM]
            att_s[half:, at : at + HEAD_DIM] = att[j][h][:, HEAD_DIM:]
    for second, copy in loads:
        if not second:
            copy.wait()
    for j in range(pieces):
        wo_s[:, j * cols : (j + 1) * cols] = w1_s[j, :, hidden : hidden + cols]
        last = w1_s[j, :, hidden + cols - HEAD_DIM :].astype(F32)
        bup_s[j] = last.T[HEAD_DIM : HEAD_DIM + 1, :]
    ffn_s[...] = dot_nt(att_s[...], wo_s[...])

    def first_norm(r):
        value = x_ref[r, :].astype(F32)
        attn = ffn_s[r, :] + b_out
        valid = mask_s[r, :1] > 0.0
        add_sum(6, jnp.where(valid, value * value, 0.0))
        add_sum(7, jnp.where(valid, attn * attn, 0.0))
        unit, inverse = normal(value + attn)
        normed = unit * gain_a + shift_a
        n1_s[r, :] = unit
        rs_s[r, :] = jnp.broadcast_to(inverse, (chunk, LANES))
        nrm_s[r, :] = normed
        nb_s[r, :] = normed.astype(BF16)

    row_loop(first_norm)
    ffn_s[...] = jnp.zeros_like(ffn_s)
    for second, copy in loads:
        if second:
            copy.wait()

    wide = 256
    per = hidden // wide

    def chunk_of(c):
        return c // per, pl.ds(pl.multiple_of(c % per * wide, wide), wide)

    def product_of(c):
        j, at = chunk_of(c)
        return dot(nb_s[...], w1_s[j, :, at]) + bup_s[j, :, at]

    act_s[...] = jnp.zeros_like(act_s)
    two_s[0] = product_of(0)
    count = pieces * per

    @pl.loop(0, count)
    def _(c):
        j, at = chunk_of(c)
        back, behind = chunk_of(jnp.maximum(c - 1, 0))
        now = c % 2
        two_s[1 - now] = product_of(jnp.minimum(c + 1, count - 1))
        ffn_s[...] += dot_nt(act_s[...], w2_s[back, :, behind])
        pre = two_s[now]
        cdf = 0.5 * (1.0 + lax.erf(pre * (0.5**0.5)))
        pdf = jnp.exp(pre * pre * -0.5) * (2.0 * jnp.pi) ** -0.5
        act = (pre * cdf).astype(BF16)
        hid_s[j, :, at] = act
        slope_s[j, :, at] = cdf + pre * pdf
        act_s[...] = act

    ffn_s[...] += dot_nt(act_s[...], w2_s[pieces - 1, :, (per - 1) * wide :])

    def second_norm(r):
        ffn = ffn_s[r, :] + b_down
        valid = mask_s[r, :1] > 0.0
        add_sum(8, jnp.where(valid, ffn * ffn, 0.0))
        unit, inverse = normal(nrm_s[r, :] + ffn)
        lo_ref[r, :] = (unit * gain_f + shift_f).astype(BF16)
        grad = og_ref[r, :].astype(F32)
        add_sum(4, grad * unit)
        add_sum(5, grad)
        d_two = norm_back(grad, unit, inverse, gain_f)
        low = d_two.astype(BF16)
        add_sum(1, low.astype(F32))
        acc_s[r, :] = d_two
        gf_s[r, :] = low

    row_loop(second_norm)
    gft_s[...] = gf_s[...].T
    nbt_s[...] = nb_s[...].T

    places = [place_of(i, share, placed) for i in range(blocks)]

    def copies(j, lanes, target, place, sem, to):
        return [
            pltpu.make_async_copy(
                g_s.at[j].at[places[i], lanes], target.at[place, i, pl.ds(0, share), to], sem.at[j, i]
            )
            for i in range(blocks)
        ]

    lanes_d, lanes_u, lanes_o = (
        pl.ds(0, hidden),
        pl.ds(hidden, hidden),
        pl.ds(2 * hidden, cols),
    )
    to_d, to_u, to_o = pl.ds(0, hidden), pl.ds(0, hidden), pl.ds(hidden, cols)
    def start_all(j, place, lanes, to, sem, targets):
        for away in (1, 0):

            @pl.when(j % 2 == away)
            def _():
                for copy in copies(j, lanes, targets[1 - away], place, sem, to):
                    copy.start()

    @pl.loop(0, pieces)
    def _(step):
        away = 1 - step // (pieces // 2)
        place = step % (pieces // 2)
        j = 2 * place + away
        pre_s[...] = dot(gf_s[...], w2_s[j]) * slope_s[j]
        low = pre_s[...].astype(BF16)
        sums_ref[pl.ds(10 + j, 1), :] = jnp.sum(low.astype(F32), axis=0, keepdims=True)
        g_s[j, :, lanes_d] = dot(gft_s[...], hid_s[j]).astype(BF16)
        start_all(j, place, lanes_d, to_d, down_sem, (sent_d, kept_d))
        g_s[j, :, lanes_u] = dot(nbt_s[...], low).astype(BF16)
        start_all(j, place, lanes_u, to_u, up_sem, (sent_u, kept_u))
        acc_s[...] += dot_nt(low, w1_s[j, :, :hidden])

    def first_back(r):
        grad = acc_s[r, :]
        unit = n1_s[r, :]
        add_sum(2, grad * unit)
        add_sum(3, grad)
        d_one = norm_back(grad, unit, rs_s[r, :1], gain_a)
        low = d_one.astype(BF16)
        add_sum(0, low.astype(F32))
        done_ref[r, :] = d_one
        gf_s[r, :] = low

    row_loop(first_back)
    low = gf_s[...]
    gout = dot_tn(low, att_s[...]).astype(BF16)
    for j in range(pieces):
        g_s[j, :, 2 * hidden : 2 * hidden + cols] = gout[:, j * cols : (j + 1) * cols]
        for copy in copies(j, lanes_o, sent_u if j % 2 else kept_u, j // 2, out_sem, to_o):
            copy.start()
    small = []
    for j in range(pieces):
        low_s[j] = jnp.concatenate([sums_ref[:9], sums_ref[10 + j : 11 + j], sums_ref[9:15]]).astype(BF16)
        target = sent_d if j % 2 else kept_d
        for i in range(blocks):
            under = target.at[j // 2, i, pl.ds(share, EXTRA), :]
            small.append(pltpu.make_async_copy(low_s.at[j], under, low_sem.at[j, i]))
            small[-1].start()
    back = dot(low, wo_s[...]).astype(BF16)
    for j in range(pieces):
        for h in range(cols // HEAD_DIM):
            at = j * cols + h * HEAD_DIM
            ga[j][h, :, :HEAD_DIM] = back[:half, at : at + HEAD_DIM]
            ga[j][h, :, HEAD_DIM:] = back[half:, at : at + HEAD_DIM]
    for j in range(pieces):
        target_d, target_u = (sent_d, sent_u) if j % 2 else (kept_d, kept_u)
        for copy in copies(j, lanes_d, target_d, j // 2, down_sem, to_d):
            copy.wait()
        for copy in copies(j, lanes_u, target_u, j // 2, up_sem, to_u):
            copy.wait()
        for copy in copies(j, lanes_o, target_u, j // 2, out_sem, to_o):
            copy.wait()
    for copy in small:
        copy.wait()


def middle(blocks, weights, plan, att, tokens, out_grad, positions, lengths, vectors, hidden):
    rows, width = tokens.shape
    cols = width // 4
    share = width // blocks
    shape = jax.ShapeDtypeStruct
    vmem = pltpu.VMEM
    loads = sum(len(entries) for entries in plan)
    return pl.pallas_call(
        functools.partial(middle_kernel, plan=plan, blocks=blocks),
        in_specs=[ANY_SPEC] * len(weights) + [VMEM_SPEC] * 6 + [SMEM_SPEC, VMEM_SPEC],
        out_specs=[VMEM_SPEC] * 2 + [ANY_SPEC] * 4 + [VMEM_SPEC] * 4,
        out_shape=[
            shape((rows, width), BF16),
            shape((rows, width), F32),
        ]
        + [shape((2, blocks, share + EXTRA, hidden), BF16)] * 2
        + [shape((2, blocks, share, hidden + cols), BF16)] * 2
        + [shape(att[0].shape, BF16)] * 4,
        scratch_shapes=[
            vmem((4, width, weights[0].shape[-1]), BF16),
            vmem((4, width, hidden), BF16),
            vmem((rows, width), BF16),
            vmem((width, width), BF16),
            vmem((4, rows, hidden), BF16),
            vmem((4, rows, hidden), F32),
            vmem((rows, width), F32),
            vmem((rows, width), BF16),
            vmem((rows, width), F32),
            vmem((rows, LANES), F32),
            vmem((rows, width), F32),
            vmem((rows, width), BF16),
            vmem((width, rows), BF16),
            vmem((width, rows), BF16),
            vmem((rows, width), F32),
            vmem((rows, hidden), F32),
            vmem((4, width, 2 * hidden + cols), BF16),
            vmem((4, 1, hidden), F32),
            vmem((rows, LANES), F32),
            vmem((16, width), F32),
            vmem((4, EXTRA, width), BF16),
            vmem((2, rows, 256), F32),
            vmem((rows, 256), BF16),
            pltpu.SemaphoreType.DMA((loads,)),
            pltpu.SemaphoreType.DMA((4, blocks)),
            pltpu.SemaphoreType.DMA((4, blocks)),
            pltpu.SemaphoreType.DMA((4, blocks)),
            pltpu.SemaphoreType.DMA((4, blocks)),
        ],
        compiler_params=params(),
        cost_estimate=cost(1000, 1000),
        name="middle",
    )(*weights, *att, tokens, out_grad, positions, lengths, vectors)


def reduce_kernel(*refs, jobs, inputs, outputs, terms, extra, extra_in):
    ins = refs[:inputs]
    more = refs[inputs : inputs + extra_in]
    outs = refs[inputs + extra_in : inputs + extra_in + outputs]
    rest = refs[inputs + extra_in + outputs :]
    extra_out = rest[: len(rest) - terms - 1]
    held, sems = rest[len(extra_out) : -1], rest[-1]
    loads = []
    for _, _, _, parts, _ in jobs:
        for source, index, start, size in parts:
            at = len(loads)
            picked = ins[source].at[index + (slice(None), pl.ds(start, size))]
            loads.append(pltpu.make_async_copy(picked, held[at], sems.at[at]))
            loads[-1].start()
    at = 0
    for out, start, lead, parts, base in jobs:
        mine = range(at, at + len(parts))
        at += len(parts)
        for i in mine:
            loads[i].wait()
        size = parts[0][3]
        for index in itertools.product(*map(range, lead)):
            total = held[mine[0]][index].astype(F32)
            for i in mine[1:]:
                total += held[i][index].astype(F32)
            target = outs[out]
            target[base + index + (slice(None), slice(start, start + size))] = total.astype(target.dtype)
    if extra is not None:
        extra(outs, more, extra_out)


class Sum:
    def __init__(self, names, width):
        self.names, self.width, self.terms, self.picks = list(names), width, [], {}

    def join(self, array, start=0, names=None):
        self.terms.append((array, start, list(self.names if names is None else names)))

    def parts(self, picks):
        return [
            (array, tuple(picks.get(name, slice(None)) for name in names), start, self.width)
            for array, start, names in self.terms
        ]

    def away(self, name):
        parts = self.parts({**self.picks, name: 1})
        self.picks[name] = 0
        self.names.remove(name)
        return parts

    def all(self):
        return self.parts(self.picks)


def reduce_call(name, groups, dtype, extra=None, extra_in=(), extra_out=(), keep=True):
    arrays, jobs, shapes, scratch = [], [], [], []
    for out, columns in enumerate(groups):
        start = 0
        stacked = isinstance(columns, tuple)
        for at, parts in enumerate(columns):
            coded = []
            for array, index, first, size in parts:
                known = [i for i, other in enumerate(arrays) if other is array]
                if not known:
                    arrays.append(array)
                coded.append((known[0] if known else len(arrays) - 1, index, first, size))
                sizes = [n for n, i in zip(array.shape, index) if isinstance(i, slice)]
                sizes += [array.shape[-2], size]
                scratch.append(pltpu.VMEM(tuple(sizes), array.dtype))
            jobs.append((out, start, tuple(sizes[:-2]), coded, (at,) if stacked else ()))
            start += 0 if stacked else coded[0][3]
        front = (len(columns),) if stacked else ()
        shapes.append(front + tuple(sizes[:-1]) + (coded[0][3] if stacked else start,))
    outs = [jax.ShapeDtypeStruct(shape, dtype) for shape in shapes]
    held = [] if keep else [pltpu.VMEM(shape, dtype) for shape in shapes]
    result = pl.pallas_call(
        functools.partial(
            reduce_kernel if keep else reduce_inside,
            jobs=jobs,
            inputs=len(arrays),
            outputs=len(outs),
            terms=len(scratch),
            extra=extra,
            extra_in=len(extra_in),
        ),
        in_specs=[HBM_SPEC] * len(arrays) + [VMEM_SPEC] * len(extra_in),
        out_specs=[VMEM_SPEC] * (len(outs) * keep + len(extra_out)),
        out_shape=outs * keep + list(extra_out),
        scratch_shapes=held + scratch + [pltpu.SemaphoreType.DMA((len(scratch),))],
        compiler_params=params(),
        cost_estimate=cost(1000, 1000),
        name=name,
    )(*arrays, *extra_in)
    return result


def reduce_inside(*refs, inputs, extra_in, outputs, terms, **rest):
    front = inputs + extra_in
    results = refs[front : len(refs) - outputs - terms - 1]
    held = refs[len(refs) - outputs - terms - 1 : len(refs) - terms - 1]
    order = refs[:front] + held + results + refs[len(refs) - terms - 1 :]
    reduce_kernel(*order, inputs=inputs, extra_in=extra_in, outputs=outputs, terms=terms, **rest)


def body(
    tokens,
    seq_lengths,
    positions,
    w_query,
    w_key,
    w_value,
    w_out,
    w_up,
    w_down,
    b_query,
    b_value,
    b_out,
    b_up,
    b_down,
    gain_attn,
    shift_attn,
    gain_ffn,
    shift_ffn,
    out_grad,
):
    group = lax.axis_index("dp")
    member = lax.axis_index("tensor")
    dp_count = lax.axis_size("dp")
    bits = dp_count.bit_length() - 1
    rows, width = tokens.shape
    own_cols = w_query.shape[1]
    heads = own_cols // HEAD_DIM
    share = w_query.shape[0]
    hidden = w_up.shape[1]
    placed = share % 16 == 0 and bits == 3 and heads == 3
    blocks = dp_count if placed else 1
    def core(value):
        return swap(value, "tensor", 1)

    def cross(value):
        return swap(value, "tensor", 2)

    def grow(value, got, masks, bit):
        both = jnp.stack([value, got], axis=1).reshape((-1,) + value.shape[1:])
        return both, [m ^ b for m in masks for b in (0, bit)]

    across = cross(tokens)
    beside = core(tokens)
    own_qkv = jnp.concatenate([w_query, w_key, w_value], axis=1)[None]
    own_b_up = lax.dynamic_slice_in_dim(b_up, group * share, share, 0)[:, None]
    spare = -(hidden + own_cols) % LANES
    one = jnp.concatenate([w_up, w_out.T, jnp.broadcast_to(own_b_up, (share, spare))], axis=1)[None]
    two = w_down.T[None]
    biases = [b_query.reshape(1, -1), b_value.reshape(1, -1)]
    vectors = [b_out, b_down, gain_attn, shift_attn, gain_ffn, shift_ffn]
    vectors = jnp.stack([vec.astype(F32) for vec in vectors] + [jnp.zeros((width,), F32)] * 2)

    if placed:
        got_w = after(swap(own_qkv, "dp", 4), one, two)
        w_part, w_mask = grow(own_qkv, got_w, [0], 4)
        one = after(one, w_part)
        got_w, got_one, across = after((swap(w_part, "dp", 2), swap(one, "dp", 4), across), w_part)
        w_part, w_mask = grow(w_part, got_w, w_mask, 2)
        one, one_mask = grow(one, got_one, [0], 4)

        two = after(two, across)
        round_three = (swap(w_part, "dp", 1), swap(one, "dp", 2), cross(two), core(across))
        round_three = after((round_three, biases, vectors), w_part)
        (got_w, got_one, got_two, beyond), biases, vectors = round_three
        w_qkv, w_masks = [w_part, got_w], [w_mask, [m ^ 1 for m in w_mask]]
        one, one_mask = grow(one, got_one, one_mask, 2)
        two = jnp.stack([two, got_two], axis=1)
        parts = [tokens, beside, across, beyond]

        round_four = (swap(two, "dp", 4), swap(one, "dp", 1), cross(one), core(one))
        positions = after(positions, one, two)
        q, k, v = project(parts, w_qkv, w_masks, *biases, positions, seq_lengths, heads, placed)
        kept = attention_forward(0, 1, q, k, v, [])
        q_kept = kept[0]
        got_two, odd, even_far, even_near = after(round_four, q_kept)
        two, two_mask = grow(two, got_two, [0], 4)

        round_five = (swap(two, "dp", 2), cross(odd), swap(two, "dp", 1), core(even_far))
        kept, odd, two, even_far = after((kept, odd, two, even_far), q_kept)
        q_kept, out, *packed = attention_forward(1, 2, q, k, v, kept)
        kept = [q_kept, out]
        two_late, odd_far, two_odd, both_near = after(round_five, q_kept)

        far_odd = [m ^ 1 for m in one_mask]
        two_mask_odd = [m ^ 1 for m in two_mask]
        late_mask, last_mask = [m ^ 2 for m in two_mask], [m ^ 3 for m in two_mask]
        two_last = swap(two_late, "dp", 1)
        att_far = cross(packed[2])
        odd, two = after((odd, two), two_late)
        two_near, odd_near = core(two), core(odd)
        odd_far, two_late, two_odd = after((odd_far, two_late, two_odd), two_near, odd_near)
        odd_far_near, late_near, two_odd_near = core(odd_far), core(two_late), core(two_odd)
        two_last, att_far = after((two_last, att_far), odd_far_near, late_near, two_odd_near)
        att_near = core(jnp.stack([packed[1], att_far[1]]))
        ones = [(one, one_mask), (odd, far_odd), (even_far, one_mask), (odd_far, far_odd)]
        twos = [(two, two_mask), (two_odd, two_mask_odd), (two_late, late_mask), (two_last, last_mask)]
        early = [even_near, odd_near, both_near, odd_far_near, two_near, two_odd_near, late_near]
        early.append(core(two_last))
    else:
        w_qkv = [gather_bits(own_qkv[0], "dp", range(bits), 0).reshape(1, width, -1)]
        w_masks = [[0]]
        one = gather_bits(one[0], "dp", range(bits), 0).reshape(1, width, -1)
        two = gather_bits(two[0], "dp", range(bits), 0).reshape(1, width, -1)
        parts = [tokens, beside, across, core(across)]
        q, k, v = project(parts, w_qkv, w_masks, *biases, positions, seq_lengths, heads, placed)
        q_kept, out, *packed = attention_forward(0, heads, q, k, v, [])
        kept = [q_kept, out]
        ones = [(one, [0]), (cross(one), [0])]
        twos = [(jnp.stack([two, cross(two)], axis=1), [0])]
        early = [core(array) for array, _ in ones + twos]
        att_far = cross(packed[2])
        att_near = core(jnp.stack([packed[1], att_far[1]]))
    att = [packed[0], att_near, att_far]
    weights = [array for array, _ in ones + twos] + early
    plan = []
    for near in range(2):
        for a, (_, masks) in enumerate(ones):
            far = a // (len(ones) // 2)
            plan.append([((z,), False, near + 2 * far, mask) for z, mask in enumerate(masks)])
        for _, masks in twos:
            plan.append(
                [
                    ((z, far), True, near + 2 * far, mask)
                    for z, mask in enumerate(masks)
                    for far in range(2)
                ]
            )
    layer_out, d_one, sent_d, kept_d, sent_u, kept_u, *back = middle(
        blocks, weights, plan, att, tokens, out_grad, positions, seq_lengths, vectors, hidden
    )
    grads = [back[0]] + [swap(back[j], "tensor", j) for j in (1, 2, 3)]

    def add(*terms):
        total = terms[0].astype(F32)
        for term in terms[1:]:
            total = total + term.astype(F32)
        return total

    def send(away, name):
        return cross(away) if name == "x" else swap(away, "dp", 1 << name)

    def axes_of(array, lead):
        return array.reshape(array.shape[:lead] + (2,) * bits + array.shape[lead + 1 :])

    names = list(range(bits))[::-1]
    late = list(range(1, bits))
    shape = jax.ShapeDtypeStruct
    three = 3 * HEAD_DIM

    got_d, got_u = core(sent_d), core(sent_u)
    if placed:
        down, up = Sum(["x"] + names, hidden), Sum(["x"] + names, hidden + own_cols)
        for array in (kept_u, got_u):
            up.join(axes_of(array, 1))
        (move_u,) = reduce_call("sum_up", [[up.away(0)]], BF16)
        got_d = after(got_d, move_u)
        for array in (kept_d, got_d):
            down.join(axes_of(array, 1))
        (move_d,) = reduce_call("sum_down", [[down.away("x")]], BF16)
        move_d = after(move_d, grads)
        grads = after(grads, move_d)
        down_names, up_names = ["x"] + late + [0], [0, "x"] + late
    q_kept, out = kept
    if placed:
        before = attention_backward(0, heads - 1, q_kept, k, v, out, grads, parts, blocks, [])
        last = before[0]
        down.join(after(send(move_d, down_names.pop(0)), last))
        up.join(after(send(move_u, up_names.pop(0)), last))
        groups = [[down.away(down_names[0])], [up.away(up_names[0])]]
        move_d, move_u = reduce_call("sum_second", groups, BF16)
        q_kept = after(q_kept, move_d)
        more = (before[0], w_qkv, w_masks)
        g_last, g_w, *first = attention_backward(
            heads - 1, 1, q_kept, k, v, out, grads, parts, blocks, before[1:], more
        )
        g_parts = [before[0], g_last]
    else:
        g_all, g_w = attention_backward(0, heads, q_kept, k, v, out, grads, parts, blocks, [])
    if placed:
        down.join(after(send(move_d, down_names.pop(0)), g_last))
        up.join(after(send(move_u, up_names.pop(0)), g_last))
        got_part = [core(part) for part in first[:2]]
    half = rows // 2
    own_parts = ((rows, half), (rows + half, half), (0, rows))
    if placed:
        qkv = Sum(["h"] + names, 4 * HEAD_DIM)
        qkv.join(axes_of(g_w, 1))
        groups = [[down.away(down_names[0])], [up.away(up_names[0])], [qkv.away(0)]]
        groups.append(tuple([(first[2], (i,), 0, width), (got_part[i], (), 0, width)] for i in range(2)))
        move_d, move_u, move_qkv, crossed = reduce_call("sum_third", groups, BF16)
        crossed = cross(crossed)
        g_parts = after(g_parts, move_d)
        second = input_part(g_parts, w_qkv, w_masks, own_parts, placed)
        near = [core(part) for part in second[:2]]
        down.join(after(send(move_d, down_names.pop(0)), *second))
        up.join(after(send(move_u, up_names.pop(0)), *second))
        qkv.join(after(send(move_qkv, 0), *second))
        crossed = after(crossed, *second)
        others = list(itertools.product(range(2), repeat=len(late)))[1:]
        groups = [[down.away(down_names[0])], [up.away(up_names[0])]]
        groups += [[qkv.parts({**qkv.picks, **dict(zip(late, pick))})] for pick in others]
        move_d, move_u, *moves_qkv = reduce_call("sum_fourth", groups, BF16)
        down.join(send(move_d, down_names.pop(0)))
        got_u = send(move_u, up_names.pop(0))
        gots_qkv = [
            swap(move, "dp", sum(bit << name for bit, name in zip(pick, late)))
            for move, pick in zip(moves_qkv, others)
        ]
        qkv.picks.update(dict.fromkeys(late, 0))
        for name in late:
            qkv.names.remove(name)

        def finish_down(totals, ins, outs):
            outs[0][...] = totals[0][:share]
            outs[1][...] = totals[0][share:]
            for i in range(2):
                part = pl.ds(i * half, half)
                total = ins[0][part, :]
                for term in (ins[1][part, :], ins[2][i], ins[3 + i][...]):
                    total += term.astype(F32)
                outs[2][part, :] = total.astype(BF16)

        g_down, small, input_grad = reduce_call(
            "finish_down",
            [[down.all()]],
            F32,
            finish_down,
            (d_one, second[2], crossed, *near),
            (
                shape((share, hidden), F32),
                shape((EXTRA, width), F32),
                shape((rows, width), BF16),
            ),
            keep=False,
        )
        g_down = g_down.T
        got_u, gots_qkv = after((got_u, gots_qkv), small)
        up.join(got_u)
        for got in gots_qkv:
            qkv.join(got)
    else:
        first = input_part([g_all], w_qkv, w_masks, ((3 * rows, rows), (2 * rows, rows)), placed)
        crossed = cross(add(first[1], core(first[0])).astype(BF16))
        second = input_part([g_all], w_qkv, w_masks, own_parts, placed)
        near = jnp.concatenate([core(part) for part in second[:2]])

    if placed:

        def finish(totals, _, outs):
            g_up, g_qkv = totals
            q_out, k_out, v_out, o_out, up_out, bq_out, bv_out = outs
            for h in range(heads):
                at = pl.ds(h * HEAD_DIM, HEAD_DIM)
                for kind, out in enumerate((q_out, k_out, v_out)):
                    out[:, at] = g_qkv[h, :, kind * HEAD_DIM : (kind + 1) * HEAD_DIM]
                bq_out[:, at] = g_qkv[h, 0:1, three:]
                bv_out[:, at] = g_qkv[h, 8:9, three:]
            up_out[...] = g_up[:, :hidden]
            o_out[...] = g_up[:, hidden:].T

        g_q, g_k, g_v, g_out, g_up, bias_q, bias_v = reduce_call(
            "finish",
            [[up.all()], [qkv.all()]],
            F32,
            finish,
            (),
            (
                [shape((share, own_cols), F32)] * 3
                + [shape((own_cols, share), F32), shape((share, hidden), F32)]
                + [shape((1, own_cols), F32)] * 2
            ),
            keep=False,
        )
        bias_q, bias_v = bias_q[0], bias_v[0]
    else:
        input_grad = add(d_one, second[2], near, crossed).astype(BF16)
        two_s = (2,) * bits

        def whole_sum(mine, got):
            total = add(mine, got)
            return total[0, 0] + cross(total[1, 0].astype(BF16)).astype(F32)

        def home(total, lead):
            shaped = total.reshape(total.shape[:lead] + two_s + (share, total.shape[-1]))
            return scatter_bits(shaped, "dp", range(bits), lead)

        total = whole_sum(kept_d, got_d)
        g_down, small = home(total[:width], 0).T, total[width:]
        total = home(whole_sum(kept_u, got_u), 0)
        g_up, g_out = total[:, :hidden], total[:, hidden:].T
        g_qkv = home(g_w[:, 0, :, :three].astype(F32), 1).reshape(heads, share, 3, HEAD_DIM)
        g_q, g_k, g_v = (g_qkv[:, :, i].transpose(1, 0, 2).reshape(share, own_cols) for i in range(3))
        bias_rows = g_w[:, 0, 0:16:8, three:].astype(F32)
        for bit in range(bits):
            small = small + swap(small, "dp", 1 << bit)
            bias_rows = bias_rows + swap(bias_rows, "dp", 1 << bit)
        bias_q, bias_v = bias_rows[:, 0].reshape(own_cols), bias_rows[:, 1].reshape(own_cols)
    count = jnp.sum(seq_lengths).astype(F32) * width
    rms = jnp.sqrt(jnp.sum(small[6:9], axis=-1) / count)
    return (
        layer_out,
        input_grad,
        g_q,
        g_k,
        g_v,
        g_out,
        g_up,
        g_down,
        bias_q,
        bias_v,
        small[0],
        small[9],
        small[1],
        small[2],
        small[3],
        small[4],
        small[5],
        rms,
    )


def solution(mesh):
    in_specs = (
        P(("dp", "tensor"), None),
        P(),
        P("dp", None),
        P("dp", "tensor"),
        P("dp", "tensor"),
        P("dp", "tensor"),
        P("tensor", "dp"),
        P("dp", "tensor"),
        P("tensor", "dp"),
        P("tensor"),
        P("tensor"),
        P(),
        P("tensor"),
        P(),
        P(),
        P(),
        P(),
        P(),
        P(("dp", "tensor"), None),
    )
    out_specs = (
        P(("dp", "tensor"), None),
        P(("dp", "tensor"), None),
        P("dp", "tensor"),
        P("dp", "tensor"),
        P("dp", "tensor"),
        P("tensor", "dp"),
        P("dp", "tensor"),
        P("tensor", "dp"),
        P("tensor"),
        P("tensor"),
        P(),
        P("tensor"),
        P(),
        P(),
        P(),
        P(),
        P(),
        P(),
    )
    return jax.shard_map(body, mesh=mesh, in_specs=in_specs, out_specs=out_specs, check_vma=False)
```

```python
import functools
import itertools
import math

import jax
import jax.numpy as jnp
from jax import lax
from jax.experimental import pallas as pl
from jax.experimental.pallas import tpu as pltpu
from jax.sharding import PartitionSpec as P

HEAD_DIM = 64
LANES = 128
EPSILON = 1e-12
MASKED = -1e30
BF16 = jnp.bfloat16
F32 = jnp.float32
NT = (((1,), (1,)), ((), ()))
TN = (((0,), (0,)), ((), ()))
EXTRA = 16


def dot(left, right):
    return jnp.dot(left, right, preferred_element_type=F32)


def dot_nt(left, right):
    return lax.dot_general(left, right, NT, preferred_element_type=F32)


def dot_tn(left, right):
    return lax.dot_general(left, right, TN, preferred_element_type=F32)


def place_of(mask, height, placed):
    start = (lax.axis_index("dp") ^ mask) * height if placed else 0
    return pl.ds(pl.multiple_of(start, height), height)


def valid_row(positions_ref, lengths_ref, j, rows):
    start = (lax.axis_index("tensor") ^ j) * rows
    own = positions_ref[:, pl.ds(pl.multiple_of(start, rows), rows)]
    return own < lengths_ref[lax.axis_index("dp")]


def in_three(column):
    first = column.astype(BF16)
    rest = column - first.astype(F32)
    second = rest.astype(BF16)
    third = (rest - second.astype(F32)).astype(BF16)
    return first, second, third


def swap(value, axis, bits):
    size = lax.axis_size(axis)
    return lax.ppermute(value, axis, [(i, i ^ bits) for i in range(size)])


def bit_of(axis, bit):
    return (lax.axis_index(axis) >> bit) & 1


def gather_bits(block, axis, order, at):
    done = []
    for bit in order:
        place = at + sum(other > bit for other in done)
        got = swap(block, axis, 1 << bit)
        upper = bit_of(axis, bit) == 1
        low = jnp.where(upper, got, block)
        high = jnp.where(upper, block, got)
        block = jnp.stack([low, high], axis=place)
        done.append(bit)
    return block


def scatter_bits(partial, axis, order, at):
    left = sorted(order, reverse=True)
    for bit in order:
        place = at + left.index(bit)
        mine = bit_of(axis, bit)
        away = lax.dynamic_index_in_dim(partial, 1 - mine, place, keepdims=False)
        keep = lax.dynamic_index_in_dim(partial, mine, place, keepdims=False)
        got = swap(away.astype(BF16), axis, 1 << bit)
        partial = keep.astype(F32) + got.astype(F32)
        left.remove(bit)
    return partial


def after(value, *others):
    return lax.optimization_barrier((value,) + others)[0]


def params(mebibytes=63):
    return pltpu.CompilerParams(vmem_limit_bytes=mebibytes << 20)


def cost(flops, moved, exps=0):
    return pl.CostEstimate(flops=flops, bytes_accessed=moved, transcendentals=exps)


SMEM_SPEC = pl.BlockSpec(memory_space=pltpu.SMEM)
VMEM_SPEC = pl.BlockSpec(memory_space=pltpu.VMEM)
ANY_SPEC = pl.BlockSpec(memory_space=pl.ANY)
HBM_SPEC = pl.BlockSpec(memory_space=pltpu.HBM)


def project_kernel(*refs, masks, heads, placed):
    x_refs, w_refs = refs[:4], refs[4 : 4 + len(masks)]
    bq_ref, bv_ref, positions_ref, lengths_ref, q_out, k_out, v_out, w_s, x_s, m_s, sems = refs[
        4 + len(masks) :
    ]
    rows = x_refs[0].shape[0]
    loads = [pltpu.make_async_copy(x_refs[j], x_s.at[j], sems.at[j]) for j in range(4)]
    for load in loads:
        load.start()
    for ref, entries in zip(w_refs, masks, strict=True):
        for z, mask in enumerate(entries):
            w_s[place_of(mask, ref.shape[1], placed), :] = ref[z]
    lane = lax.broadcasted_iota(jnp.int32, (1, LANES), 1)
    head_lane = lane < HEAD_DIM
    one_q = jnp.where(lane == HEAD_DIM, 1.0, 0.0)
    one_k = jnp.where((lane > HEAD_DIM) & (lane <= HEAD_DIM + 3), 1.0, 0.0)
    one_v = jnp.where((lane >= HEAD_DIM) & (lane < HEAD_DIM + 3), 1.0, 0.0)
    b_query = bq_ref[...].astype(F32)
    bias = jnp.concatenate([b_query, jnp.zeros_like(b_query), bv_ref[...].astype(F32)], axis=1)
    for j in range(4):
        masked = jnp.where(valid_row(positions_ref, lengths_ref, j, rows), 0.0, MASKED)
        m_s[j] = jnp.broadcast_to(masked, (8, rows))
    for load in loads:
        load.wait()

    @pl.loop(0, 4)
    def _(j):
        part = pl.ds(pl.multiple_of(j * rows, rows), rows)
        whole = dot(x_s[j], w_s[...]) + bias
        masked = jnp.broadcast_to(m_s[j, 0:1, :], (LANES, rows)).T

        def columns(group):
            start = group // 2 * LANES
            both = whole[:, start : start + LANES]
            if both.shape[1] < LANES:
                both = jnp.concatenate([both, both], axis=1)
            return pltpu.roll(both, HEAD_DIM, 1) if group % 2 else both

        for h in range(heads):
            query = columns(h).astype(BF16).astype(F32) * (HEAD_DIM**-0.5)
            q_out[h, part, :] = jnp.where(head_lane, query, one_q).astype(BF16)
            key = jnp.where(head_lane, columns(heads + h), one_k)
            k_out[h, part, :] = jnp.where(lane == HEAD_DIM, masked, key).astype(BF16)
            value = jnp.where(head_lane, columns(2 * heads + h), one_v)
            v_out[h, part, :] = value.astype(BF16)


def project(parts, pieces, masks, b_query, b_value, positions, lengths, heads, placed):
    rows, width = parts[0].shape
    seq = 4 * rows
    return pl.pallas_call(
        functools.partial(project_kernel, masks=masks, heads=heads, placed=placed),
        in_specs=[ANY_SPEC] * 4 + [VMEM_SPEC] * (3 + len(pieces)) + [SMEM_SPEC],
        out_specs=[VMEM_SPEC] * 3,
        out_shape=[jax.ShapeDtypeStruct((heads, seq, LANES), BF16)] * 3,
        scratch_shapes=[
            pltpu.VMEM((width, pieces[0].shape[2]), BF16),
            pltpu.VMEM((4, rows, width), BF16),
            pltpu.VMEM((4, 8, rows), F32),
            pltpu.SemaphoreType.DMA((4,)),
        ],
        compiler_params=params(32),
        cost_estimate=cost(1000, 1000),
        name="project",
    )(*parts, *pieces, b_query, b_value, positions, lengths)


def forward_kernel(q_ref, k_ref, v_ref, *refs, unroll):
    q_out, o_out, own, near, far, packed = refs[-6:]
    seq = q_ref.shape[1]
    block = seq // 8
    lane = lax.broadcasted_iota(jnp.int32, (1, LANES), 1)
    head_lane = lane < HEAD_DIM

    def place(i):
        return pl.ds(pl.multiple_of(i * block, block), block)

    def scores_of(i):
        query = q_ref[0, place(i), :]
        scores = dot_nt(query, k_ref[0])
        return query, scores, jnp.max(scores, axis=-1, keepdims=True)

    def attend(i, query, scores, top):
        expon = jnp.exp(scores - top).astype(BF16)
        total = dot(expon, v_ref[0])
        row_sum = total[:, HEAD_DIM : HEAD_DIM + 1]
        out = total * (1.0 / row_sum)
        o_out[0, place(i), :] = out
        one, two, three = in_three(-(top + jnp.log(row_sum)))
        q_out[0, place(i), :] = jnp.where(
            lane == HEAD_DIM + 1,
            one,
            jnp.where(lane == HEAD_DIM + 2, two, jnp.where(lane == HEAD_DIM + 3, three, query)),
        )
        return out

    @pl.loop(0, 8 // unroll)
    def _(step):
        held = scores_of(step * unroll)
        even = None
        for u in range(unroll):
            i = step * unroll + u
            following = scores_of(i + 1) if u < unroll - 1 else None
            out = attend(i, *held)
            if u % 2 == 0:
                even = out
            else:
                pair = jnp.where(head_lane, even, pltpu.roll(out, HEAD_DIM, 1))
                packed[step * (unroll // 2) + u // 2] = pair.astype(BF16)
            held = following

    own[0] = packed[0]
    near[0] = packed[1]
    far[0, 0] = packed[2]
    far[1, 0] = packed[3]


def attention_forward(first, count, q, k, v, before):
    heads, seq, _ = q.shape
    block = seq // 8
    one = pl.BlockSpec((1, seq, LANES), lambda i: (first + i, 0, 0))
    piece = pl.BlockSpec((1, block, LANES), lambda i: (first + i, 0, 0))
    pieces = pl.BlockSpec((2, 1, block, LANES), lambda i: (0, first + i, 0, 0))
    shape = jax.ShapeDtypeStruct
    return pl.pallas_call(
        functools.partial(forward_kernel, unroll=4 if first else 2),
        grid=(count,),
        in_specs=[one] * 3 + [ANY_SPEC] * len(before),
        out_specs=[one, one, piece, piece, pieces],
        out_shape=[shape((heads, seq, LANES), BF16), shape((heads, seq, LANES), F32)]
        + [shape((heads, block, LANES), BF16)] * 2
        + [shape((2, heads, block, LANES), BF16)],
        scratch_shapes=[pltpu.VMEM((4, block, LANES), BF16)],
        input_output_aliases={3 + i: i for i in range(len(before))},
        compiler_params=params(32),
        cost_estimate=cost(1000, 1000),
        name="attention_forward",
    )(q, k, v, *before)


def by_head(w_refs, masks, heads, placed, target):
    for ref, entries in zip(w_refs, masks, strict=True):
        for z, mask in enumerate(entries):
            place = place_of(mask, ref.shape[1], placed)
            for h in range(heads):
                for kind in range(3):
                    start = (kind * heads + h) * HEAD_DIM
                    stop = (h * 3 + kind) * HEAD_DIM
                    target[place, stop : stop + HEAD_DIM] = ref[z, :, start : start + HEAD_DIM]


def through_weights(g_refs, part, w_s):
    three = 3 * HEAD_DIM
    total, h = None, 0
    for ref in g_refs:
        for i in range(ref.shape[0]):
            term = dot_nt(ref[i, part, :], w_s[:, h * three : (h + 1) * three])
            total = term if total is None else total + term
            h += 1
    return total


def backward_kernel(q_ref, k_ref, v_ref, o_ref, *refs, placed, masks, heads):
    d_refs, x_refs = refs[:4], refs[4:8]
    if masks:
        g_ref, gw_ref, *dx_refs, dk_s, dv_s, gw_s, d_s, w_s = refs[-10:]
        by_head(refs[9 : 9 + len(masks)], masks, heads, placed, w_s)
    else:
        g_ref, gw_ref, dk_s, dv_s, gw_s, d_s = refs[-6:]
    seq = q_ref.shape[1]
    block = seq // 8
    rows = seq // 4
    lane = lax.broadcasted_iota(jnp.int32, (1, LANES), 1)
    head_lane = lane < HEAD_DIM
    scale = HEAD_DIM**-0.5
    for j in range(4):
        d_s[j] = d_refs[j][0]
    dk_s[...] = jnp.zeros_like(dk_s)
    dv_s[...] = jnp.zeros_like(dv_s)

    @pl.loop(0, 4)
    def _(j):
        for half in range(2):
            place = pl.ds(pl.multiple_of((2 * j + half) * block, block), block)
            query = q_ref[0, place, :]
            grad = d_s[j].astype(F32)
            if half == 1:
                grad = pltpu.roll(grad, HEAD_DIM, 1)
            grad = jnp.where(head_lane, grad, 0.0)
            delta = jnp.sum(grad * o_ref[0, place, :], axis=-1, keepdims=True)
            one, two, three = in_three(-delta)
            grad = grad.astype(BF16)
            grad_and = jnp.where(
                lane == HEAD_DIM,
                one,
                jnp.where(lane == HEAD_DIM + 1, two, jnp.where(lane == HEAD_DIM + 2, three, grad)),
            )
            probs = jnp.exp(dot_nt(k_ref[0], query))
            lifted = dot_nt(v_ref[0], grad_and)
            grad_scores = (probs * lifted).astype(BF16)
            dv_s[...] += dot(probs.astype(BF16), grad)
            dk_s[...] += dot(grad_scores, query)
            grad_query = dot_tn(grad_scores, k_ref[0]) * scale
            g_ref[0, place, :LANES] = jnp.where(head_lane, grad_query, 0.0).astype(BF16)

    both = jnp.where(head_lane, g_ref[0, :, :LANES].astype(F32), pltpu.roll(dk_s[...], HEAD_DIM, 1))
    g_ref[0, :, :LANES] = both.astype(BF16)
    g_ref[0, :, LANES:] = dv_s[:, :HEAD_DIM].astype(BF16)
    grads = g_ref[0]
    bias = jnp.sum(grads.astype(F32), axis=0, keepdims=True)
    share = gw_ref.shape[2]
    line = lax.broadcasted_iota(jnp.int32, (share, 1), 0)
    side = jnp.where(line < 8, bias[:, :HEAD_DIM], 0.0)
    side = jnp.where((line >= 8) & (line < 16), bias[:, LANES:], side).astype(BF16)
    total = dot_tn(grads[:rows], x_refs[0][...])
    for j in range(1, 4):
        total += dot_tn(grads[j * rows : (j + 1) * rows], x_refs[j][...])
    gw_s[...] = total.T.astype(BF16)
    for i in range(gw_ref.shape[1]):
        gw_ref[0, i, :, : 3 * HEAD_DIM] = gw_s[place_of(i, share, placed), :]
        gw_ref[0, i, :, 3 * HEAD_DIM :] = side
    if masks:
        half = rows // 2
        spread = (3 * rows, 3 * rows + half, 2 * rows)
        for out, start in zip(dx_refs, spread, strict=True):
            count = math.prod(out.shape[:-1])
            total = through_weights((refs[8], g_ref), pl.ds(start, count), w_s)
            out[...] = total.astype(BF16).reshape(out.shape)


def attention_backward(first, count, q, k, v, out, grads, parts, blocks, before, more=()):
    heads, seq, _ = k.shape
    rows, width = parts[0].shape
    one = pl.BlockSpec((1, seq, LANES), lambda i: (first + i, 0, 0))
    piece = pl.BlockSpec((1, seq // 8, LANES), lambda i: (first + i, 0, 0))
    whole = pl.BlockSpec((rows, width), lambda i: (0, 0))
    three = 3 * HEAD_DIM
    share = width // blocks
    shape = jax.ShapeDtypeStruct

    def fixed(array):
        return pl.BlockSpec(array.shape, lambda i: (0,) * len(array.shape))

    others, pieces, masks = more if more else (None, [], ())
    extra = [others, *pieces] if more else []
    dx = [shape((rows // 2, width), BF16)] * 2 + [shape((2, rows // 2, width), BF16)] if more else []
    return pl.pallas_call(
        functools.partial(backward_kernel, placed=blocks > 1, masks=masks, heads=heads),
        grid=(count,),
        in_specs=[one] * 4
        + [piece] * 4
        + [whole] * 4
        + [fixed(array) for array in extra]
        + [ANY_SPEC] * len(before),
        out_specs=[
            pl.BlockSpec((1, seq, three), lambda i: (i, 0, 0)),
            pl.BlockSpec((1, blocks, share, 4 * HEAD_DIM), lambda i: (first + i, 0, 0, 0)),
        ]
        + [fixed(array) for array in dx],
        out_shape=[
            shape((count, seq, three), BF16),
            shape((heads, blocks, share, 4 * HEAD_DIM), BF16),
        ]
        + dx,
        scratch_shapes=[
            pltpu.VMEM((seq, LANES), F32),
            pltpu.VMEM((seq, LANES), F32),
            pltpu.VMEM((width, three), BF16),
            pltpu.VMEM((4, seq // 8, LANES), BF16),
        ]
        + ([pltpu.VMEM((width, heads * three), BF16)] if more else []),
        input_output_aliases={12 + len(extra): 1} if before else {},
        compiler_params=params(),
        cost_estimate=cost(1000, 1000),
        name="attention_backward",
    )(q, k, v, out, *grads, *parts, *extra, *before)


def input_kernel(*refs, masks, which, placed, count, heads):
    g_refs, w_refs = refs[:count], refs[count : count + len(masks)]
    outs, w_s = refs[count + len(masks) : -1], refs[-1]
    by_head(w_refs, masks, heads, placed, w_s)
    for out, (start, size) in zip(outs, which, strict=True):
        out[...] = through_weights(g_refs, pl.ds(start, size), w_s).astype(out.dtype)


def input_part(g_parts, pieces, masks, which, placed):
    heads = sum(part.shape[0] for part in g_parts)
    three = g_parts[0].shape[2]
    width = pieces[0].shape[0] * pieces[0].shape[1] * len(pieces)
    return pl.pallas_call(
        functools.partial(
            input_kernel, masks=masks, which=which, placed=placed, count=len(g_parts), heads=heads
        ),
        in_specs=[VMEM_SPEC] * (len(g_parts) + len(pieces)),
        out_specs=[VMEM_SPEC] * len(which),
        out_shape=[jax.ShapeDtypeStruct((size, width), BF16) for _, size in which],
        scratch_shapes=[pltpu.VMEM((width, heads * three), BF16)],
        compiler_params=params(),
        cost_estimate=cost(1000, 1000),
        name="input_part",
    )(*g_parts, *pieces)


def middle_kernel(*refs, plan, blocks):
    w_refs = refs[: len(plan)]
    refs = refs[len(plan) :]
    own_ref, near_ref, far_ref = refs[:3]
    x_ref, og_ref, positions_ref, lengths_ref, vec_ref = refs[3:8]
    lo_ref, done_ref, sent_d, kept_d, sent_u, kept_u = refs[8:14]
    ga = refs[14:18]
    w1_s, w2_s, att_s, wo_s, hid_s, slope_s, nrm_s, nb_s, n1_s, rs_s, ffn_s = refs[18:29]
    gf_s, gft_s, nbt_s, acc_s, pre_s, g_s, bup_s, mask_s, sums_ref, low_s, two_s, act_s, in_sem, down_sem, up_sem, out_sem, low_sem = refs[29:]
    rows, width = x_ref.shape
    hidden = w2_s.shape[2]
    pieces = 4
    cols = width // pieces
    placed = blocks > 1
    chunk = 128
    share = width // blocks
    half = rows // 2
    b_out, b_down, gain_a, shift_a, gain_f, shift_f = (vec_ref[i : i + 1, :] for i in range(6))

    count = cols // HEAD_DIM
    att = [[own_ref[h] for h in range(count)]]
    for ref, i in ((near_ref, 0), (far_ref, 0), (near_ref, 1)):
        att.append([ref[i, h] for h in range(count)])

    loads = []
    for ref, entries in zip(w_refs, plan, strict=True):
        for index, second, j, row in entries:
            source = ref.at[index]
            target = (w2_s if second else w1_s).at[j].at[place_of(row, source.shape[0], placed)]
            copy = pltpu.make_async_copy(source, target, in_sem.at[len(loads)])
            loads.append((second, copy))
            copy.start()

    def row_loop(work):
        @pl.loop(0, rows // chunk)
        def _(i):
            work(pl.ds(pl.multiple_of(i * chunk, chunk), chunk))

    def add_sum(index, value):
        sums_ref[index : index + 1, :] += jnp.sum(value, axis=0, keepdims=True)

    def mean(value):
        return jnp.mean(value, axis=-1, keepdims=True)

    def normal(value):
        centred = value - mean(value)
        inverse = lax.rsqrt(mean(centred * centred) + EPSILON)
        return centred * inverse, inverse

    def norm_back(grad, unit, inverse, gain):
        scaled = grad * gain
        return (scaled - mean(scaled) - unit * mean(scaled * unit)) * inverse

    sums_ref[...] = jnp.zeros_like(sums_ref)
    own_valid = jnp.where(valid_row(positions_ref, lengths_ref, 0, rows), 1.0, 0.0)
    mask_s[...] = jnp.broadcast_to(own_valid, (LANES, rows)).T
    for j in range(pieces):
        for h in range(cols // HEAD_DIM):
            at = j * cols + h * HEAD_DIM
            att_s[:half, at : at + HEAD_DIM] = att[j][h][:, :HEAD_DIM]
            att_s[half:, at : at + HEAD_DIM] = att[j][h][:, HEAD_DIM:]
    for second, copy in loads:
        if not second:
            copy.wait()
    for j in range(pieces):
        wo_s[:, j * cols : (j + 1) * cols] = w1_s[j, :, hidden : hidden + cols]
        last = w1_s[j, :, hidden + cols - HEAD_DIM :].astype(F32)
        bup_s[j] = last.T[HEAD_DIM : HEAD_DIM + 1, :]
    ffn_s[...] = dot_nt(att_s[...], wo_s[...])

    def first_norm(r):
        value = x_ref[r, :].astype(F32)
        attn = ffn_s[r, :] + b_out
        valid = mask_s[r, :1] > 0.0
        add_sum(6, jnp.where(valid, value * value, 0.0))
        add_sum(7, jnp.where(valid, attn * attn, 0.0))
        unit, inverse = normal(value + attn)
        normed = unit * gain_a + shift_a
        n1_s[r, :] = unit
        rs_s[r, :] = jnp.broadcast_to(inverse, (chunk, LANES))
        nrm_s[r, :] = normed
        nb_s[r, :] = normed.astype(BF16)

    row_loop(first_norm)
    ffn_s[...] = jnp.zeros_like(ffn_s)
    for second, copy in loads:
        if second:
            copy.wait()

    wide = 384
    per = hidden // wide

    def chunk_of(c):
        return c // per, pl.ds(pl.multiple_of(c % per * wide, wide), wide)

    def product_of(c):
        j, at = chunk_of(c)
        return dot(nb_s[...], w1_s[j, :, at]) + bup_s[j, :, at]

    act_s[...] = jnp.zeros_like(act_s)
    two_s[0] = product_of(0)
    count = pieces * per

    @pl.loop(0, count)
    def _(c):
        j, at = chunk_of(c)
        back, behind = chunk_of(jnp.maximum(c - 1, 0))
        now = c % 2
        two_s[1 - now] = product_of(jnp.minimum(c + 1, count - 1))
        ffn_s[...] += dot_nt(act_s[...], w2_s[back, :, behind])
        pre = two_s[now]
        cdf = 0.5 * (1.0 + lax.erf(pre * (0.5**0.5)))
        pdf = jnp.exp(pre * pre * -0.5) * (2.0 * jnp.pi) ** -0.5
        act = (pre * cdf).astype(BF16)
        hid_s[j, :, at] = act
        slope_s[j, :, at] = cdf + pre * pdf
        act_s[...] = act

    ffn_s[...] += dot_nt(act_s[...], w2_s[pieces - 1, :, (per - 1) * wide :])

    def second_norm(r):
        ffn = ffn_s[r, :] + b_down
        valid = mask_s[r, :1] > 0.0
        add_sum(8, jnp.where(valid, ffn * ffn, 0.0))
        unit, inverse = normal(nrm_s[r, :] + ffn)
        lo_ref[r, :] = (unit * gain_f + shift_f).astype(BF16)
        grad = og_ref[r, :].astype(F32)
        add_sum(4, grad * unit)
        add_sum(5, grad)
        d_two = norm_back(grad, unit, inverse, gain_f)
        low = d_two.astype(BF16)
        add_sum(1, low.astype(F32))
        acc_s[r, :] = d_two
        gf_s[r, :] = low

    row_loop(second_norm)
    gft_s[...] = gf_s[...].T
    nbt_s[...] = nb_s[...].T

    places = [place_of(i, share, placed) for i in range(blocks)]

    def copies(j, lanes, target, place, sem, to):
        return [
            pltpu.make_async_copy(
                g_s.at[j].at[places[i], lanes], target.at[place, i, pl.ds(0, share), to], sem.at[j, i]
            )
            for i in range(blocks)
        ]

    lanes_d, lanes_u, lanes_o = (
        pl.ds(0, hidden),
        pl.ds(hidden, hidden),
        pl.ds(2 * hidden, cols),
    )
    to_d, to_u, to_o = pl.ds(0, hidden), pl.ds(0, hidden), pl.ds(hidden, cols)
    def start_all(j, place, lanes, to, sem, targets):
        for away in (1, 0):

            @pl.when(j % 2 == away)
            def _():
                for copy in copies(j, lanes, targets[1 - away], place, sem, to):
                    copy.start()

    @pl.loop(0, pieces)
    def _(step):
        away = 1 - step // (pieces // 2)
        place = step % (pieces // 2)
        j = 2 * place + away
        pre_s[...] = dot(gf_s[...], w2_s[j]) * slope_s[j]
        low = pre_s[...].astype(BF16)
        sums_ref[pl.ds(10 + j, 1), :] = jnp.sum(low.astype(F32), axis=0, keepdims=True)
        g_s[j, :, lanes_d] = dot(gft_s[...], hid_s[j]).astype(BF16)
        start_all(j, place, lanes_d, to_d, down_sem, (sent_d, kept_d))
        g_s[j, :, lanes_u] = dot(nbt_s[...], low).astype(BF16)
        start_all(j, place, lanes_u, to_u, up_sem, (sent_u, kept_u))
        acc_s[...] += dot_nt(low, w1_s[j, :, :hidden])

    def first_back(r):
        grad = acc_s[r, :]
        unit = n1_s[r, :]
        add_sum(2, grad * unit)
        add_sum(3, grad)
        d_one = norm_back(grad, unit, rs_s[r, :1], gain_a)
        low = d_one.astype(BF16)
        add_sum(0, low.astype(F32))
        done_ref[r, :] = d_one
        gf_s[r, :] = low

    row_loop(first_back)
    low = gf_s[...]
    gout = dot_tn(low, att_s[...]).astype(BF16)
    for j in range(pieces):
        g_s[j, :, 2 * hidden : 2 * hidden + cols] = gout[:, j * cols : (j + 1) * cols]
        for copy in copies(j, lanes_o, sent_u if j % 2 else kept_u, j // 2, out_sem, to_o):
            copy.start()
    small = []
    for j in range(pieces):
        low_s[j] = jnp.concatenate([sums_ref[:9], sums_ref[10 + j : 11 + j], sums_ref[9:15]]).astype(BF16)
        target = sent_d if j % 2 else kept_d
        for i in range(blocks):
            under = target.at[j // 2, i, pl.ds(share, EXTRA), :]
            small.append(pltpu.make_async_copy(low_s.at[j], under, low_sem.at[j, i]))
            small[-1].start()
    back = dot(low, wo_s[...]).astype(BF16)
    for j in range(pieces):
        for h in range(cols // HEAD_DIM):
            at = j * cols + h * HEAD_DIM
            ga[j][h, :, :HEAD_DIM] = back[:half, at : at + HEAD_DIM]
            ga[j][h, :, HEAD_DIM:] = back[half:, at : at + HEAD_DIM]
    for j in range(pieces):
        target_d, target_u = (sent_d, sent_u) if j % 2 else (kept_d, kept_u)
        for copy in copies(j, lanes_d, target_d, j // 2, down_sem, to_d):
            copy.wait()
        for copy in copies(j, lanes_u, target_u, j // 2, up_sem, to_u):
            copy.wait()
        for copy in copies(j, lanes_o, target_u, j // 2, out_sem, to_o):
            copy.wait()
    for copy in small:
        copy.wait()


def middle(blocks, weights, plan, att, tokens, out_grad, positions, lengths, vectors, hidden):
    rows, width = tokens.shape
    cols = width // 4
    share = width // blocks
    shape = jax.ShapeDtypeStruct
    vmem = pltpu.VMEM
    loads = sum(len(entries) for entries in plan)
    return pl.pallas_call(
        functools.partial(middle_kernel, plan=plan, blocks=blocks),
        in_specs=[ANY_SPEC] * len(weights) + [VMEM_SPEC] * 6 + [SMEM_SPEC, VMEM_SPEC],
        out_specs=[VMEM_SPEC] * 2 + [ANY_SPEC] * 4 + [VMEM_SPEC] * 4,
        out_shape=[
            shape((rows, width), BF16),
            shape((rows, width), F32),
        ]
        + [shape((2, blocks, share + EXTRA, hidden), BF16)] * 2
        + [shape((2, blocks, share, hidden + cols), BF16)] * 2
        + [shape(att[0].shape, BF16)] * 4,
        scratch_shapes=[
            vmem((4, width, weights[0].shape[-1]), BF16),
            vmem((4, width, hidden), BF16),
            vmem((rows, width), BF16),
            vmem((width, width), BF16),
            vmem((4, rows, hidden), BF16),
            vmem((4, rows, hidden), F32),
            vmem((rows, width), F32),
            vmem((rows, width), BF16),
            vmem((rows, width), F32),
            vmem((rows, LANES), F32),
            vmem((rows, width), F32),
            vmem((rows, width), BF16),
            vmem((width, rows), BF16),
            vmem((width, rows), BF16),
            vmem((rows, width), F32),
            vmem((rows, hidden), F32),
            vmem((4, width, 2 * hidden + cols), BF16),
            vmem((4, 1, hidden), F32),
            vmem((rows, LANES), F32),
            vmem((16, width), F32),
            vmem((4, EXTRA, width), BF16),
            vmem((2, rows, 384), F32),
            vmem((rows, 384), BF16),
            pltpu.SemaphoreType.DMA((loads,)),
            pltpu.SemaphoreType.DMA((4, blocks)),
            pltpu.SemaphoreType.DMA((4, blocks)),
            pltpu.SemaphoreType.DMA((4, blocks)),
            pltpu.SemaphoreType.DMA((4, blocks)),
        ],
        compiler_params=params(),
        cost_estimate=cost(1000, 1000),
        name="middle",
    )(*weights, *att, tokens, out_grad, positions, lengths, vectors)


def reduce_kernel(*refs, jobs, inputs, outputs, terms, extra, extra_in):
    ins = refs[:inputs]
    more = refs[inputs : inputs + extra_in]
    outs = refs[inputs + extra_in : inputs + extra_in + outputs]
    rest = refs[inputs + extra_in + outputs :]
    extra_out = rest[: len(rest) - terms - 1]
    held, sems = rest[len(extra_out) : -1], rest[-1]
    loads = []
    for _, _, _, parts, _ in jobs:
        for source, index, start, size in parts:
            at = len(loads)
            picked = ins[source].at[index + (slice(None), pl.ds(start, size))]
            loads.append(pltpu.make_async_copy(picked, held[at], sems.at[at]))
            loads[-1].start()
    at = 0
    for out, start, lead, parts, base in jobs:
        mine = range(at, at + len(parts))
        at += len(parts)
        for i in mine:
            loads[i].wait()
        size = parts[0][3]
        for index in itertools.product(*map(range, lead)):
            total = held[mine[0]][index].astype(F32)
            for i in mine[1:]:
                total += held[i][index].astype(F32)
            target = outs[out]
            target[base + index + (slice(None), slice(start, start + size))] = total.astype(target.dtype)
    if extra is not None:
        extra(outs, more, extra_out)


class Sum:
    def __init__(self, names, width):
        self.names, self.width, self.terms, self.picks = list(names), width, [], {}

    def join(self, array, start=0, names=None):
        self.terms.append((array, start, list(self.names if names is None else names)))

    def parts(self, picks):
        return [
            (array, tuple(picks.get(name, slice(None)) for name in names), start, self.width)
            for array, start, names in self.terms
        ]

    def away(self, name):
        parts = self.parts({**self.picks, name: 1})
        self.picks[name] = 0
        self.names.remove(name)
        return parts

    def all(self):
        return self.parts(self.picks)


def reduce_call(name, groups, dtype, extra=None, extra_in=(), extra_out=(), keep=True):
    arrays, jobs, shapes, scratch = [], [], [], []
    for out, columns in enumerate(groups):
        start = 0
        stacked = isinstance(columns, tuple)
        for at, parts in enumerate(columns):
            coded = []
            for array, index, first, size in parts:
                known = [i for i, other in enumerate(arrays) if other is array]
                if not known:
                    arrays.append(array)
                coded.append((known[0] if known else len(arrays) - 1, index, first, size))
                sizes = [n for n, i in zip(array.shape, index) if isinstance(i, slice)]
                sizes += [array.shape[-2], size]
                scratch.append(pltpu.VMEM(tuple(sizes), array.dtype))
            jobs.append((out, start, tuple(sizes[:-2]), coded, (at,) if stacked else ()))
            start += 0 if stacked else coded[0][3]
        front = (len(columns),) if stacked else ()
        shapes.append(front + tuple(sizes[:-1]) + (coded[0][3] if stacked else start,))
    outs = [jax.ShapeDtypeStruct(shape, dtype) for shape in shapes]
    held = [] if keep else [pltpu.VMEM(shape, dtype) for shape in shapes]
    result = pl.pallas_call(
        functools.partial(
            reduce_kernel if keep else reduce_inside,
            jobs=jobs,
            inputs=len(arrays),
            outputs=len(outs),
            terms=len(scratch),
            extra=extra,
            extra_in=len(extra_in),
        ),
        in_specs=[HBM_SPEC] * len(arrays) + [VMEM_SPEC] * len(extra_in),
        out_specs=[VMEM_SPEC] * (len(outs) * keep + len(extra_out)),
        out_shape=outs * keep + list(extra_out),
        scratch_shapes=held + scratch + [pltpu.SemaphoreType.DMA((len(scratch),))],
        compiler_params=params(),
        cost_estimate=cost(1000, 1000),
        name=name,
    )(*arrays, *extra_in)
    return result


def reduce_inside(*refs, inputs, extra_in, outputs, terms, **rest):
    front = inputs + extra_in
    results = refs[front : len(refs) - outputs - terms - 1]
    held = refs[len(refs) - outputs - terms - 1 : len(refs) - terms - 1]
    order = refs[:front] + held + results + refs[len(refs) - terms - 1 :]
    reduce_kernel(*order, inputs=inputs, extra_in=extra_in, outputs=outputs, terms=terms, **rest)


def body(
    tokens,
    seq_lengths,
    positions,
    w_query,
    w_key,
    w_value,
    w_out,
    w_up,
    w_down,
    b_query,
    b_value,
    b_out,
    b_up,
    b_down,
    gain_attn,
    shift_attn,
    gain_ffn,
    shift_ffn,
    out_grad,
):
    group = lax.axis_index("dp")
    member = lax.axis_index("tensor")
    dp_count = lax.axis_size("dp")
    bits = dp_count.bit_length() - 1
    rows, width = tokens.shape
    own_cols = w_query.shape[1]
    heads = own_cols // HEAD_DIM
    share = w_query.shape[0]
    hidden = w_up.shape[1]
    placed = share % 16 == 0 and bits == 3 and heads == 3
    blocks = dp_count if placed else 1
    def core(value):
        return swap(value, "tensor", 1)

    def cross(value):
        return swap(value, "tensor", 2)

    def grow(value, got, masks, bit):
        both = jnp.stack([value, got], axis=1).reshape((-1,) + value.shape[1:])
        return both, [m ^ b for m in masks for b in (0, bit)]

    across = cross(tokens)
    beside = core(tokens)
    own_qkv = jnp.concatenate([w_query, w_key, w_value], axis=1)[None]
    own_b_up = lax.dynamic_slice_in_dim(b_up, group * share, share, 0)[:, None]
    spare = -(hidden + own_cols) % LANES
    one = jnp.concatenate([w_up, w_out.T, jnp.broadcast_to(own_b_up, (share, spare))], axis=1)[None]
    two = w_down.T[None]
    biases = [b_query.reshape(1, -1), b_value.reshape(1, -1)]
    vectors = [b_out, b_down, gain_attn, shift_attn, gain_ffn, shift_ffn]
    vectors = jnp.stack([vec.astype(F32) for vec in vectors] + [jnp.zeros((width,), F32)] * 2)

    if placed:
        got_w = after(swap(own_qkv, "dp", 4), one, two)
        w_part, w_mask = grow(own_qkv, got_w, [0], 4)
        one = after(one, w_part)
        got_w, got_one, across = after((swap(w_part, "dp", 2), swap(one, "dp", 4), across), w_part)
        w_part, w_mask = grow(w_part, got_w, w_mask, 2)
        one, one_mask = grow(one, got_one, [0], 4)

        two = after(two, across)
        round_three = (swap(w_part, "dp", 1), swap(one, "dp", 2), cross(two), core(across))
        round_three = after((round_three, biases, vectors), w_part)
        (got_w, got_one, got_two, beyond), biases, vectors = round_three
        w_qkv, w_masks = [w_part, got_w], [w_mask, [m ^ 1 for m in w_mask]]
        one, one_mask = grow(one, got_one, one_mask, 2)
        two = jnp.stack([two, got_two], axis=1)
        parts = [tokens, beside, across, beyond]

        round_four = (swap(two, "dp", 4), swap(one, "dp", 1), cross(one), core(one))
        positions = after(positions, one, two)
        q, k, v = project(parts, w_qkv, w_masks, *biases, positions, seq_lengths, heads, placed)
        kept = attention_forward(0, 1, q, k, v, [])
        q_kept = kept[0]
        got_two, odd, even_far, even_near = after(round_four, q_kept)
        two, two_mask = grow(two, got_two, [0], 4)

        round_five = (swap(two, "dp", 2), cross(odd), swap(two, "dp", 1), core(even_far))
        kept, odd, two, even_far = after((kept, odd, two, even_far), q_kept)
        q_kept, out, *packed = attention_forward(1, 2, q, k, v, kept)
        kept = [q_kept, out]
        two_late, odd_far, two_odd, both_near = after(round_five, q_kept)

        far_odd = [m ^ 1 for m in one_mask]
        two_mask_odd = [m ^ 1 for m in two_mask]
        late_mask, last_mask = [m ^ 2 for m in two_mask], [m ^ 3 for m in two_mask]
        two_last = swap(two_late, "dp", 1)
        att_far = cross(packed[2])
        odd, two = after((odd, two), two_late)
        two_near, odd_near = core(two), core(odd)
        odd_far, two_late, two_odd = after((odd_far, two_late, two_odd), two_near, odd_near)
        odd_far_near, late_near, two_odd_near = core(odd_far), core(two_late), core(two_odd)
        two_last, att_far = after((two_last, att_far), odd_far_near, late_near, two_odd_near)
        att_near = core(jnp.stack([packed[1], att_far[1]]))
        ones = [(one, one_mask), (odd, far_odd), (even_far, one_mask), (odd_far, far_odd)]
        twos = [(two, two_mask), (two_odd, two_mask_odd), (two_late, late_mask), (two_last, last_mask)]
        early = [even_near, odd_near, both_near, odd_far_near, two_near, two_odd_near, late_near]
        early.append(core(two_last))
    else:
        w_qkv = [gather_bits(own_qkv[0], "dp", range(bits), 0).reshape(1, width, -1)]
        w_masks = [[0]]
        one = gather_bits(one[0], "dp", range(bits), 0).reshape(1, width, -1)
        two = gather_bits(two[0], "dp", range(bits), 0).reshape(1, width, -1)
        parts = [tokens, beside, across, core(across)]
        q, k, v = project(parts, w_qkv, w_masks, *biases, positions, seq_lengths, heads, placed)
        q_kept, out, *packed = attention_forward(0, heads, q, k, v, [])
        kept = [q_kept, out]
        ones = [(one, [0]), (cross(one), [0])]
        twos = [(jnp.stack([two, cross(two)], axis=1), [0])]
        early = [core(array) for array, _ in ones + twos]
        att_far = cross(packed[2])
        att_near = core(jnp.stack([packed[1], att_far[1]]))
    att = [packed[0], att_near, att_far]
    weights = [array for array, _ in ones + twos] + early
    plan = []
    for near in range(2):
        for a, (_, masks) in enumerate(ones):
            far = a // (len(ones) // 2)
            plan.append([((z,), False, near + 2 * far, mask) for z, mask in enumerate(masks)])
        for _, masks in twos:
            plan.append(
                [
                    ((z, far), True, near + 2 * far, mask)
                    for z, mask in enumerate(masks)
                    for far in range(2)
                ]
            )
    layer_out, d_one, sent_d, kept_d, sent_u, kept_u, *back = middle(
        blocks, weights, plan, att, tokens, out_grad, positions, seq_lengths, vectors, hidden
    )
    grads = [back[0]] + [swap(back[j], "tensor", j) for j in (1, 2, 3)]

    def add(*terms):
        total = terms[0].astype(F32)
        for term in terms[1:]:
            total = total + term.astype(F32)
        return total

    def send(away, name):
        return cross(away) if name == "x" else swap(away, "dp", 1 << name)

    def axes_of(array, lead):
        return array.reshape(array.shape[:lead] + (2,) * bits + array.shape[lead + 1 :])

    names = list(range(bits))[::-1]
    late = list(range(1, bits))
    shape = jax.ShapeDtypeStruct
    three = 3 * HEAD_DIM

    got_d, got_u = core(sent_d), core(sent_u)
    if placed:
        down, up = Sum(["x"] + names, hidden), Sum(["x"] + names, hidden + own_cols)
        for array in (kept_u, got_u):
            up.join(axes_of(array, 1))
        (move_u,) = reduce_call("sum_up", [[up.away(0)]], BF16)
        got_d = after(got_d, move_u)
        for array in (kept_d, got_d):
            down.join(axes_of(array, 1))
        (move_d,) = reduce_call("sum_down", [[down.away("x")]], BF16)
        move_d = after(move_d, grads)
        grads = after(grads, move_d)
        down_names, up_names = ["x"] + late + [0], [0, "x"] + late
    q_kept, out = kept
    if placed:
        before = attention_backward(0, heads - 1, q_kept, k, v, out, grads, parts, blocks, [])
        last = before[0]
        down.join(after(send(move_d, down_names.pop(0)), last))
        up.join(after(send(move_u, up_names.pop(0)), last))
        groups = [[down.away(down_names[0])], [up.away(up_names[0])]]
        move_d, move_u = reduce_call("sum_second", groups, BF16)
        q_kept = after(q_kept, move_d)
        more = (before[0], w_qkv, w_masks)
        g_last, g_w, *first = attention_backward(
            heads - 1, 1, q_kept, k, v, out, grads, parts, blocks, before[1:], more
        )
        g_parts = [before[0], g_last]
    else:
        g_all, g_w = attention_backward(0, heads, q_kept, k, v, out, grads, parts, blocks, [])
    if placed:
        down.join(after(send(move_d, down_names.pop(0)), g_last))
        up.join(after(send(move_u, up_names.pop(0)), g_last))
        got_part = [core(part) for part in first[:2]]
    half = rows // 2
    own_parts = ((rows, half), (rows + half, half), (0, rows))
    if placed:
        qkv = Sum(["h"] + names, 4 * HEAD_DIM)
        qkv.join(axes_of(g_w, 1))
        groups = [[down.away(down_names[0])], [up.away(up_names[0])], [qkv.away(0)]]
        groups.append(tuple([(first[2], (i,), 0, width), (got_part[i], (), 0, width)] for i in range(2)))
        move_d, move_u, move_qkv, crossed = reduce_call("sum_third", groups, BF16)
        crossed = cross(crossed)
        g_parts = after(g_parts, move_d)
        second = input_part(g_parts, w_qkv, w_masks, own_parts, placed)
        near = [core(part) for part in second[:2]]
        down.join(after(send(move_d, down_names.pop(0)), *second))
        up.join(after(send(move_u, up_names.pop(0)), *second))
        qkv.join(after(send(move_qkv, 0), *second))
        crossed = after(crossed, *second)
        others = list(itertools.product(range(2), repeat=len(late)))[1:]
        groups = [[down.away(down_names[0])], [up.away(up_names[0])]]
        groups += [[qkv.parts({**qkv.picks, **dict(zip(late, pick))})] for pick in others]
        move_d, move_u, *moves_qkv = reduce_call("sum_fourth", groups, BF16)
        down.join(send(move_d, down_names.pop(0)))
        got_u = send(move_u, up_names.pop(0))
        gots_qkv = [
            swap(move, "dp", sum(bit << name for bit, name in zip(pick, late)))
            for move, pick in zip(moves_qkv, others)
        ]
        qkv.picks.update(dict.fromkeys(late, 0))
        for name in late:
            qkv.names.remove(name)

        def finish_down(totals, ins, outs):
            outs[0][...] = totals[0][:share]
            outs[1][...] = totals[0][share:]
            for i in range(2):
                part = pl.ds(i * half, half)
                total = ins[0][part, :]
                for term in (ins[1][part, :], ins[2][i], ins[3 + i][...]):
                    total += term.astype(F32)
                outs[2][part, :] = total.astype(BF16)

        g_down, small, input_grad = reduce_call(
            "finish_down",
            [[down.all()]],
            F32,
            finish_down,
            (d_one, second[2], crossed, *near),
            (
                shape((share, hidden), F32),
                shape((EXTRA, width), F32),
                shape((rows, width), BF16),
            ),
            keep=False,
        )
        g_down = g_down.T
        got_u, gots_qkv = after((got_u, gots_qkv), small)
        up.join(got_u)
        for got in gots_qkv:
            qkv.join(got)
    else:
        first = input_part([g_all], w_qkv, w_masks, ((3 * rows, rows), (2 * rows, rows)), placed)
        crossed = cross(add(first[1], core(first[0])).astype(BF16))
        second = input_part([g_all], w_qkv, w_masks, own_parts, placed)
        near = jnp.concatenate([core(part) for part in second[:2]])

    if placed:

        def finish(totals, _, outs):
            g_up, g_qkv = totals
            q_out, k_out, v_out, o_out, up_out, bq_out, bv_out = outs
            for h in range(heads):
                at = pl.ds(h * HEAD_DIM, HEAD_DIM)
                for kind, out in enumerate((q_out, k_out, v_out)):
                    out[:, at] = g_qkv[h, :, kind * HEAD_DIM : (kind + 1) * HEAD_DIM]
                bq_out[:, at] = g_qkv[h, 0:1, three:]
                bv_out[:, at] = g_qkv[h, 8:9, three:]
            up_out[...] = g_up[:, :hidden]
            o_out[...] = g_up[:, hidden:].T

        g_q, g_k, g_v, g_out, g_up, bias_q, bias_v = reduce_call(
            "finish",
            [[up.all()], [qkv.all()]],
            F32,
            finish,
            (),
            (
                [shape((share, own_cols), F32)] * 3
                + [shape((own_cols, share), F32), shape((share, hidden), F32)]
                + [shape((1, own_cols), F32)] * 2
            ),
            keep=False,
        )
        bias_q, bias_v = bias_q[0], bias_v[0]
    else:
        input_grad = add(d_one, second[2], near, crossed).astype(BF16)
        two_s = (2,) * bits

        def whole_sum(mine, got):
            total = add(mine, got)
            return total[0, 0] + cross(total[1, 0].astype(BF16)).astype(F32)

        def home(total, lead):
            shaped = total.reshape(total.shape[:lead] + two_s + (share, total.shape[-1]))
            return scatter_bits(shaped, "dp", range(bits), lead)

        total = whole_sum(kept_d, got_d)
        g_down, small = home(total[:width], 0).T, total[width:]
        total = home(whole_sum(kept_u, got_u), 0)
        g_up, g_out = total[:, :hidden], total[:, hidden:].T
        g_qkv = home(g_w[:, 0, :, :three].astype(F32), 1).reshape(heads, share, 3, HEAD_DIM)
        g_q, g_k, g_v = (g_qkv[:, :, i].transpose(1, 0, 2).reshape(share, own_cols) for i in range(3))
        bias_rows = g_w[:, 0, 0:16:8, three:].astype(F32)
        for bit in range(bits):
            small = small + swap(small, "dp", 1 << bit)
            bias_rows = bias_rows + swap(bias_rows, "dp", 1 << bit)
        bias_q, bias_v = bias_rows[:, 0].reshape(own_cols), bias_rows[:, 1].reshape(own_cols)
    count = jnp.sum(seq_lengths).astype(F32) * width
    rms = jnp.sqrt(jnp.sum(small[6:9], axis=-1) / count)
    return (
        layer_out,
        input_grad,
        g_q,
        g_k,
        g_v,
        g_out,
        g_up,
        g_down,
        bias_q,
        bias_v,
        small[0],
        small[9],
        small[1],
        small[2],
        small[3],
        small[4],
        small[5],
        rms,
    )


def solution(mesh):
    in_specs = (
        P(("dp", "tensor"), None),
        P(),
        P("dp", None),
        P("dp", "tensor"),
        P("dp", "tensor"),
        P("dp", "tensor"),
        P("tensor", "dp"),
        P("dp", "tensor"),
        P("tensor", "dp"),
        P("tensor"),
        P("tensor"),
        P(),
        P("tensor"),
        P(),
        P(),
        P(),
        P(),
        P(),
        P(("dp", "tensor"), None),
    )
    out_specs = (
        P(("dp", "tensor"), None),
        P(("dp", "tensor"), None),
        P("dp", "tensor"),
        P("dp", "tensor"),
        P("dp", "tensor"),
        P("tensor", "dp"),
        P("dp", "tensor"),
        P("tensor", "dp"),
        P("tensor"),
        P("tensor"),
        P(),
        P("tensor"),
        P(),
        P(),
        P(),
        P(),
        P(),
        P(),
    )
    return jax.shard_map(body, mesh=mesh, in_specs=in_specs, out_specs=out_specs, check_vma=False)
```
